32 devices in a mesh: fsdp: 8 (over z, y), tp: 4 (over x, core).
Axes of the slice: x: 2, y: 2, z: 4, core: 2. Of those that a mesh axis runs over, the one named last changes fastest.
Arguments:
- tokens: bfloat16 [16384, 1536], P(('fsdp', 'tp')), may hold values from -6 to 6
- cotangent: bfloat16 [16384, 1536], P(('fsdp', 'tp')), may hold values from -6 to 6
- w_query: bfloat16 [1536, 1536], P('fsdp', 'tp'), may hold values from -0.15625 to 0.15625
- w_key: bfloat16 [1536, 1536], P('fsdp', 'tp'), may hold values from -0.15625 to 0.15625
- w_value: bfloat16 [1536, 1536], P('fsdp', 'tp'), may hold values from -0.15625 to 0.15625
- w_house: bfloat16 [1536, 1536], P('fsdp', 'tp'), may hold values from -0.15625 to 0.15625
- w_beta: bfloat16 [1536, 12], P('fsdp', 'tp'), may hold values from -0.15625 to 0.15625
- w_out: bfloat16 [1536, 1536], P('fsdp', 'tp'), may hold values from -0.625 to 0.625
- w_gate: bfloat16 [1536, 4096], P('fsdp', 'tp'), may hold values from -0.15625 to 0.15625
- w_up: bfloat16 [1536, 4096], P('fsdp', 'tp'), may hold values from -0.15625 to 0.15625
- w_down: bfloat16 [1536, 4096], P('fsdp', 'tp'), may hold values from -0.09375 to 0.09375
- gain_attn: bfloat16 [1536], P('fsdp'), may hold values from 0.5 to 1.5
- gain_ffn: bfloat16 [1536], P('fsdp'), may hold values from 0.5 to 1.5
- pack_index: int32 [8, 2, 1024], P('fsdp'), may hold values from 0 to 2047, as said below
- seq_start: int32 [8, 2, 1024], P('fsdp'), may hold values from 0 to 768, as said below
Outputs:
- activations: bfloat16 [16384, 1536], P(('fsdp', 'tp'))
- grad_tokens: bfloat16 [16384, 1536], P(('fsdp', 'tp'))
- grad_w_query: float32 [1536, 1536], P('fsdp', 'tp')
- grad_w_key: float32 [1536, 1536], P('fsdp', 'tp')
- grad_w_value: float32 [1536, 1536], P('fsdp', 'tp')
- grad_w_house: float32 [1536, 1536], P('fsdp', 'tp')
- grad_w_beta: float32 [1536, 12], P('fsdp', 'tp')
- grad_w_out: float32 [1536, 1536], P('fsdp', 'tp')
- grad_w_gate: float32 [1536, 4096], P('fsdp', 'tp')
- grad_w_up: float32 [1536, 4096], P('fsdp', 'tp')
- grad_w_down: float32 [1536, 4096], P('fsdp', 'tp')
- grad_gain_attn: float32 [1536], P('fsdp')
- grad_gain_ffn: float32 [1536], P('fsdp')
The draws below stay inside these ranges and needn't reach their ends.
Inputs may be any that keep to these rules, and one draw needn't show every extreme that they name: For each group, pack_index over its 2 bins is a permutation of the group's rows; every sequence occupies a run of rows both in the bin and in tokens. `seq_start`: sequences are whole multiples of 128 rows, from 256 to 1024 long, and fill each bin exactly; some bin holds one sequence of 1024 rows.
All inputs are finite; a program needn't handle non-finite values.
Results may differ from the reference program's by a relative error of at most 0.017.
Values may be sent and summed in bfloat16 or wider, within the bound.
A program may use at most 312 MiB of HBM per device.

```python
import jax
import jax.numpy as jnp
import numpy as np
from jax import lax

D = 1536
H = 12
FF = 4096
QUANT = 128
UT_BLOCK = 64
BINS_G = 2
BIN = 1024
GROUPS = 8
TOKENS = 16384


split_table = np.array([[1, 0, 0, 0, 0, 0, 0, 0], [1, 0, 0, 0, 0, 0, 1, 0], [1, 0, 1, 0, 0, 0, 0, 0], [1, 0, 0, 0, 0, 1, 0, 0], [1, 0, 0, 1, 0, 0, 0, 0], [1, 0, 0, 0, 1, 0, 0, 0], [1, 0, 0, 0, 1, 0, 1, 0], [1, 0, 1, 0, 0, 0, 1, 0], [1, 0, 1, 0, 1, 0, 0, 0], [1, 0, 0, 1, 0, 0, 1, 0], [1, 0, 0, 1, 0, 1, 0, 0], [1, 0, 1, 0, 0, 1, 0, 0], [1, 0, 1, 0, 1, 0, 1, 0]], dtype=np.int32)


def packing_draw(key):
    base_key = jax.random.fold_in(key, 11)
    total_bins = GROUPS * BINS_G
    pattern = jax.random.randint(jax.random.fold_in(base_key, 1), (total_bins,), 0, 13, dtype=jnp.int32)
    bin_number = jnp.arange(total_bins, dtype=jnp.int32)
    pattern = jnp.where(bin_number == 0, 0, jnp.where(bin_number == total_bins - 1, 12, pattern))
    start_flags = jnp.asarray(split_table)[pattern]
    quarter_idx = jnp.arange(8, dtype=jnp.int32)
    first_quant = lax.cummax(start_flags * quarter_idx[None, :], axis=1).reshape(GROUPS, BINS_G, 8)
    row_index = jnp.arange(BIN, dtype=jnp.int32)
    quant_of_row = row_index // QUANT
    start_rows = first_quant[:, :, quant_of_row] * QUANT
    quanta = BINS_G * 8
    group_quant = jnp.arange(quanta, dtype=jnp.int32)
    seq_first = (first_quant + (jnp.arange(BINS_G, dtype=jnp.int32) * 8)[None, :, None]).reshape(GROUPS, quanta)

    def shuffle(sub_key):
        return jax.random.permutation(sub_key, quanta).astype(jnp.int32)
    priority = jax.vmap(shuffle)(jax.random.split(jax.random.fold_in(base_key, 2), GROUPS))
    seq_priority = jnp.take_along_axis(priority, seq_first, axis=1)
    earlier = jnp.sum((seq_priority[:, None, :] < seq_priority[:, :, None]).astype(jnp.int32), axis=2)
    orig_quant = (earlier + (group_quant[None, :] - seq_first)).reshape(GROUPS, BINS_G, 8)
    pack_rows = orig_quant[:, :, quant_of_row] * QUANT + row_index % QUANT
    return (start_rows.astype(jnp.int32), pack_rows.astype(jnp.int32))


def draw_seq_start(key, part):
    return packing_draw(key)[0]


def draw_pack_index(key, part):
    return packing_draw(key)[1]


def raised(drawn, own_key, source, target, blocks, factor):
    owner, partner = [(jnp.arange(drawn.shape[axis_at]) // (drawn.shape[axis_at] // blocks)).reshape([-1 if axis == axis_at else 1 for axis in range(drawn.ndim)]) for axis_at in (source, target)]
    chosen = jax.random.permutation(own_key, blocks)[partner]
    strong = (owner == chosen) | (owner == (partner + blocks // 2) % blocks)
    return jnp.where(strong, factor * drawn, drawn)


def shard_levels(own_key, shape, cuts, low, high):
    level, own = 1.0, jax.random.fold_in(own_key, 6)
    for position, blocks in cuts:
        steps = jnp.exp(jax.random.uniform(jax.random.fold_in(own, position), (blocks,), jnp.float32, low / len(cuts), high / len(cuts)))
        level = level * jnp.repeat(steps, shape[position] // blocks).reshape([-1 if axis == position else 1 for axis in range(len(shape))])
    return level


def bell_draw(own_key, extent, spread, reach, cuts=(), held_as=jnp.bfloat16):
    values = jax.random.normal(own_key, extent, jnp.float32) * spread
    if len(cuts) > 0:
        values = shard_levels(own_key, extent, cuts, -0.22, 0.18) * values
    return jnp.clip(values, min=-reach, max=reach).astype(held_as)


def gaussian_with(rng, dims, scale, bound, cuts, heavy, kind=jnp.bfloat16):
    values = scale * jax.random.normal(rng, dims, jnp.float32)
    if cuts:
        values = values * shard_levels(rng, dims, cuts, -0.22, 0.18)
    return jnp.clip(raised(values, jax.random.fold_in(rng, 3), *heavy), -bound, bound).astype(kind)


def setup_inputs(seed: int = 0) -> dict:
    arg_keys = jax.random.split(jax.random.key(seed), 16)
    tokens = gaussian_with(arg_keys[0], (TOKENS, D), 1.0, 6.0, ((0, 32),), (0, 1, 32, 2.75))
    cotangent = gaussian_with(arg_keys[1], (TOKENS, D), 1.0, 6.0, ((0, 32),), (0, 1, 32, 2.75))
    w_query = bell_draw(arg_keys[2], (D, D), D ** -0.5, 0.15625, ((0, 8), (1, 4)))
    w_key = bell_draw(arg_keys[3], (D, D), D ** -0.5, 0.15625, ((0, 8), (1, 4)))
    w_value = bell_draw(arg_keys[4], (D, D), D ** -0.5, 0.15625, ((0, 8), (1, 4)))
    w_house = bell_draw(arg_keys[5], (D, D), D ** -0.5, 0.15625, ((0, 8), (1, 4)))
    w_beta = bell_draw(arg_keys[6], (D, H), D ** -0.5, 0.15625, ((0, 8), (1, 4)))
    w_out = bell_draw(arg_keys[7], (D, D), (D // 16) ** -0.5, 0.625, ((0, 8), (1, 4)))
    w_gate = bell_draw(arg_keys[8], (D, FF), D ** -0.5, 0.15625, ((0, 8), (1, 4)))
    w_up = bell_draw(arg_keys[9], (D, FF), D ** -0.5, 0.15625, ((0, 8), (1, 4)))
    w_down = bell_draw(arg_keys[10], (D, FF), FF ** -0.5, 0.09375, ((0, 8), (1, 4)))
    gain_attn = jnp.clip(1.0 + 0.1 * jax.random.normal(arg_keys[11], (D,), jnp.float32), 0.5, 1.5).astype(jnp.bfloat16)
    gain_ffn = jnp.clip(1.0 + 0.1 * jax.random.normal(arg_keys[12], (D,), jnp.float32), 0.5, 1.5).astype(jnp.bfloat16)
    pack_index = draw_pack_index(jax.random.fold_in(arg_keys[15], 71), 0)
    seq_start = draw_seq_start(jax.random.fold_in(arg_keys[15], 71), 0)
    return {"tokens": tokens, "cotangent": cotangent, "w_query": w_query, "w_key": w_key, "w_value": w_value, "w_house": w_house, "w_beta": w_beta, "w_out": w_out, "w_gate": w_gate, "w_up": w_up, "w_down": w_down, "gain_attn": gain_attn, "gain_ffn": gain_ffn, "pack_index": pack_index, "seq_start": seq_start}


epsilon = 1e-06
highest = lax.Precision.HIGHEST

@jax.custom_vjp
def low(v):
    return lax.optimization_barrier(v.astype(jnp.bfloat16)).astype(jnp.float32)

@jax.custom_vjp
def low_back(v):
    return v

def low_keep(v):
    return (low(v), None)

def low_pass(kept, grad):
    return (grad,)

def back_keep(v):
    return (v, None)

def back_low(kept, grad):
    return (low(grad),)
low.defvjp(low_keep, low_pass)
low_back.defvjp(back_keep, back_low)

def both_ways(value_in):
    return low_back(low(value_in))

def rms_rows(value_in):
    return value_in * lax.rsqrt(lax.optimization_barrier(jnp.mean(value_in * value_in, axis=-1, keepdims=True)) + epsilon)

def path_head(query_rows, key_rows, value_rows, house_unit, beta_heads, seq_begin):
    row_count, head_dim = query_rows.shape
    blocks = row_count // UT_BLOCK
    q_blocks = query_rows.reshape(blocks, UT_BLOCK, head_dim)
    k_blocks = key_rows.reshape(blocks, UT_BLOCK, head_dim)
    w_blocks = house_unit.reshape(blocks, UT_BLOCK, head_dim)
    b_blocks = beta_heads.reshape(blocks, UT_BLOCK)
    inner_idx = jnp.arange(UT_BLOCK, dtype=jnp.int32)
    strict = inner_idx[:, None] > inner_idx[None, :]
    lower_eq = inner_idx[:, None] >= inner_idx[None, :]
    identity = jnp.broadcast_to(jnp.eye(UT_BLOCK, dtype=jnp.float32), (blocks, UT_BLOCK, UT_BLOCK))
    gram_mat = jnp.einsum('bsd,btd->bst', w_blocks, w_blocks, precision=highest)
    left_mat = identity + jnp.where(strict, gram_mat * b_blocks[:, None, :], 0.0)
    right_mat = identity + jnp.where(strict, gram_mat * b_blocks[:, :, None], 0.0)
    left_inv = lax.linalg.triangular_solve(left_mat, identity, left_side=True, lower=True)
    right_inv = lax.linalg.triangular_solve(right_mat, identity, left_side=True, lower=True)
    wk_prod = jnp.einsum('bsd,bjd->bsj', w_blocks, k_blocks, precision=highest)
    pushed = jnp.einsum('bst,btj->bsj', left_inv, jnp.where(strict, wk_prod, 0.0), precision=highest)
    k_end = k_blocks - jnp.einsum('bsj,bsd->bjd', pushed * b_blocks[:, :, None], w_blocks, precision=highest)
    qw_prod = jnp.where(lower_eq, jnp.einsum('bid,bsd->bis', q_blocks, w_blocks, precision=highest), 0.0)
    pulled = jnp.einsum('bis,bst->bit', qw_prod, right_inv, precision=highest)
    q_start = q_blocks - jnp.einsum('bit,btd->bid', pulled * b_blocks[:, None, :], w_blocks, precision=highest)
    near_scores = jnp.einsum('bid,bjd->bij', q_blocks, k_blocks, precision=highest) - jnp.einsum('bis,bsj->bij', qw_prod * b_blocks[:, None, :], pushed, precision=highest)
    row_block = jnp.arange(row_count, dtype=jnp.int32) // UT_BLOCK

    def advance(current, block_step):
        next_block = block_step + 1
        w_next = lax.dynamic_index_in_dim(w_blocks, next_block, 0, keepdims=False)
        inv_next = lax.dynamic_index_in_dim(right_inv, next_block, 0, keepdims=False)
        b_next = lax.dynamic_index_in_dim(b_blocks, next_block, 0, keepdims=False)
        coefficient = jnp.dot(jnp.dot(current, w_next.T, precision=highest), inv_next, precision=highest) * b_next[None, :]
        moved_rows = current - jnp.dot(coefficient, w_next, precision=highest)
        current = jnp.where((row_block > next_block)[:, None], moved_rows, current)
        k_here = lax.dynamic_index_in_dim(k_end, block_step, 0, keepdims=False)
        return (current, jnp.dot(current, k_here.T, precision=highest))
    steps_down = jnp.arange(blocks - 2, -1, -1, dtype=jnp.int32)
    final_rows, slabs = lax.scan(jax.checkpoint(advance), q_start.reshape(row_count, head_dim), steps_down)
    far_blocks = jnp.concatenate([slabs[::-1], jnp.zeros((1, row_count, UT_BLOCK), jnp.float32)], axis=0)
    far_scores = far_blocks.transpose(1, 0, 2).reshape(row_count, row_count)
    near_full = jnp.einsum('bij,bc->bicj', near_scores, jnp.eye(blocks, dtype=jnp.float32), precision=highest).reshape(row_count, row_count)
    same_block = row_block[:, None] == row_block[None, :]
    scores = jnp.where(same_block, near_full, far_scores) * head_dim ** (-0.5)
    columns = jnp.arange(row_count, dtype=jnp.int32)
    valid = (columns[None, :] >= seq_begin[:, None]) & (columns[None, :] <= columns[:, None])
    logits = jnp.where(valid, scores, -jnp.inf)
    row_max = lax.optimization_barrier(jnp.max(logits, axis=1, keepdims=True))
    expos = jnp.exp(logits - row_max)
    weights_prob = expos / lax.optimization_barrier(jnp.sum(expos, axis=1, keepdims=True))
    return jnp.dot(weights_prob, value_rows, precision=highest)

def attend(query_in, keys_in, values_in, house_in, beta_in, seq_begin):
    row_count = query_in.shape[0]
    head_count = beta_in.shape[1]
    head_dim = query_in.shape[1] // head_count

    def split_heads(array_in):
        return array_in.reshape(row_count, head_count, head_dim).transpose(1, 0, 2)
    house_heads = split_heads(house_in)
    house_unit = house_heads * lax.rsqrt(lax.optimization_barrier(jnp.sum(house_heads * house_heads, axis=-1, keepdims=True)) + epsilon)
    beta_heads = (2.0 * jax.nn.sigmoid(beta_in)).T
    result = jax.vmap(path_head, in_axes=(0, 0, 0, 0, 0, None))(split_heads(query_in), split_heads(keys_in), split_heads(values_in), house_unit, beta_heads, seq_begin)
    return result.transpose(1, 0, 2).reshape(row_count, head_count * head_dim)

def bin_layer(x_bin, seq_begin, weights):
    w_query, w_key, w_value, w_house, w_beta, w_out, w_gate, w_up, w_down, gain_attn, gain_ffn = weights
    normed = low(rms_rows(x_bin) * gain_attn)
    query_rows = both_ways(jnp.dot(normed, w_query, precision=highest))
    key_rows = both_ways(jnp.dot(normed, w_key, precision=highest))
    value_rows = both_ways(jnp.dot(normed, w_value, precision=highest))
    house_raw = both_ways(jnp.dot(normed, w_house, precision=highest))
    beta_raw = both_ways(jnp.dot(normed, w_beta, precision=highest))
    mixed_heads = low(attend(query_rows, key_rows, value_rows, house_raw, beta_raw, seq_begin))
    attn_part = low_back(jnp.dot(mixed_heads, w_out.T, precision=highest))
    hidden_in = x_bin + attn_part
    normed_two = low(rms_rows(hidden_in) * gain_ffn)
    gate_pre = low_back(jnp.dot(normed_two, w_gate, precision=highest))
    up_part = low_back(jnp.dot(normed_two, w_up, precision=highest))
    hidden = low(jax.nn.silu(gate_pre) * up_part)
    return hidden_in + low_back(jnp.dot(hidden, w_down.T, precision=highest))

def reference(tokens, cotangent, w_query, w_key, w_value, w_house, w_beta, w_out, w_gate, w_up, w_down, gain_attn, gain_ffn, pack_index, seq_start):
    group_rows = BINS_G * BIN
    offsets = (jnp.arange(GROUPS, dtype=jnp.int32) * group_rows)[:, None, None]
    source = (pack_index + offsets).reshape(-1).astype(jnp.int32)
    begins = seq_start.reshape(GROUPS * BINS_G, BIN).astype(jnp.int32)
    params = tuple((weight_arr.astype(jnp.float32) for weight_arr in (w_query, w_key, w_value, w_house, w_beta, w_out, w_gate, w_up, w_down, gain_attn, gain_ffn)))

    def forward(inputs, weights):
        packed = inputs[source].reshape(GROUPS * BINS_G, BIN, D)

        def one_bin(bin_item):
            return bin_layer(bin_item[0], bin_item[1], weights)
        results = lax.map(jax.checkpoint(one_bin), (packed, begins))
        return jnp.zeros_like(inputs).at[source].set(results.reshape(-1, D))
    output, pullback = jax.vjp(forward, tokens.astype(jnp.float32), params)
    grad_inputs, grad_weights = pullback(cotangent.astype(jnp.float32))
    return (output.astype(jnp.bfloat16), grad_inputs.astype(jnp.bfloat16), grad_weights[0], grad_weights[1], grad_weights[2], grad_weights[3], grad_weights[4], grad_weights[5], grad_weights[6], grad_weights[7], grad_weights[8], grad_weights[9], grad_weights[10])
```

```python
import functools

import jax
import jax.numpy as jnp
from jax import lax
from jax.experimental import pallas as pl
from jax.experimental.pallas import tpu as pltpu
from jax.sharding import PartitionSpec as P

BLOCK = 128
epsilon = 1e-06
bf16 = jnp.bfloat16
f32 = jnp.float32


def mm(a, b):
    return lax.dot_general(a, b, (((1,), (0,)), ((), ())), preferred_element_type=f32)


def mm_rt(a, b):
    return lax.dot_general(a, b, (((1,), (1,)), ((), ())), preferred_element_type=f32)


def mm_lt(a, b):
    return lax.dot_general(a, b, (((0,), (0,)), ((), ())), preferred_element_type=f32)


def iotas():
    rows = lax.broadcasted_iota(jnp.int32, (BLOCK, BLOCK), 0)
    cols = lax.broadcasted_iota(jnp.int32, (BLOCK, BLOCK), 1)
    return rows, cols


def strengths(u, r_col):
    uf = u.astype(f32)
    inv_sq = 1.0 / (jnp.sum(uf * uf, axis=1, keepdims=True) + epsilon)
    beta = 2.0 / (1.0 + jnp.exp(-r_col))
    return beta, inv_sq


def prep_kernel(heads, q_ref, k_ref, u_ref, r_ref, near_ref, q0_ref, kp_ref, inv_ref, t_ref):
    rows, cols = iotas()
    strict = rows > cols
    lower = rows >= cols
    diff = rows ^ cols
    eye = jnp.where(rows == cols, 1.0, 0.0).astype(f32)
    eye_b = eye.astype(bf16)
    chunks = q_ref.shape[0] // BLOCK
    items = [(c, h) for c in range(chunks) for h in range(heads)]
    state = []
    for c, h in items:
        rs, cs = pl.ds(c * BLOCK, BLOCK), pl.ds(h * BLOCK, BLOCK)
        q, k, u = q_ref[rs, cs], k_ref[rs, cs], u_ref[rs, cs]
        beta, inv_sq = strengths(u, r_ref[rs, h : h + 1].astype(f32))
        bp = beta * inv_sq
        big = mm_rt(jnp.concatenate([u, q], axis=0), jnp.concatenate([u, k], axis=0))
        gram = big[:BLOCK, :BLOCK]
        e_s = jnp.where(strict, big[:BLOCK, BLOCK:], 0.0)
        a_s = jnp.where(lower, big[BLOCK:, :BLOCK], 0.0)
        n0 = big[BLOCK:, BLOCK:]
        low = jnp.where(strict, gram * bp, 0.0)
        eu = jnp.concatenate([e_s * bp, u.astype(f32) * bp], axis=1).astype(bf16)
        state.append([q, k, u, a_s.astype(bf16), n0, low, eu, eye - jnp.where(diff < 2, low, 0.0)])
    size = 2
    while size < BLOCK:
        sel = (diff >= size) & (diff < 2 * size)
        prods = []
        for st in state:
            xb = st[7].astype(bf16)
            prods.append((xb, mm(jnp.where(sel, st[5], 0.0).astype(bf16), xb)))
        for st, (xb, y) in zip(state, prods):
            st[7] = st[7] - mm(xb, y.astype(bf16))
        size *= 2
    for (c, h), (q, k, u, a_b, n0, low, eu, x) in zip(items, state):
        rs, cs = pl.ds(c * BLOCK, BLOCK), pl.ds(h * BLOCK, BLOCK)
        xb = x.astype(bf16)
        t = mm(xb, eu).astype(bf16)
        top = mm(a_b, t)
        bot = mm_lt(u, t)
        inv_ref[c, h] = xb
        t_ref[c, h] = t
        near_ref[c, h] = n0 - top[:, :BLOCK]
        q0_ref[rs, cs] = (q.astype(f32) - top[:, BLOCK:]).astype(bf16)
        ket = mm_rt(eye_b, k) - bot[:, :BLOCK]
        kp_ref[c, h] = jnp.concatenate([ket, eye - bot[:, BLOCK:]], axis=1).astype(bf16)


def fwd_kernel(
    heads, depth, scale, first_ref, q0_ref, near_ref, kp_ref, v_ref, o_ref, linv_ref, e_ref, cur_ref, s_ref, m_ref, acc_ref
):
    i = pl.program_id(0)
    first = first_ref[i]
    rows, cols = iotas()
    lower = rows >= cols
    neg = jnp.float32(-1e30)
    for h in range(heads):
        s0 = jnp.where(lower, near_ref[0, h], neg)
        s_ref[0, h] = s0
        m_ref[h] = s0
        cur_ref[0, 0, h] = q0_ref[:, h * BLOCK : (h + 1) * BLOCK]
    for d in range(1, depth):

        @pl.when(i - d >= first)
        def _():
            j = i - d
            for h in range(heads):
                both = mm(cur_ref[0, d - 1, h], kp_ref[j, h])
                s = both[:, :BLOCK]
                s_ref[d, h] = s
                m_ref[h] = jnp.maximum(m_ref[h], s)
                if d + 1 < depth:
                    cur_ref[0, d, h] = both[:, BLOCK:].astype(bf16)

    peaks = []
    for h in range(heads):
        peak = jnp.max(m_ref[h], axis=1, keepdims=True)
        peaks.append(peak)
        e0 = jnp.exp((s_ref[0, h] - peak) * scale)
        m_ref[h] = e0
        eb = e0.astype(bf16)
        e_ref[0, 0, h] = eb
        v = v_ref[pl.ds(pl.multiple_of(i * BLOCK, BLOCK), BLOCK), h * BLOCK : (h + 1) * BLOCK]
        acc_ref[h] = mm(eb, v)
    for d in range(1, depth):

        @pl.when(i - d >= first)
        def _():
            j = i - d
            for h in range(heads):
                e = jnp.exp((s_ref[d, h] - peaks[h]) * scale)
                m_ref[h] = m_ref[h] + e
                eb = e.astype(bf16)
                e_ref[0, d, h] = eb
                v = v_ref[pl.ds(pl.multiple_of(j * BLOCK, BLOCK), BLOCK), h * BLOCK : (h + 1) * BLOCK]
                acc_ref[h] = acc_ref[h] + mm(eb, v)

    for h in range(heads):
        linv = 1.0 / jnp.sum(m_ref[h], axis=1, keepdims=True)
        cs = slice(h * BLOCK, (h + 1) * BLOCK)
        o_ref[:, cs] = (acc_ref[h] * linv).astype(bf16)
        linv_ref[:, cs] = jnp.broadcast_to(linv, (BLOCK, BLOCK))


def bwd_kernel(heads, depth, scale, last_ref, *refs):
    (do_ref, o_ref, linv_ref, q_ref, k_ref, v_ref, u_ref, r_ref, kp_ref, inv_ref, t_ref) = refs[:11]
    e_refs = refs[11 : 11 + depth]
    cur_refs = refs[11 + depth : 10 + 2 * depth]
    out_ref, dop_ref, del_ref, g_ref, dv_ref, acc_ref = refs[10 + 2 * depth :]
    j = pl.program_id(0)
    last = last_ref[j]
    rows, cols = iotas()
    strict = rows > cols
    lower = rows >= cols
    upper = rows <= cols
    total = dop_ref.shape[0]

    @pl.when(j == 0)
    def _():
        for c in range(total // BLOCK):
            rs = pl.ds(c * BLOCK, BLOCK)
            for h in range(heads):
                cs = slice(h * BLOCK, (h + 1) * BLOCK)
                dop = do_ref[rs, cs].astype(f32) * linv_ref[rs, cs]
                delta = jnp.sum(dop * o_ref[rs, cs].astype(f32), axis=1, keepdims=True)
                dop_ref[rs, cs] = dop.astype(bf16)
                del_ref[rs, cs] = jnp.broadcast_to(delta, (BLOCK, BLOCK))
                g_ref[c, h] = jnp.zeros((BLOCK, BLOCK), bf16)

    here = pl.ds(pl.multiple_of(j * BLOCK, BLOCK), BLOCK)
    near = []
    for h in range(heads):
        cs = slice(h * BLOCK, (h + 1) * BLOCK)
        dop = dop_ref[here, cs]
        e = e_refs[0][0, 0, h]
        dp = mm_rt(dop, v_ref[:, cs])
        near.append((e.astype(f32) * (dp - del_ref[here, cs]) * scale).astype(bf16))
        dv_ref[h] = mm_lt(e, dop)
        acc_ref[h] = jnp.zeros((BLOCK, 2 * BLOCK), f32)
    for d in range(1, depth):

        @pl.when(j + d <= last)
        def _():
            i = j + d
            there = pl.ds(pl.multiple_of(i * BLOCK, BLOCK), BLOCK)
            for h in range(heads):
                cs = slice(h * BLOCK, (h + 1) * BLOCK)
                dop = dop_ref[there, cs]
                e = e_refs[d][0, 0, h]
                dp = mm_rt(dop, v_ref[:, cs])
                ds = (e.astype(f32) * (dp - del_ref[there, cs]) * scale).astype(bf16)
                dv_ref[h] = dv_ref[h] + mm_lt(e, dop)
                dsg = jnp.concatenate([ds, g_ref[i, h]], axis=1)
                acc_ref[h] = acc_ref[h] + mm_lt(cur_refs[d - 1][0, 0, h], dsg)
                g_ref[i, h] = mm_rt(dsg, kp_ref[0, h]).astype(bf16)

    lane = cols
    dr_all = jnp.zeros((BLOCK, BLOCK), f32)
    width = heads * BLOCK
    for h in range(heads):
        cs = slice(h * BLOCK, (h + 1) * BLOCK)
        q, k, u = q_ref[:, cs], k_ref[:, cs], u_ref[:, cs]
        beta, inv_sq = strengths(u, r_ref[:, h : h + 1].astype(f32))
        bp = beta * inv_sq
        kq = mm_rt(u, jnp.concatenate([k, q], axis=0))
        e_s = jnp.where(strict, kq[:, :BLOCK], 0.0).astype(bf16)
        a_t = jnp.where(upper, kq[:, BLOCK:], 0.0).astype(bf16)
        dn = near[h]
        dq = g_ref[j, h]
        acc = acc_ref[h]
        bmat = jnp.concatenate([jnp.concatenate([dn, dq], axis=1), acc.astype(bf16)], axis=0)
        yz = mm(jnp.concatenate([a_t, u], axis=1), bmat).astype(bf16)
        ru = mm_rt(jnp.concatenate([e_s, u], axis=1), bmat)
        inv = inv_ref[0, h]
        left = mm_lt(inv, yz) * (-bp)
        right = -mm(inv, (ru * bp).astype(bf16))
        d_s = jnp.where(strict, -mm_rt(left.astype(bf16), t_ref[0, h]), 0.0).astype(bf16)
        d_e = jnp.where(strict, left[:, :BLOCK], 0.0).astype(bf16)
        d_at = jnp.where(upper, right[:, :BLOCK], 0.0).astype(bf16)
        d_a = d_at.astype(f32).T.astype(bf16)
        uk = jnp.concatenate([u, k], axis=0)
        uq = jnp.concatenate([u, q], axis=0)
        du = left[:, BLOCK:] + right[:, BLOCK:]
        du = du + mm(jnp.concatenate([d_s, d_e], axis=1), uk)
        d_st = d_s.astype(f32).T.astype(bf16)
        du = du + mm(jnp.concatenate([d_st, d_at], axis=1), uq)
        dq_o = dq.astype(f32) + mm(jnp.concatenate([d_a, dn], axis=1), uk)
        dk_o = acc[:, :BLOCK].T + mm_lt(jnp.concatenate([d_e, dn], axis=0), uq)
        uf = u.astype(f32)
        rad = jnp.sum(uf * du, axis=1, keepdims=True)
        du = du - (inv_sq * rad) * uf
        dr = 0.5 * rad * (1.0 - 0.5 * beta)
        dr_all = jnp.where(lane == h, dr, dr_all)
        out_ref[:, cs] = dq_o.astype(bf16)
        out_ref[:, width + h * BLOCK : width + (h + 1) * BLOCK] = dk_o.astype(bf16)
        out_ref[:, 2 * width + h * BLOCK : 2 * width + (h + 1) * BLOCK] = dv_ref[h].astype(bf16)
        out_ref[:, 3 * width + h * BLOCK : 3 * width + (h + 1) * BLOCK] = du.astype(bf16)
    out_ref[:, 4 * width :] = dr_all.astype(bf16)


def attention_prep(proj, heads):
    total = proj.shape[0]
    count = total // BLOCK
    width = heads * BLOCK
    step = 2
    wide = lambda col: pl.BlockSpec((step * BLOCK, width), lambda i: (i, col))
    tile = lambda n: pl.BlockSpec((step, heads, BLOCK, n), lambda i: (i, 0, 0, 0))
    shape = lambda n, t: jax.ShapeDtypeStruct((count, heads, BLOCK, n), t)
    return pl.pallas_call(
        functools.partial(prep_kernel, heads),
        grid=(count // step,),
        in_specs=[wide(0), wide(1), wide(3), pl.BlockSpec((step * BLOCK, BLOCK), lambda i: (i, 4 * heads))],
        out_specs=[tile(BLOCK), pl.BlockSpec((step * BLOCK, width), lambda i: (i, 0)), tile(2 * BLOCK), tile(BLOCK), tile(2 * BLOCK)],
        out_shape=[
            shape(BLOCK, f32),
            jax.ShapeDtypeStruct((total, width), bf16),
            shape(2 * BLOCK, bf16),
            shape(BLOCK, bf16),
            shape(2 * BLOCK, bf16),
        ],
        name="attn_prep",
    )(proj, proj, proj, proj)


def attention_fwd(proj, prep, first, heads, depth):
    near, q0, kp, _, _ = prep
    total = proj.shape[0]
    count = total // BLOCK
    width = heads * BLOCK
    scale = float(BLOCK) ** -0.5
    spec = pltpu.PrefetchScalarGridSpec(
        num_scalar_prefetch=1,
        grid=(count,),
        in_specs=[
            pl.BlockSpec((BLOCK, width), lambda i, f: (i, 0)),
            pl.BlockSpec((1, heads, BLOCK, BLOCK), lambda i, f: (i, 0, 0, 0)),
            pl.BlockSpec((count, heads, BLOCK, 2 * BLOCK), lambda i, f: (0, 0, 0, 0)),
            pl.BlockSpec((total, width), lambda i, f: (0, 2)),
        ],
        out_specs=[
            pl.BlockSpec((BLOCK, width), lambda i, f: (i, 0)),
            pl.BlockSpec((BLOCK, width), lambda i, f: (i, 0)),
            pl.BlockSpec((1, depth, heads, BLOCK, BLOCK), lambda i, f: (i, 0, 0, 0, 0)),
            pl.BlockSpec((1, depth - 1, heads, BLOCK, BLOCK), lambda i, f: (i, 0, 0, 0, 0)),
        ],
        scratch_shapes=[
            pltpu.VMEM((depth, heads, BLOCK, BLOCK), f32),
            pltpu.VMEM((heads, BLOCK, BLOCK), f32),
            pltpu.VMEM((heads, BLOCK, BLOCK), f32),
        ],
    )
    return pl.pallas_call(
        functools.partial(fwd_kernel, heads, depth, scale),
        grid_spec=spec,
        out_shape=[
            jax.ShapeDtypeStruct((total, width), bf16),
            jax.ShapeDtypeStruct((total, width), f32),
            jax.ShapeDtypeStruct((count, depth, heads, BLOCK, BLOCK), bf16),
            jax.ShapeDtypeStruct((count, depth - 1, heads, BLOCK, BLOCK), bf16),
        ],
        name="attn_fwd",
    )(first, q0, near, kp, proj)


def attention_bwd(proj, prep, saved, d_mixed, last, heads, depth):
    _, _, kp, inv, t_all = prep
    mixed, linv, e_all, cur_all = saved
    total = proj.shape[0]
    count = total // BLOCK
    width = heads * BLOCK
    scale = float(BLOCK) ** -0.5
    full = lambda: pl.BlockSpec((total, width), lambda j, f: (0, 0))
    wide = lambda col: pl.BlockSpec((BLOCK, width), lambda j, f: (j, col))
    tile = lambda n: pl.BlockSpec((1, heads, BLOCK, n), lambda j, f: (j, 0, 0, 0))

    def diagonal(d, slot):
        return pl.BlockSpec(
            (1, 1, heads, BLOCK, BLOCK), lambda j, f: (jnp.minimum(j + d, count - 1), slot, 0, 0, 0)
        )

    spec = pltpu.PrefetchScalarGridSpec(
        num_scalar_prefetch=1,
        grid=(count,),
        in_specs=[
            full(),
            full(),
            full(),
            wide(0),
            wide(1),
            wide(2),
            wide(3),
            pl.BlockSpec((BLOCK, BLOCK), lambda j, f: (j, 4 * heads)),
            tile(2 * BLOCK),
            tile(BLOCK),
            tile(2 * BLOCK),
        ]
        + [diagonal(d, d) for d in range(depth)]
        + [diagonal(d, d - 1) for d in range(1, depth)],
        out_specs=pl.BlockSpec((BLOCK, 4 * width + BLOCK), lambda j, f: (j, 0)),
        scratch_shapes=[
            pltpu.VMEM((total, width), bf16),
            pltpu.VMEM((total, width), f32),
            pltpu.VMEM((count, heads, BLOCK, BLOCK), bf16),
            pltpu.VMEM((heads, BLOCK, BLOCK), f32),
            pltpu.VMEM((heads, BLOCK, 2 * BLOCK), f32),
        ],
    )
    return pl.pallas_call(
        functools.partial(bwd_kernel, heads, depth, scale),
        grid_spec=spec,
        out_shape=jax.ShapeDtypeStruct((total, 4 * width + BLOCK), bf16),
        name="attn_bwd",
    )(last, d_mixed, mixed, linv, proj, proj, proj, proj, proj, kp, inv, t_all, *([e_all] * depth), *([cur_all] * (depth - 1)))


def block_tables(packing, begins):
    bins, bin_rows = packing.shape
    per_bin = bin_rows // BLOCK
    place = packing[:, ::BLOCK].reshape(-1) // BLOCK
    start = begins[:, ::BLOCK] // BLOCK + jnp.arange(bins, dtype=jnp.int32)[:, None] * per_bin
    start = start.reshape(-1)
    count = bins * per_bin
    slots = jnp.arange(count, dtype=jnp.int32)
    onehot = place[:, None] == slots[None, :]
    start_place = jnp.sum(jnp.where(start[:, None] == slots[None, :], place[None, :], 0), axis=1)
    first = jnp.sum(jnp.where(onehot, start_place[:, None], 0), axis=0).astype(jnp.int32)
    member = first[None, :] == first[:, None]
    last = jnp.max(jnp.where(member, slots[None, :], 0), axis=1).astype(jnp.int32)
    return first, last, per_bin


def rows_contract(a, b):
    return lax.dot_general(a, b, (((0,), (0,)), ((), ())), preferred_element_type=f32)


def cols_contract(a, b):
    return lax.dot_general(a, b, (((1,), (1,)), ((), ())), preferred_element_type=f32)


def unit_rows(x):
    scale = lax.rsqrt(jnp.mean(x * x, axis=1, keepdims=True) + epsilon)
    return x * scale, scale


def norm_back(grad_normed, unit, scale, gain):
    grad_unit = grad_normed * gain
    grad_gain = jnp.sum(grad_normed * unit, axis=0)
    grad_rows = scale * (grad_unit - unit * jnp.mean(grad_unit * unit, axis=1, keepdims=True))
    return grad_rows, grad_gain


def local(
    tokens,
    cotangent,
    w_query,
    w_key,
    w_value,
    w_house,
    w_beta,
    w_out,
    w_gate,
    w_up,
    w_down,
    gain_attn,
    gain_ffn,
    pack_index,
    seq_start,
):
    first, last, depth = block_tables(pack_index[0], seq_start[0])
    width = w_query.shape[1]
    heads = w_beta.shape[1]
    hidden_width = w_gate.shape[1]
    shard = w_query.shape[0]
    extras = jnp.concatenate(
        [w_beta, gain_attn[:, None], gain_ffn[:, None], jnp.zeros((shard, BLOCK - heads - 2), bf16)], axis=1
    )
    attn_pack = jnp.concatenate([w_query, w_key, w_value, w_house, extras, w_out], axis=1)
    ffn_pack = jnp.concatenate([w_gate, w_up, w_down], axis=1)
    full_tokens = lax.all_gather(tokens, "tp", axis=0, tiled=True)
    attn_full = lax.all_gather(attn_pack, "fsdp", axis=0, tiled=True)
    ffn_full = lax.all_gather(ffn_pack, "fsdp", axis=0, tiled=True)
    full_cot = lax.all_gather(cotangent, "tp", axis=0, tiled=True)
    proj_width = 4 * width + BLOCK
    w_in = attn_full[:, :proj_width]
    full_out = attn_full[:, proj_width:]
    gain_one = attn_full[:, 4 * width + heads].astype(f32)
    gain_two = attn_full[:, 4 * width + heads + 1].astype(f32)

    all_unit, _ = unit_rows(full_tokens.astype(f32))
    normed = (all_unit * gain_one).astype(bf16)
    proj = jnp.dot(normed, w_in, preferred_element_type=f32).astype(bf16)
    prep = attention_prep(proj, heads)
    saved = attention_fwd(proj, prep, first, heads, depth)
    mixed = saved[0]
    attn_part = lax.psum_scatter(
        cols_contract(mixed, full_out).astype(bf16), "tp", scatter_dimension=0, tiled=True
    ).astype(f32)
    x_own = tokens.astype(f32)
    unit_one, scale_one = unit_rows(x_own)
    hidden_in = x_own + attn_part
    unit_two, scale_two = unit_rows(hidden_in)
    normed_two = lax.all_gather((unit_two * gain_two).astype(bf16), "tp", axis=0, tiled=True)
    gate_pre = jnp.dot(normed_two, ffn_full[:, :hidden_width], preferred_element_type=f32)
    up_part = jnp.dot(normed_two, ffn_full[:, hidden_width : 2 * hidden_width], preferred_element_type=f32)
    full_down = ffn_full[:, 2 * hidden_width :]
    hidden = (jax.nn.silu(gate_pre) * up_part).astype(bf16)
    ffn_part = lax.psum_scatter(
        cols_contract(hidden, full_down).astype(bf16), "tp", scatter_dimension=0, tiled=True
    ).astype(f32)
    out_y = (hidden_in + ffn_part).astype(bf16)
    grad_hidden = jnp.dot(full_cot, full_down, preferred_element_type=f32)
    sigma = jax.nn.sigmoid(gate_pre)
    grad_gate = (grad_hidden * up_part * sigma * (1.0 + gate_pre * (1.0 - sigma))).astype(bf16)
    grad_up = (grad_hidden * jax.nn.silu(gate_pre)).astype(bf16)
    gate_up = jnp.concatenate([grad_gate, grad_up], axis=1)
    grad_two = lax.psum_scatter(
        cols_contract(gate_up, ffn_full[:, : 2 * hidden_width]).astype(bf16), "tp", scatter_dimension=0, tiled=True
    ).astype(f32)
    norm_two_grad, grad_gain_two = norm_back(grad_two, unit_two, scale_two, gain_two)
    grad_hidden_in = cotangent.astype(f32) + norm_two_grad
    grad_attn = lax.all_gather(grad_hidden_in.astype(bf16), "tp", axis=0, tiled=True)
    ffn_grads = jnp.concatenate(
        [rows_contract(normed_two, gate_up), rows_contract(full_cot, hidden)], axis=1
    ).astype(bf16)
    ffn_sum = lax.psum_scatter(ffn_grads, "fsdp", scatter_dimension=0, tiled=True).astype(f32)
    d_mixed = jnp.dot(grad_attn, full_out, preferred_element_type=f32).astype(bf16)
    d_proj = attention_bwd(proj, prep, saved, d_mixed, last, heads, depth)
    grad_one = lax.psum_scatter(
        cols_contract(d_proj, w_in).astype(bf16), "tp", scatter_dimension=0, tiled=True
    ).astype(f32)
    norm_one_grad, grad_gain_one = norm_back(grad_one, unit_one, scale_one, gain_one)
    out_dx = (grad_hidden_in + norm_one_grad).astype(bf16)
    attn_grads = jnp.concatenate(
        [rows_contract(normed, d_proj), rows_contract(grad_attn, mixed)], axis=1
    ).astype(bf16)
    attn_sum = lax.psum_scatter(attn_grads, "fsdp", scatter_dimension=0, tiled=True).astype(f32)
    gains = lax.psum(jnp.stack([grad_gain_one, grad_gain_two]), ("fsdp", "tp"))
    gains = lax.dynamic_slice_in_dim(gains, lax.axis_index("fsdp") * shard, shard, 1)
    return (
        out_y,
        out_dx,
        attn_sum[:, :width],
        attn_sum[:, width : 2 * width],
        attn_sum[:, 2 * width : 3 * width],
        attn_sum[:, 3 * width : 4 * width],
        attn_sum[:, 4 * width : 4 * width + heads],
        attn_sum[:, proj_width:],
        ffn_sum[:, :hidden_width],
        ffn_sum[:, hidden_width : 2 * hidden_width],
        ffn_sum[:, 2 * hidden_width :],
        gains[0],
        gains[1],
    )


def solution(mesh):
    rows = P(("fsdp", "tp"), None)
    weight = P("fsdp", "tp")
    return jax.shard_map(
        local,
        mesh=mesh,
        in_specs=(rows, rows) + (weight,) * 9 + (P("fsdp"), P("fsdp"), P("fsdp", None, None), P("fsdp", None, None)),
        out_specs=(rows, rows) + (weight,) * 9 + (P("fsdp"), P("fsdp")),
        check_vma=False,
    )
```

```python
import functools

import jax
import jax.numpy as jnp
from jax import lax
from jax.experimental import pallas as pl
from jax.experimental.pallas import tpu as pltpu
from jax.sharding import PartitionSpec as P

BLOCK = 128
epsilon = 1e-06
bf16 = jnp.bfloat16
f32 = jnp.float32


def mm(a, b):
    return lax.dot_general(a, b, (((1,), (0,)), ((), ())), preferred_element_type=f32)


def mm_rt(a, b):
    return lax.dot_general(a, b, (((1,), (1,)), ((), ())), preferred_element_type=f32)


def mm_lt(a, b):
    return lax.dot_general(a, b, (((0,), (0,)), ((), ())), preferred_element_type=f32)


def iotas():
    rows = lax.broadcasted_iota(jnp.int32, (BLOCK, BLOCK), 0)
    cols = lax.broadcasted_iota(jnp.int32, (BLOCK, BLOCK), 1)
    return rows, cols


def strengths(u, r_col):
    uf = u.astype(f32)
    inv_sq = 1.0 / (jnp.sum(uf * uf, axis=1, keepdims=True) + epsilon)
    beta = 2.0 / (1.0 + jnp.exp(-r_col))
    return beta, inv_sq


def prep_kernel(heads, q_ref, k_ref, u_ref, r_ref, near_ref, q0_ref, kp_ref, inv_ref, t_ref):
    rows, cols = iotas()
    strict = rows > cols
    lower = rows >= cols
    diff = rows ^ cols
    eye = jnp.where(rows == cols, 1.0, 0.0).astype(f32)
    eye_b = eye.astype(bf16)
    chunks = q_ref.shape[0] // BLOCK
    items = [(c, h) for c in range(chunks) for h in range(heads)]
    state = []
    for c, h in items:
        rs, cs = pl.ds(c * BLOCK, BLOCK), pl.ds(h * BLOCK, BLOCK)
        q, k, u = q_ref[rs, cs], k_ref[rs, cs], u_ref[rs, cs]
        beta, inv_sq = strengths(u, r_ref[rs, h : h + 1].astype(f32))
        bp = beta * inv_sq
        big = mm_rt(jnp.concatenate([u, q], axis=0), jnp.concatenate([u, k], axis=0))
        gram = big[:BLOCK, :BLOCK]
        e_s = jnp.where(strict, big[:BLOCK, BLOCK:], 0.0)
        a_s = jnp.where(lower, big[BLOCK:, :BLOCK], 0.0)
        n0 = big[BLOCK:, BLOCK:]
        low = jnp.where(strict, gram * bp, 0.0)
        eu = jnp.concatenate([e_s * bp, u.astype(f32) * bp], axis=1).astype(bf16)
        state.append([q, k, u, a_s.astype(bf16), n0, low, eu, eye - jnp.where(diff < 2, low, 0.0)])
    size = 2
    while size < BLOCK:
        sel = (diff >= size) & (diff < 2 * size)
        prods = []
        for st in state:
            xb = st[7].astype(bf16)
            prods.append((xb, mm(jnp.where(sel, st[5], 0.0).astype(bf16), xb)))
        for st, (xb, y) in zip(state, prods):
            st[7] = st[7] - mm(xb, y.astype(bf16))
        size *= 2
    for (c, h), (q, k, u, a_b, n0, low, eu, x) in zip(items, state):
        rs, cs = pl.ds(c * BLOCK, BLOCK), pl.ds(h * BLOCK, BLOCK)
        xb = x.astype(bf16)
        t = mm(xb, eu).astype(bf16)
        top = mm(a_b, t)
        bot = mm_lt(u, t)
        inv_ref[c, h] = xb
        t_ref[c, h] = t
        near_ref[c, h] = n0 - top[:, :BLOCK]
        q0_ref[rs, cs] = (q.astype(f32) - top[:, BLOCK:]).astype(bf16)
        ket = mm_rt(eye_b, k) - bot[:, :BLOCK]
        kp_ref[c, h] = jnp.concatenate([ket, eye - bot[:, BLOCK:]], axis=1).astype(bf16)


def fwd_kernel(
    heads, depth, scale, first_ref, q0_ref, near_ref, kp_ref, v_ref, o_ref, linv_ref, e_ref, cur_ref, s_ref, m_ref, acc_ref
):
    i = pl.program_id(0)
    first = first_ref[i]
    rows, cols = iotas()
    lower = rows >= cols
    neg = jnp.float32(-1e30)
    for h in range(heads):
        s0 = jnp.where(lower, near_ref[0, h], neg)
        s_ref[0, h] = s0
        m_ref[h] = s0
        cur_ref[0, 0, h] = q0_ref[:, h * BLOCK : (h + 1) * BLOCK]
    for d in range(1, depth):

        @pl.when(i - d >= first)
        def _():
            j = i - d
            for h in range(heads):
                both = mm(cur_ref[0, d - 1, h], kp_ref[j, h])
                s = both[:, :BLOCK]
                s_ref[d, h] = s
                m_ref[h] = jnp.maximum(m_ref[h], s)
                if d + 1 < depth:
                    cur_ref[0, d, h] = both[:, BLOCK:].astype(bf16)

    peaks = []
    for h in range(heads):
        peak = jnp.max(m_ref[h], axis=1, keepdims=True)
        peaks.append(peak)
        e0 = jnp.exp((s_ref[0, h] - peak) * scale)
        m_ref[h] = e0
        eb = e0.astype(bf16)
        e_ref[0, 0, h] = eb
        v = v_ref[pl.ds(pl.multiple_of(i * BLOCK, BLOCK), BLOCK), h * BLOCK : (h + 1) * BLOCK]
        acc_ref[h] = mm(eb, v)
    for d in range(1, depth):

        @pl.when(i - d >= first)
        def _():
            j = i - d
            for h in range(heads):
                e = jnp.exp((s_ref[d, h] - peaks[h]) * scale)
                m_ref[h] = m_ref[h] + e
                eb = e.astype(bf16)
                e_ref[0, d, h] = eb
                v = v_ref[pl.ds(pl.multiple_of(j * BLOCK, BLOCK), BLOCK), h * BLOCK : (h + 1) * BLOCK]
                acc_ref[h] = acc_ref[h] + mm(eb, v)

    for h in range(heads):
        linv = 1.0 / jnp.sum(m_ref[h], axis=1, keepdims=True)
        cs = slice(h * BLOCK, (h + 1) * BLOCK)
        o_ref[:, cs] = (acc_ref[h] * linv).astype(bf16)
        linv_ref[:, cs] = jnp.broadcast_to(linv, (BLOCK, BLOCK))


def bwd_kernel(heads, depth, scale, last_ref, *refs):
    (do_ref, o_ref, linv_ref, q_ref, k_ref, v_ref, u_ref, r_ref, kp_ref, inv_ref, t_ref) = refs[:11]
    e_refs = refs[11 : 11 + depth]
    cur_refs = refs[11 + depth : 10 + 2 * depth]
    out_ref, dop_ref, del_ref, g_ref, dv_ref, acc_ref = refs[10 + 2 * depth :]
    j = pl.program_id(0)
    last = last_ref[j]
    rows, cols = iotas()
    strict = rows > cols
    lower = rows >= cols
    upper = rows <= cols
    total = dop_ref.shape[0]

    @pl.when(j == 0)
    def _():
        for c in range(total // BLOCK):
            rs = pl.ds(c * BLOCK, BLOCK)
            for h in range(heads):
                cs = slice(h * BLOCK, (h + 1) * BLOCK)
                dop = do_ref[rs, cs].astype(f32) * linv_ref[rs, cs]
                delta = jnp.sum(dop * o_ref[rs, cs].astype(f32), axis=1, keepdims=True)
                dop_ref[rs, cs] = dop.astype(bf16)
                del_ref[rs, cs] = jnp.broadcast_to(delta, (BLOCK, BLOCK))
                g_ref[c, h] = jnp.zeros((BLOCK, BLOCK), bf16)

    here = pl.ds(pl.multiple_of(j * BLOCK, BLOCK), BLOCK)
    near = []
    for h in range(heads):
        cs = slice(h * BLOCK, (h + 1) * BLOCK)
        dop = dop_ref[here, cs]
        e = e_refs[0][0, 0, h]
        dp = mm_rt(dop, v_ref[:, cs])
        near.append((e.astype(f32) * (dp - del_ref[here, cs]) * scale).astype(bf16))
        dv_ref[h] = mm_lt(e, dop)
        acc_ref[h] = jnp.zeros((BLOCK, 2 * BLOCK), f32)
    for d in range(1, depth):

        @pl.when(j + d <= last)
        def _():
            i = j + d
            there = pl.ds(pl.multiple_of(i * BLOCK, BLOCK), BLOCK)
            for h in range(heads):
                cs = slice(h * BLOCK, (h + 1) * BLOCK)
                dop = dop_ref[there, cs]
                e = e_refs[d][0, 0, h]
                dp = mm_rt(dop, v_ref[:, cs])
                ds = (e.astype(f32) * (dp - del_ref[there, cs]) * scale).astype(bf16)
                dv_ref[h] = dv_ref[h] + mm_lt(e, dop)
                dsg = jnp.concatenate([ds, g_ref[i, h]], axis=1)
                acc_ref[h] = acc_ref[h] + mm_lt(cur_refs[d - 1][0, 0, h], dsg)
                g_ref[i, h] = mm_rt(dsg, kp_ref[0, h]).astype(bf16)

    lane = cols
    dr_all = jnp.zeros((BLOCK, BLOCK), f32)
    width = heads * BLOCK
    for h in range(heads):
        cs = slice(h * BLOCK, (h + 1) * BLOCK)
        q, k, u = q_ref[:, cs], k_ref[:, cs], u_ref[:, cs]
        beta, inv_sq = strengths(u, r_ref[:, h : h + 1].astype(f32))
        bp = beta * inv_sq
        kq = mm_rt(u, jnp.concatenate([k, q], axis=0))
        e_s = jnp.where(strict, kq[:, :BLOCK], 0.0).astype(bf16)
        a_t = jnp.where(upper, kq[:, BLOCK:], 0.0).astype(bf16)
        dn = near[h]
        dq = g_ref[j, h]
        acc = acc_ref[h]
        bmat = jnp.concatenate([jnp.concatenate([dn, dq], axis=1), acc.astype(bf16)], axis=0)
        yz = mm(jnp.concatenate([a_t, u], axis=1), bmat).astype(bf16)
        ru = mm_rt(jnp.concatenate([e_s, u], axis=1), bmat)
        inv = inv_ref[0, h]
        left = mm_lt(inv, yz) * (-bp)
        right = -mm(inv, (ru * bp).astype(bf16))
        d_s = jnp.where(strict, -mm_rt(left.astype(bf16), t_ref[0, h]), 0.0).astype(bf16)
        d_e = jnp.where(strict, left[:, :BLOCK], 0.0).astype(bf16)
        d_at = jnp.where(upper, right[:, :BLOCK], 0.0).astype(bf16)
        d_a = d_at.astype(f32).T.astype(bf16)
        uk = jnp.concatenate([u, k], axis=0)
        uq = jnp.concatenate([u, q], axis=0)
        du = left[:, BLOCK:] + right[:, BLOCK:]
        du = du + mm(jnp.concatenate([d_s, d_e], axis=1), uk)
        d_st = d_s.astype(f32).T.astype(bf16)
        du = du + mm(jnp.concatenate([d_st, d_at], axis=1), uq)
        dq_o = dq.astype(f32) + mm(jnp.concatenate([d_a, dn], axis=1), uk)
        dk_o = acc[:, :BLOCK].T + mm_lt(jnp.concatenate([d_e, dn], axis=0), uq)
        uf = u.astype(f32)
        rad = jnp.sum(uf * du, axis=1, keepdims=True)
        du = du - (inv_sq * rad) * uf
        dr = 0.5 * rad * (1.0 - 0.5 * beta)
        dr_all = jnp.where(lane == h, dr, dr_all)
        out_ref[:, cs] = dq_o.astype(bf16)
        out_ref[:, width + h * BLOCK : width + (h + 1) * BLOCK] = dk_o.astype(bf16)
        out_ref[:, 2 * width + h * BLOCK : 2 * width + (h + 1) * BLOCK] = dv_ref[h].astype(bf16)
        out_ref[:, 3 * width + h * BLOCK : 3 * width + (h + 1) * BLOCK] = du.astype(bf16)
    out_ref[:, 4 * width :] = dr_all.astype(bf16)


def attention_prep(proj, heads):
    total = proj.shape[0]
    count = total // BLOCK
    width = heads * BLOCK
    step = 2
    wide = lambda col: pl.BlockSpec((step * BLOCK, width), lambda i: (i, col))
    tile = lambda n: pl.BlockSpec((step, heads, BLOCK, n), lambda i: (i, 0, 0, 0))
    shape = lambda n, t: jax.ShapeDtypeStruct((count, heads, BLOCK, n), t)
    return pl.pallas_call(
        functools.partial(prep_kernel, heads),
        grid=(count // step,),
        in_specs=[wide(0), wide(1), wide(3), pl.BlockSpec((step * BLOCK, BLOCK), lambda i: (i, 4 * heads))],
        out_specs=[tile(BLOCK), pl.BlockSpec((step * BLOCK, width), lambda i: (i, 0)), tile(2 * BLOCK), tile(BLOCK), tile(2 * BLOCK)],
        out_shape=[
            shape(BLOCK, f32),
            jax.ShapeDtypeStruct((total, width), bf16),
            shape(2 * BLOCK, bf16),
            shape(BLOCK, bf16),
            shape(2 * BLOCK, bf16),
        ],
        cost_estimate=pl.CostEstimate(flops=count * heads * 22 * 2 * BLOCK**3 * 4, bytes_accessed=20 * total * width, transcendentals=0),
        name="attn_prep",
    )(proj, proj, proj, proj)


def attention_fwd(proj, prep, first, heads, depth):
    near, q0, kp, _, _ = prep
    total = proj.shape[0]
    count = total // BLOCK
    width = heads * BLOCK
    scale = float(BLOCK) ** -0.5
    spec = pltpu.PrefetchScalarGridSpec(
        num_scalar_prefetch=1,
        grid=(count,),
        in_specs=[
            pl.BlockSpec((BLOCK, width), lambda i, f: (i, 0)),
            pl.BlockSpec((1, heads, BLOCK, BLOCK), lambda i, f: (i, 0, 0, 0)),
            pl.BlockSpec((count, heads, BLOCK, 2 * BLOCK), lambda i, f: (0, 0, 0, 0)),
            pl.BlockSpec((total, width), lambda i, f: (0, 2)),
        ],
        out_specs=[
            pl.BlockSpec((BLOCK, width), lambda i, f: (i, 0)),
            pl.BlockSpec((BLOCK, width), lambda i, f: (i, 0)),
            pl.BlockSpec((1, depth, heads, BLOCK, BLOCK), lambda i, f: (i, 0, 0, 0, 0)),
            pl.BlockSpec((1, depth - 1, heads, BLOCK, BLOCK), lambda i, f: (i, 0, 0, 0, 0)),
        ],
        scratch_shapes=[
            pltpu.VMEM((depth, heads, BLOCK, BLOCK), f32),
            pltpu.VMEM((heads, BLOCK, BLOCK), f32),
            pltpu.VMEM((heads, BLOCK, BLOCK), f32),
        ],
    )
    return pl.pallas_call(
        functools.partial(fwd_kernel, heads, depth, scale),
        grid_spec=spec,
        out_shape=[
            jax.ShapeDtypeStruct((total, width), bf16),
            jax.ShapeDtypeStruct((total, width), f32),
            jax.ShapeDtypeStruct((count, depth, heads, BLOCK, BLOCK), bf16),
            jax.ShapeDtypeStruct((count, depth - 1, heads, BLOCK, BLOCK), bf16),
        ],
        cost_estimate=pl.CostEstimate(flops=count * heads * 24 * 2 * BLOCK**3 * 4, bytes_accessed=20 * total * width, transcendentals=0),
        name="attn_fwd",
    )(first, q0, near, kp, proj)


def attention_bwd(proj, prep, saved, d_mixed, last, heads, depth):
    _, _, kp, inv, t_all = prep
    mixed, linv, e_all, cur_all = saved
    total = proj.shape[0]
    count = total // BLOCK
    width = heads * BLOCK
    scale = float(BLOCK) ** -0.5
    full = lambda: pl.BlockSpec((total, width), lambda j, f: (0, 0))
    wide = lambda col: pl.BlockSpec((BLOCK, width), lambda j, f: (j, col))
    tile = lambda n: pl.BlockSpec((1, heads, BLOCK, n), lambda j, f: (j, 0, 0, 0))

    def diagonal(d, slot):
        return pl.BlockSpec(
            (1, 1, heads, BLOCK, BLOCK), lambda j, f: (jnp.minimum(j + d, count - 1), slot, 0, 0, 0)
        )

    spec = pltpu.PrefetchScalarGridSpec(
        num_scalar_prefetch=1,
        grid=(count,),
        in_specs=[
            full(),
            full(),
            full(),
            wide(0),
            wide(1),
            wide(2),
            wide(3),
            pl.BlockSpec((BLOCK, BLOCK), lambda j, f: (j, 4 * heads)),
            tile(2 * BLOCK),
            tile(BLOCK),
            tile(2 * BLOCK),
        ]
        + [diagonal(d, d) for d in range(depth)]
        + [diagonal(d, d - 1) for d in range(1, depth)],
        out_specs=pl.BlockSpec((BLOCK, 4 * width + BLOCK), lambda j, f: (j, 0)),
        scratch_shapes=[
            pltpu.VMEM((total, width), bf16),
            pltpu.VMEM((total, width), f32),
            pltpu.VMEM((count, heads, BLOCK, BLOCK), bf16),
            pltpu.VMEM((heads, BLOCK, BLOCK), f32),
            pltpu.VMEM((heads, BLOCK, 2 * BLOCK), f32),
        ],
    )
    return pl.pallas_call(
        functools.partial(bwd_kernel, heads, depth, scale),
        grid_spec=spec,
        out_shape=jax.ShapeDtypeStruct((total, 4 * width + BLOCK), bf16),
        cost_estimate=pl.CostEstimate(flops=count * heads * 60 * 2 * BLOCK**3 * 4, bytes_accessed=40 * total * width, transcendentals=0),
        name="attn_bwd",
    )(last, d_mixed, mixed, linv, proj, proj, proj, proj, proj, kp, inv, t_all, *([e_all] * depth), *([cur_all] * (depth - 1)))


def block_tables(packing, begins):
    bins, bin_rows = packing.shape
    per_bin = bin_rows // BLOCK
    place = packing[:, ::BLOCK].reshape(-1) // BLOCK
    start = begins[:, ::BLOCK] // BLOCK + jnp.arange(bins, dtype=jnp.int32)[:, None] * per_bin
    start = start.reshape(-1)
    count = bins * per_bin
    slots = jnp.arange(count, dtype=jnp.int32)
    onehot = place[:, None] == slots[None, :]
    start_place = jnp.sum(jnp.where(start[:, None] == slots[None, :], place[None, :], 0), axis=1)
    first = jnp.sum(jnp.where(onehot, start_place[:, None], 0), axis=0).astype(jnp.int32)
    member = first[None, :] == first[:, None]
    last = jnp.max(jnp.where(member, slots[None, :], 0), axis=1).astype(jnp.int32)
    return first, last, per_bin


def rows_contract(a, b):
    return lax.dot_general(a, b, (((0,), (0,)), ((), ())), preferred_element_type=f32)


def cols_contract(a, b):
    return lax.dot_general(a, b, (((1,), (1,)), ((), ())), preferred_element_type=f32)


def unit_rows(x):
    scale = lax.rsqrt(jnp.mean(x * x, axis=1, keepdims=True) + epsilon)
    return x * scale, scale


def norm_back(grad_normed, unit, scale, gain):
    grad_unit = grad_normed * gain
    return scale * (grad_unit - unit * jnp.mean(grad_unit * unit, axis=1, keepdims=True))


def ring_order(count):
    return list(range(0, count, 2)) + list(range(1, count, 2))[::-1]


def ring_tables(axis):
    count = lax.axis_size(axis)
    order = ring_order(count)
    place = [order.index(i) for i in range(count)]
    right = [(order[p], order[(p + 1) % count]) for p in range(count)]
    left = [(order[p], order[(p - 1) % count]) for p in range(count)]
    spot = jnp.asarray(place, jnp.int32)[lax.axis_index(axis)]
    owners = jnp.asarray(order, jnp.int32)
    owner = lambda shift: owners[(spot + shift) % count]
    return count, right, left, owner


class RingGather:
    def __init__(self, x, axis):
        self.axis, self.x = axis, x
        self.count, self.right, self.left, self.owner = ring_tables(axis)
        self.moving = (x, x)
        self.hops = []

    def hop(self):
        from_left, from_right = self.moving
        if len(self.hops) == self.count // 2 - 1:
            half = self.x.shape[0] // 2
            from_left, from_right = from_left[:half], from_right[half:]
        self.moving = (
            lax.ppermute(from_left, self.axis, self.right),
            lax.ppermute(from_right, self.axis, self.left),
        )
        self.hops.append(self.moving)

    def before(self, *values):
        held = lax.optimization_barrier((self.moving,) + values)
        self.moving = held[0]
        self.hops[-1] = self.moving
        return held[1] if len(values) == 1 else held[1:]

    def finish(self):
        while len(self.hops) < self.count // 2:
            self.hop()
        rows = self.x.shape[0]
        put = lax.dynamic_update_slice_in_dim
        out = put(jnp.zeros((self.count * rows, self.x.shape[1]), self.x.dtype), self.x, self.owner(0) * rows, 0)
        for s, (from_left, from_right) in enumerate(self.hops[:-1], 1):
            out = put(out, from_left, self.owner(-s) * rows, 0)
            out = put(out, from_right, self.owner(s) * rows, 0)
        far = self.owner(self.count // 2) * rows
        out = put(out, self.hops[-1][0], far, 0)
        return put(out, self.hops[-1][1], far + rows // 2, 0)


class RingScatter:
    def __init__(self, parts, axis):
        self.axis, self.parts = axis, parts
        self.count, self.right, self.left, self.owner = ring_tables(axis)
        self.rows = parts.shape[0] // self.count
        self.top = self.count // 2
        self.done = 0
        half = self.rows // 2
        self.moving = (self.piece(self.top, 0, half), self.piece(-self.top, half, half))

    def piece(self, shift, start=0, size=None):
        size = self.rows if size is None else size
        return lax.dynamic_slice_in_dim(self.parts, self.owner(shift) * self.rows + start, size, 0)

    def hop(self):
        to_right, to_left = self.moving
        if self.done > 0:
            s = self.top - self.done
            a, b = self.piece(s), self.piece(-s)
            if self.done == 1:
                half = self.rows // 2
                to_right = jnp.concatenate([a[:half] + to_right, a[half:]], axis=0)
                to_left = jnp.concatenate([b[:half], b[half:] + to_left], axis=0)
            else:
                to_right, to_left = a + to_right, b + to_left
        self.moving = (lax.ppermute(to_right, self.axis, self.right), lax.ppermute(to_left, self.axis, self.left))
        self.done += 1

    def before(self, *values):
        held = lax.optimization_barrier((self.moving,) + values)
        self.moving = held[0]
        return held[1] if len(values) == 1 else held[1:]

    def finish(self):
        while self.done < self.top:
            self.hop()
        return self.piece(0).astype(f32) + self.moving[0].astype(f32) + self.moving[1].astype(f32)


def tp_sum(x):
    count = lax.axis_size("tp")
    me = lax.axis_index("tp")
    pieces = [x] + [lax.ppermute(x, "tp", [(i, (i + s) % count) for i in range(count)]) for s in range(1, count)]
    stacked = jnp.stack(pieces)
    slots = (me - jnp.arange(count, dtype=jnp.int32)) % count
    total = jnp.zeros_like(x)
    for r in range(count):
        total = total + jnp.sum(jnp.where((slots == r)[:, None, None], stacked, 0.0), axis=0)
    return total


def after(x, *others):
    return lax.optimization_barrier((x,) + others)[0]


def local(
    tokens,
    cotangent,
    w_query,
    w_key,
    w_value,
    w_house,
    w_beta,
    w_out,
    w_gate,
    w_up,
    w_down,
    gain_attn,
    gain_ffn,
    pack_index,
    seq_start,
):
    first, last, depth = block_tables(pack_index[0], seq_start[0])
    width = w_query.shape[1]
    heads = w_beta.shape[1]
    hidden_width = w_gate.shape[1]
    shard = w_query.shape[0]
    extras = jnp.concatenate(
        [w_beta, gain_attn[:, None], gain_ffn[:, None], jnp.zeros((shard, BLOCK - heads - 2), bf16)], axis=1
    )
    attn_pack = jnp.concatenate([w_query, w_key, w_value, w_house, extras, w_out], axis=1)
    ffn_pack = jnp.concatenate([w_gate, w_up, w_down], axis=1)
    full_tokens = lax.all_gather(tokens, "tp", axis=0, tiled=True)
    attn_full = RingGather(attn_pack, "fsdp").finish()
    ffn_ring = RingGather(after(ffn_pack, attn_full), "fsdp")
    ffn_ring.hop()
    full_cot = lax.all_gather(after(cotangent, full_tokens), "tp", axis=0, tiled=True)
    proj_width = 4 * width + BLOCK
    w_in = attn_full[:, :proj_width]
    full_out = attn_full[:, proj_width:]
    pick = (jnp.arange(BLOCK)[None, :] == heads + jnp.arange(8)[:, None]).astype(bf16)
    gain_rows = cols_contract(pick, attn_full[:, 4 * width : proj_width])
    gain_one, gain_two = gain_rows[0], gain_rows[1]

    all_unit, _ = unit_rows(full_tokens.astype(f32))
    normed = (all_unit * gain_one).astype(bf16)
    proj = jnp.dot(normed, w_in, preferred_element_type=f32).astype(bf16)
    proj = ffn_ring.before(proj)
    ffn_ring.hop()
    prep = list(attention_prep(proj, heads))
    prep[0] = ffn_ring.before(prep[0])
    ffn_ring.hop()
    saved = attention_fwd(proj, prep, first, heads, depth)
    mixed, full_cot = ffn_ring.before(saved[0], full_cot)
    ffn_full = ffn_ring.finish()
    attn_part = lax.psum_scatter(
        cols_contract(mixed, full_out).astype(bf16), "tp", scatter_dimension=0, tiled=True
    ).astype(f32)
    x_own = tokens.astype(f32)
    unit_one, scale_one = unit_rows(x_own)
    hidden_in = x_own + attn_part
    unit_two, scale_two = unit_rows(hidden_in)
    normed_two = lax.all_gather((unit_two * gain_two).astype(bf16), "tp", axis=0, tiled=True)
    gate_pre = jnp.dot(normed_two, ffn_full[:, :hidden_width], preferred_element_type=f32)
    up_part = jnp.dot(normed_two, ffn_full[:, hidden_width : 2 * hidden_width], preferred_element_type=f32)
    full_down = ffn_full[:, 2 * hidden_width :]
    hidden = (jax.nn.silu(gate_pre) * up_part).astype(bf16)
    ffn_rows = cols_contract(hidden, full_down).astype(bf16)
    grad_hidden = jnp.dot(full_cot, full_down, preferred_element_type=f32)
    sigma = jax.nn.sigmoid(gate_pre)
    grad_gate = (grad_hidden * up_part * sigma * (1.0 + gate_pre * (1.0 - sigma))).astype(bf16)
    grad_up = (grad_hidden * jax.nn.silu(gate_pre)).astype(bf16)
    gate_up = jnp.concatenate([grad_gate, grad_up], axis=1)
    grad_two = lax.psum_scatter(
        cols_contract(gate_up, ffn_full[:, : 2 * hidden_width]).astype(bf16), "tp", scatter_dimension=0, tiled=True
    ).astype(f32)
    ffn_grads = jnp.concatenate(
        [rows_contract(normed_two, gate_up), rows_contract(full_cot, hidden)], axis=1
    ).astype(bf16)
    ffn_back = RingScatter(ffn_grads, "fsdp")
    ffn_back.hop()
    grad_two, mixed = ffn_back.before(grad_two, mixed)
    ffn_back.hop()
    norm_two_grad = norm_back(grad_two, unit_two, scale_two, gain_two)
    grad_hidden_in = cotangent.astype(f32) + norm_two_grad
    grad_attn = lax.all_gather(grad_hidden_in.astype(bf16), "tp", axis=0, tiled=True)
    ffn_part = lax.psum_scatter(after(ffn_rows, grad_attn), "tp", scatter_dimension=0, tiled=True).astype(f32)
    out_y = (hidden_in + ffn_part).astype(bf16)
    grad_out = rows_contract(grad_attn, mixed)
    d_mixed = jnp.dot(grad_attn, full_out, preferred_element_type=f32).astype(bf16)
    d_mixed, grad_out = ffn_back.before(d_mixed, grad_out)
    ffn_back.hop()
    d_proj = attention_bwd(proj, prep, saved, d_mixed, last, heads, depth)
    d_proj = ffn_back.before(d_proj)
    attn_grads = jnp.concatenate([rows_contract(normed, d_proj), grad_out], axis=1).astype(bf16)
    attn_back = RingScatter(attn_grads, "fsdp")
    attn_back.hop()
    d_proj = after(d_proj, attn_grads)
    grad_one = lax.psum_scatter(
        cols_contract(d_proj, w_in).astype(bf16), "tp", scatter_dimension=0, tiled=True
    ).astype(f32)
    norm_one_grad = norm_back(grad_one, unit_one, scale_one, gain_one)
    out_dx = (grad_hidden_in + norm_one_grad).astype(bf16)
    ffn_sum = ffn_back.finish()
    attn_sum = attn_back.finish()
    own = lambda grads, weights: jnp.sum(grads * weights.astype(f32), axis=1)
    own_one = own(attn_sum[:, : 4 * width], attn_pack[:, : 4 * width]) + own(
        attn_sum[:, 4 * width : 4 * width + heads], w_beta
    )
    own_two = own(ffn_sum[:, : 2 * hidden_width], ffn_pack[:, : 2 * hidden_width])
    gains = tp_sum(jnp.stack([own_one, own_two])) / jnp.stack([gain_attn, gain_ffn]).astype(f32)
    return (
        out_y,
        out_dx,
        attn_sum[:, :width],
        attn_sum[:, width : 2 * width],
        attn_sum[:, 2 * width : 3 * width],
        attn_sum[:, 3 * width : 4 * width],
        attn_sum[:, 4 * width : 4 * width + heads],
        attn_sum[:, proj_width:],
        ffn_sum[:, :hidden_width],
        ffn_sum[:, hidden_width : 2 * hidden_width],
        ffn_sum[:, 2 * hidden_width :],
        gains[0],
        gains[1],
    )


def solution(mesh):
    rows = P(("fsdp", "tp"), None)
    weight = P("fsdp", "tp")
    return jax.shard_map(
        local,
        mesh=mesh,
        in_specs=(rows, rows) + (weight,) * 9 + (P("fsdp"), P("fsdp"), P("fsdp", None, None), P("fsdp", None, None)),
        out_specs=(rows, rows) + (weight,) * 9 + (P("fsdp"), P("fsdp")),
        check_vma=False,
    )
```

```python
import functools

import jax
import jax.numpy as jnp
from jax import lax
from jax.experimental import pallas as pl
from jax.experimental.pallas import tpu as pltpu
from jax.sharding import PartitionSpec as P

BLOCK = 128
epsilon = 1e-06
bf16 = jnp.bfloat16
f32 = jnp.float32


def mm(a, b):
    return lax.dot_general(a, b, (((1,), (0,)), ((), ())), preferred_element_type=f32)


def mm_rt(a, b):
    return lax.dot_general(a, b, (((1,), (1,)), ((), ())), preferred_element_type=f32)


def mm_lt(a, b):
    return lax.dot_general(a, b, (((0,), (0,)), ((), ())), preferred_element_type=f32)


def iotas():
    rows = lax.broadcasted_iota(jnp.int32, (BLOCK, BLOCK), 0)
    cols = lax.broadcasted_iota(jnp.int32, (BLOCK, BLOCK), 1)
    return rows, cols


def strengths(u, r_col):
    uf = u.astype(f32)
    inv_sq = 1.0 / (jnp.sum(uf * uf, axis=1, keepdims=True) + epsilon)
    beta = 2.0 / (1.0 + jnp.exp(-r_col))
    return beta, inv_sq


def prep_kernel(heads, chunks, table_ref, *refs):
    q_refs, k_refs, u_refs, r_refs = (refs[n * chunks : (n + 1) * chunks] for n in range(4))
    near_ref, q0_ref, kp_ref, inv_ref, t_ref = refs[4 * chunks :]
    rows, cols = iotas()
    strict = rows > cols
    lower = rows >= cols
    diff = rows ^ cols
    eye = jnp.where(rows == cols, 1.0, 0.0).astype(f32)
    eye_b = eye.astype(bf16)
    items = [(c, h) for c in range(chunks) for h in range(heads)]
    state = []
    for c, h in items:
        cs = pl.ds(h * BLOCK, BLOCK)
        q, k, u = q_refs[c][:, cs], k_refs[c][:, cs], u_refs[c][:, cs]
        beta, inv_sq = strengths(u, r_refs[c][:, h : h + 1].astype(f32))
        bp = beta * inv_sq
        big = mm_rt(jnp.concatenate([u, q], axis=0), jnp.concatenate([u, k], axis=0))
        gram = big[:BLOCK, :BLOCK]
        e_s = jnp.where(strict, big[:BLOCK, BLOCK:], 0.0)
        a_s = jnp.where(lower, big[BLOCK:, :BLOCK], 0.0)
        n0 = big[BLOCK:, BLOCK:]
        low = jnp.where(strict, gram * bp, 0.0)
        eu = jnp.concatenate([e_s * bp, u.astype(f32) * bp], axis=1).astype(bf16)
        state.append([q, k, u, a_s.astype(bf16), n0, low, eu, eye - jnp.where(diff < 2, low, 0.0)])
    size = 2
    while size < BLOCK:
        sel = (diff >= size) & (diff < 2 * size)
        prods = []
        for st in state:
            xb = st[7].astype(bf16)
            prods.append((xb, mm(jnp.where(sel, st[5], 0.0).astype(bf16), xb)))
        for st, (xb, y) in zip(state, prods):
            st[7] = st[7] - mm(xb, y.astype(bf16))
        size *= 2
    for (c, h), (q, k, u, a_b, n0, low, eu, x) in zip(items, state):
        rs, cs = pl.ds(c * BLOCK, BLOCK), pl.ds(h * BLOCK, BLOCK)
        xb = x.astype(bf16)
        t = mm(xb, eu).astype(bf16)
        top = mm(a_b, t)
        bot = mm_lt(u, t)
        inv_ref[c, h] = xb
        t_ref[c, h] = t
        near_ref[c, h] = n0 - top[:, :BLOCK]
        q0_ref[rs, cs] = (q.astype(f32) - top[:, BLOCK:]).astype(bf16)
        ket = mm_rt(eye_b, k) - bot[:, :BLOCK]
        kp_ref[c, h] = jnp.concatenate([ket, eye - bot[:, BLOCK:]], axis=1).astype(bf16)


def fwd_kernel(
    heads, depth, scale, first_ref, table_ref, slot_ref, q0_ref, near_ref, kp_ref, v_ref, o_ref, linv_ref, e_ref, cur_ref, s_ref, m_ref, acc_ref
):
    i = pl.program_id(0)
    first = first_ref[i]
    rows, cols = iotas()
    lower = rows >= cols
    neg = jnp.float32(-1e30)
    for h in range(heads):
        s0 = jnp.where(lower, near_ref[0, h], neg)
        s_ref[0, h] = s0
        m_ref[h] = s0
        cur_ref[0, 0, h] = q0_ref[:, h * BLOCK : (h + 1) * BLOCK]
    for d in range(1, depth):

        @pl.when(i - d >= first)
        def _():
            j = i - d
            for h in range(heads):
                both = mm(cur_ref[0, d - 1, h], kp_ref[j, h])
                s = both[:, :BLOCK]
                s_ref[d, h] = s
                m_ref[h] = jnp.maximum(m_ref[h], s)
                if d + 1 < depth:
                    cur_ref[0, d, h] = both[:, BLOCK:].astype(bf16)

    peaks = []
    for h in range(heads):
        peak = jnp.max(m_ref[h], axis=1, keepdims=True)
        peaks.append(peak)
        e0 = jnp.exp((s_ref[0, h] - peak) * scale)
        m_ref[h] = e0
        eb = e0.astype(bf16)
        e_ref[0, 0, h] = eb
        v = v_ref[pl.ds(pl.multiple_of(table_ref[i] * BLOCK, BLOCK), BLOCK), h * BLOCK : (h + 1) * BLOCK]
        acc_ref[h] = mm(eb, v)
    for d in range(1, depth):

        @pl.when(i - d >= first)
        def _():
            j = i - d
            for h in range(heads):
                e = jnp.exp((s_ref[d, h] - peaks[h]) * scale)
                m_ref[h] = m_ref[h] + e
                eb = e.astype(bf16)
                e_ref[0, d, h] = eb
                v = v_ref[pl.ds(pl.multiple_of(table_ref[j] * BLOCK, BLOCK), BLOCK), h * BLOCK : (h + 1) * BLOCK]
                acc_ref[h] = acc_ref[h] + mm(eb, v)

    for h in range(heads):
        linv = 1.0 / jnp.sum(m_ref[h], axis=1, keepdims=True)
        cs = slice(h * BLOCK, (h + 1) * BLOCK)
        o_ref[:, cs] = (acc_ref[h] * linv).astype(bf16)
        linv_ref[:, cs] = jnp.broadcast_to(linv, (BLOCK, BLOCK))


def bwd_kernel(heads, depth, scale, last_ref, table_ref, slot_ref, *refs):
    (do_ref, o_ref, linv_ref, q_ref, k_ref, v_ref, u_ref, r_ref, kp_ref, inv_ref, t_ref) = refs[:11]
    e_refs = refs[11 : 11 + depth]
    cur_refs = refs[11 + depth : 10 + 2 * depth]
    out_ref, dop_ref, del_ref, g_ref, dv_ref, acc_ref = refs[-6:]
    j = pl.program_id(0)
    last = last_ref[j]
    rows, cols = iotas()
    strict = rows > cols
    lower = rows >= cols
    upper = rows <= cols
    total = dop_ref.shape[0]

    @pl.when(j == 0)
    def _():
        for c in range(total // BLOCK):
            rs = pl.ds(c * BLOCK, BLOCK)
            for h in range(heads):
                cs = slice(h * BLOCK, (h + 1) * BLOCK)
                there = pl.ds(pl.multiple_of(slot_ref[c] * BLOCK, BLOCK), BLOCK)
                dop = do_ref[there, cs].astype(f32) * linv_ref[rs, cs]
                delta = jnp.sum(dop * o_ref[there, cs].astype(f32), axis=1, keepdims=True)
                dop_ref[rs, cs] = dop.astype(bf16)
                del_ref[rs, cs] = jnp.broadcast_to(delta, (BLOCK, BLOCK))
                g_ref[c, h] = jnp.zeros((BLOCK, BLOCK), bf16)

    here = pl.ds(pl.multiple_of(j * BLOCK, BLOCK), BLOCK)
    near = []
    for h in range(heads):
        cs = slice(h * BLOCK, (h + 1) * BLOCK)
        dop = dop_ref[here, cs]
        e = e_refs[0][0, 0, h]
        dp = mm_rt(dop, v_ref[:, cs])
        near.append((e.astype(f32) * (dp - del_ref[here, cs]) * scale).astype(bf16))
        dv_ref[h] = mm_lt(e, dop)
        acc_ref[h] = jnp.zeros((BLOCK, 2 * BLOCK), f32)
    for d in range(1, depth):

        @pl.when(j + d <= last)
        def _():
            i = j + d
            there = pl.ds(pl.multiple_of(i * BLOCK, BLOCK), BLOCK)
            for h in range(heads):
                cs = slice(h * BLOCK, (h + 1) * BLOCK)
                dop = dop_ref[there, cs]
                e = e_refs[d][0, 0, h]
                dp = mm_rt(dop, v_ref[:, cs])
                ds = (e.astype(f32) * (dp - del_ref[there, cs]) * scale).astype(bf16)
                dv_ref[h] = dv_ref[h] + mm_lt(e, dop)
                dsg = jnp.concatenate([ds, g_ref[i, h]], axis=1)
                acc_ref[h] = acc_ref[h] + mm_lt(cur_refs[d - 1][0, 0, h], dsg)
                g_ref[i, h] = mm_rt(dsg, kp_ref[0, h]).astype(bf16)

    lane = cols
    dr_all = jnp.zeros((BLOCK, BLOCK), f32)
    width = heads * BLOCK
    for h in range(heads):
        cs = slice(h * BLOCK, (h + 1) * BLOCK)
        q, k, u = q_ref[:, cs], k_ref[:, cs], u_ref[:, cs]
        beta, inv_sq = strengths(u, r_ref[:, h : h + 1].astype(f32))
        bp = beta * inv_sq
        kq = mm_rt(u, jnp.concatenate([k, q], axis=0))
        e_s = jnp.where(strict, kq[:, :BLOCK], 0.0).astype(bf16)
        a_t = jnp.where(upper, kq[:, BLOCK:], 0.0).astype(bf16)
        dn = near[h]
        dq = g_ref[j, h]
        acc = acc_ref[h]
        bmat = jnp.concatenate([jnp.concatenate([dn, dq], axis=1), acc.astype(bf16)], axis=0)
        yz = mm(jnp.concatenate([a_t, u], axis=1), bmat).astype(bf16)
        ru = mm_rt(jnp.concatenate([e_s, u], axis=1), bmat)
        inv = inv_ref[0, h]
        left = mm_lt(inv, yz) * (-bp)
        right = -mm(inv, (ru * bp).astype(bf16))
        d_s = jnp.where(strict, -mm_rt(left.astype(bf16), t_ref[0, h]), 0.0).astype(bf16)
        d_e = jnp.where(strict, left[:, :BLOCK], 0.0).astype(bf16)
        d_at = jnp.where(upper, right[:, :BLOCK], 0.0).astype(bf16)
        d_a = d_at.astype(f32).T.astype(bf16)
        uk = jnp.concatenate([u, k], axis=0)
        uq = jnp.concatenate([u, q], axis=0)
        du = left[:, BLOCK:] + right[:, BLOCK:]
        du = du + mm(jnp.concatenate([d_s, d_e], axis=1), uk)
        d_st = d_s.astype(f32).T.astype(bf16)
        du = du + mm(jnp.concatenate([d_st, d_at], axis=1), uq)
        dq_o = dq.astype(f32) + mm(jnp.concatenate([d_a, dn], axis=1), uk)
        dk_o = acc[:, :BLOCK].T + mm_lt(jnp.concatenate([d_e, dn], axis=0), uq)
        uf = u.astype(f32)
        rad = jnp.sum(uf * du, axis=1, keepdims=True)
        du = du - (inv_sq * rad) * uf
        dr = 0.5 * rad * (1.0 - 0.5 * beta)
        dr_all = jnp.where(lane == h, dr, dr_all)
        out_ref[:, cs] = dq_o.astype(bf16)
        out_ref[:, width + h * BLOCK : width + (h + 1) * BLOCK] = dk_o.astype(bf16)
        out_ref[:, 2 * width + h * BLOCK : 2 * width + (h + 1) * BLOCK] = dv_ref[h].astype(bf16)
        out_ref[:, 3 * width + h * BLOCK : 3 * width + (h + 1) * BLOCK] = du.astype(bf16)
    out_ref[:, 4 * width :] = dr_all.astype(bf16)


def attention_prep(proj, table, heads):
    count = table.shape[0]
    width = heads * BLOCK
    step = 2

    def rows(c, n, col):
        return pl.BlockSpec((BLOCK, n), lambda i, t: (t[i * step + c], col))

    tile = lambda n: pl.BlockSpec((step, heads, BLOCK, n), lambda i, t: (i, 0, 0, 0))
    shape = lambda n, t: jax.ShapeDtypeStruct((count, heads, BLOCK, n), t)
    spec = pltpu.PrefetchScalarGridSpec(
        num_scalar_prefetch=1,
        grid=(count // step,),
        in_specs=[rows(c, width, col) for col in (0, 1, 3) for c in range(step)]
        + [rows(c, BLOCK, 4 * heads) for c in range(step)],
        out_specs=[
            tile(BLOCK),
            pl.BlockSpec((step * BLOCK, width), lambda i, t: (i, 0)),
            tile(2 * BLOCK),
            tile(BLOCK),
            tile(2 * BLOCK),
        ],
    )
    return pl.pallas_call(
        functools.partial(prep_kernel, heads, step),
        grid_spec=spec,
        out_shape=[
            shape(BLOCK, f32),
            jax.ShapeDtypeStruct((count * BLOCK, width), bf16),
            shape(2 * BLOCK, bf16),
            shape(BLOCK, bf16),
            shape(2 * BLOCK, bf16),
        ],
        cost_estimate=pl.CostEstimate(
            flops=count * heads * 45 * BLOCK**3, bytes_accessed=6 * count * BLOCK * width, transcendentals=0
        ),
        name="attn_prep",
    )(table, *([proj] * (4 * step)))


def attention_fwd(proj, prep, first, table, slot, heads):
    near, q0, kp, _, _ = prep
    count = table.shape[0]
    depth = count
    width = heads * BLOCK
    scale = float(BLOCK) ** -0.5
    spec = pltpu.PrefetchScalarGridSpec(
        num_scalar_prefetch=3,
        grid=(count,),
        in_specs=[
            pl.BlockSpec((BLOCK, width), lambda i, f, t, w: (i, 0)),
            pl.BlockSpec((1, heads, BLOCK, BLOCK), lambda i, f, t, w: (i, 0, 0, 0)),
            pl.BlockSpec((count, heads, BLOCK, 2 * BLOCK), lambda i, f, t, w: (0, 0, 0, 0)),
            pl.BlockSpec((proj.shape[0], width), lambda i, f, t, w: (0, 2)),
        ],
        out_specs=[
            pl.BlockSpec((BLOCK, width), lambda i, f, t, w: (w[i], 0)),
            pl.BlockSpec((BLOCK, width), lambda i, f, t, w: (i, 0)),
            pl.BlockSpec((1, depth, heads, BLOCK, BLOCK), lambda i, f, t, w: (i, 0, 0, 0, 0)),
            pl.BlockSpec((1, depth - 1, heads, BLOCK, BLOCK), lambda i, f, t, w: (i, 0, 0, 0, 0)),
        ],
        scratch_shapes=[
            pltpu.VMEM((depth, heads, BLOCK, BLOCK), f32),
            pltpu.VMEM((heads, BLOCK, BLOCK), f32),
            pltpu.VMEM((heads, BLOCK, BLOCK), f32),
        ],
    )
    return pl.pallas_call(
        functools.partial(fwd_kernel, heads, depth, scale),
        grid_spec=spec,
        out_shape=[
            jax.ShapeDtypeStruct((count * BLOCK, width), bf16),
            jax.ShapeDtypeStruct((count * BLOCK, width), f32),
            jax.ShapeDtypeStruct((count, depth, heads, BLOCK, BLOCK), bf16),
            jax.ShapeDtypeStruct((count, depth - 1, heads, BLOCK, BLOCK), bf16),
        ],
        cost_estimate=pl.CostEstimate(
            flops=count * heads * 48 * BLOCK**3, bytes_accessed=6 * count * BLOCK * width, transcendentals=0
        ),
        name="attn_fwd",
    )(first, table, slot, q0, near, kp, proj)


def attention_bwd(proj, prep, saved, d_mixed, last, table, slot, heads, filled):
    _, _, kp, inv, t_all = prep
    mixed, linv, e_all, cur_all = saved
    count = table.shape[0]
    depth = count
    total = count * BLOCK
    width = heads * BLOCK
    scale = float(BLOCK) ** -0.5
    full = lambda: pl.BlockSpec((total, width), lambda j, f, t, w: (0, 0))
    wide = lambda col: pl.BlockSpec((BLOCK, width), lambda j, f, t, w: (t[j], col))
    tile = lambda n: pl.BlockSpec((1, heads, BLOCK, n), lambda j, f, t, w: (j, 0, 0, 0))

    def diagonal(d, slot):
        return pl.BlockSpec(
            (1, 1, heads, BLOCK, BLOCK), lambda j, f, t, w: (jnp.minimum(j + d, count - 1), slot, 0, 0, 0)
        )

    in_specs = [
        full(),
        full(),
        full(),
        wide(0),
        wide(1),
        wide(2),
        wide(3),
        pl.BlockSpec((BLOCK, BLOCK), lambda j, f, t, w: (t[j], 4 * heads)),
        tile(2 * BLOCK),
        tile(BLOCK),
        tile(2 * BLOCK),
    ]
    in_specs += [diagonal(d, d) for d in range(depth)] + [diagonal(d, d - 1) for d in range(1, depth)]
    operands = [last, table, slot, d_mixed, mixed, linv, proj, proj, proj, proj, proj, kp, inv, t_all]
    operands += [e_all] * depth + [cur_all] * (depth - 1)
    aliases = {}
    if filled is not None:
        aliases = {len(operands): 0}
        in_specs.append(pl.BlockSpec(memory_space=pl.ANY))
        operands.append(filled)
    spec = pltpu.PrefetchScalarGridSpec(
        num_scalar_prefetch=3,
        grid=(count,),
        in_specs=in_specs,
        out_specs=pl.BlockSpec((BLOCK, 4 * width + BLOCK), lambda j, f, t, w: (t[j], 0)),
        scratch_shapes=[
            pltpu.VMEM((total, width), bf16),
            pltpu.VMEM((total, width), f32),
            pltpu.VMEM((count, heads, BLOCK, BLOCK), bf16),
            pltpu.VMEM((heads, BLOCK, BLOCK), f32),
            pltpu.VMEM((heads, BLOCK, 2 * BLOCK), f32),
        ],
    )
    return pl.pallas_call(
        functools.partial(bwd_kernel, heads, depth, scale),
        grid_spec=spec,
        out_shape=jax.ShapeDtypeStruct((proj.shape[0], 4 * width + BLOCK), bf16),
        input_output_aliases=aliases,
        cost_estimate=pl.CostEstimate(
            flops=count * heads * 120 * BLOCK**3, bytes_accessed=8 * total * width, transcendentals=0
        ),
        name="attn_bwd",
    )(*operands)


def gather_kernel(group, table_ref, *refs):
    outs = refs[-(len(refs) // (group + 1)) :]
    for m, dst in enumerate(outs):
        for c in range(group):
            dst[c * BLOCK : (c + 1) * BLOCK, :] = refs[m * group + c][...]


def gather_blocks(x, tables, group):
    streams, count = tables.shape
    cols = x.shape[1]

    def source(m, c):
        return pl.BlockSpec((BLOCK, cols), lambda i, t: (t[m * count + i * group + c], 0))

    spec = pltpu.PrefetchScalarGridSpec(
        num_scalar_prefetch=1,
        grid=(count // group,),
        in_specs=[source(m, c) for m in range(streams) for c in range(group)],
        out_specs=[pl.BlockSpec((group * BLOCK, cols), lambda i, t: (i, 0))] * streams,
    )
    return pl.pallas_call(
        functools.partial(gather_kernel, group),
        grid_spec=spec,
        out_shape=[jax.ShapeDtypeStruct((count * BLOCK, cols), x.dtype)] * streams,
        cost_estimate=pl.CostEstimate(flops=0, bytes_accessed=4 * streams * count * BLOCK * cols, transcendentals=0),
        name="gather_blocks",
    )(tables.reshape(-1), *([x] * (group * streams)))


def pick_kernel(bounds, table_ref, *refs):
    at = table_ref[pl.program_id(0)]
    for n, (low, high) in enumerate(bounds):

        @pl.when((at >= low) & (at < high))
        def _():
            refs[-1][...] = refs[n][...]


def pick_blocks(parts, table):
    cols = parts[0].shape[1]
    bounds, low = [], 0
    for part in parts:
        bounds.append((low, low + part.shape[0] // BLOCK))
        low = bounds[-1][1]

    def source(low, high):
        return pl.BlockSpec((BLOCK, cols), lambda i, t: (jnp.clip(t[i] - low, 0, high - low - 1), 0))

    spec = pltpu.PrefetchScalarGridSpec(
        num_scalar_prefetch=1,
        grid=(table.shape[0],),
        in_specs=[source(*bound) for bound in bounds],
        out_specs=pl.BlockSpec((BLOCK, cols), lambda i, t: (i, 0)),
    )
    return pl.pallas_call(
        functools.partial(pick_kernel, bounds),
        grid_spec=spec,
        out_shape=jax.ShapeDtypeStruct((table.shape[0] * BLOCK, cols), parts[0].dtype),
        cost_estimate=pl.CostEstimate(flops=0, bytes_accessed=4 * table.shape[0] * BLOCK * cols, transcendentals=0),
        name="pick_blocks",
    )(table, *parts)


def place_kernel(count, rows, spot_ref, *refs):
    pieces, out, bufs, sem_in, sem_out = refs[:count], refs[count], refs[count + 1], refs[count + 2], refs[count + 3]
    loads = [pltpu.make_async_copy(pieces[n], bufs.at[n], sem_in.at[n]) for n in range(count)]
    for load in loads:
        load.start()
    stores = []
    for n in range(count):
        loads[n].wait()
        to = out.at[pl.ds(pl.multiple_of(spot_ref[n] * rows, rows), rows), :]
        stores.append(pltpu.make_async_copy(bufs.at[n], to, sem_out.at[n]))
        stores[n].start()
    for store in stores:
        store.wait()


def place_pieces(pieces, spots, count):
    rows, cols = pieces[0].shape
    held = len(pieces)
    dtype = pieces[0].dtype
    spec = pltpu.PrefetchScalarGridSpec(
        num_scalar_prefetch=1,
        grid=(1,),
        in_specs=[pl.BlockSpec(memory_space=pl.ANY)] * held,
        out_specs=pl.BlockSpec(memory_space=pl.ANY),
        scratch_shapes=[
            pltpu.VMEM((held, rows, cols), dtype),
            pltpu.SemaphoreType.DMA((held,)),
            pltpu.SemaphoreType.DMA((held,)),
        ],
    )
    where = jnp.concatenate([jnp.reshape(spot, (1,)) for spot in spots]).astype(jnp.int32)
    return pl.pallas_call(
        functools.partial(place_kernel, held, rows),
        grid_spec=spec,
        out_shape=jax.ShapeDtypeStruct((count * rows, cols), dtype),
        cost_estimate=pl.CostEstimate(flops=0, bytes_accessed=4 * held * rows * cols, transcendentals=0),
        name="place_pieces",
    )(where, *pieces)


def open_kernel(spot_ref, x_ref, out_ref):
    out_ref[...] = x_ref[...]


def open_buffer(x, spot, count):
    rows, cols = x.shape
    spec = pltpu.PrefetchScalarGridSpec(
        num_scalar_prefetch=1,
        grid=(2,),
        in_specs=[pl.BlockSpec((rows // 2, cols), lambda i, t: (i, 0))],
        out_specs=pl.BlockSpec((rows // 2, cols), lambda i, t: (2 * t[0] + i, 0)),
    )
    return pl.pallas_call(
        open_kernel,
        grid_spec=spec,
        out_shape=jax.ShapeDtypeStruct((count * rows, cols), x.dtype),
        cost_estimate=pl.CostEstimate(flops=0, bytes_accessed=4 * rows * cols, transcendentals=0),
        name="open_buffer",
    )(jnp.reshape(spot, (1,)).astype(jnp.int32), x)


def rows_contract(a, b):
    return lax.dot_general(a, b, (((0,), (0,)), ((), ())), preferred_element_type=f32)


def cols_contract(a, b):
    return lax.dot_general(a, b, (((1,), (1,)), ((), ())), preferred_element_type=f32)


def unit_rows(x):
    scale = lax.rsqrt(jnp.mean(x * x, axis=1, keepdims=True) + epsilon)
    return x * scale, scale


def norm_back(grad_normed, unit, scale, gain):
    grad_unit = grad_normed * gain
    return scale * (grad_unit - unit * jnp.mean(grad_unit * unit, axis=1, keepdims=True))


def ring_order(count):
    return list(range(0, count, 2)) + list(range(1, count, 2))[::-1]


def ring_tables(axis):
    count = lax.axis_size(axis)
    order = ring_order(count)
    right = [(order[p], order[(p + 1) % count]) for p in range(count)]
    left = [(order[p], order[(p - 1) % count]) for p in range(count)]
    me = lax.axis_index(axis)
    spot = jnp.where(me % 2 == 0, me // 2, count - 1 - me // 2)

    def owner(shift):
        at = (spot + shift + count) % count
        return jnp.where(at < count // 2, 2 * at, 2 * (count - 1 - at) + 1)

    return count, right, left, owner


class RingGather:
    def __init__(self, x, axis, whole=False):
        self.axis, self.x, self.whole = axis, x, whole
        self.count, self.right, self.left, self.owner = ring_tables(axis)
        self.moving = (x, x)
        self.hops = []

    def hop(self):
        from_left, from_right = self.moving
        if len(self.hops) == self.count // 2 - 1:
            half = self.x.shape[0] // 2
            from_left, from_right = from_left[:half], from_right[half:]
        self.moving = (
            lax.ppermute(from_left, self.axis, self.right),
            lax.ppermute(from_right, self.axis, self.left),
        )
        self.hops.append(self.moving)

    def before(self, *values):
        held = lax.optimization_barrier((self.moving,) + values)
        self.moving = held[0]
        self.hops[-1] = self.moving
        return held[1] if len(values) == 1 else held[1:]

    def finish(self):
        while len(self.hops) < self.count // 2:
            self.hop()
        rows = self.x.shape[0]
        put = lax.dynamic_update_slice_in_dim
        pieces, spots = [self.x], [self.owner(0)]
        for s, (from_left, from_right) in enumerate(self.hops[:-1], 1):
            pieces += [from_left, from_right]
            spots += [self.owner(-s), self.owner(s)]
        if self.whole:
            out = place_pieces(pieces, spots, self.count)
        else:
            out = open_buffer(self.x, spots[0], self.count)
            for piece, spot in zip(pieces[1:], spots[1:]):
                out = put(out, piece, spot * rows, 0)
        far = self.owner(self.count // 2) * rows
        out = put(out, self.hops[-1][0], far, 0)
        return put(out, self.hops[-1][1], far + rows // 2, 0)


class RingScatter:
    def __init__(self, parts, axis):
        self.axis, self.parts = axis, parts
        self.count, self.right, self.left, self.owner = ring_tables(axis)
        self.rows = parts[0].shape[0] // self.count
        self.top = self.count // 2
        self.done = 0
        half = self.rows // 2
        self.moving = (self.piece(self.top, 0, half), self.piece(-self.top, half, half))

    def piece(self, shift, start=0, size=None):
        size = self.rows if size is None else size
        at = self.owner(shift) * self.rows + start
        return jnp.concatenate([lax.dynamic_slice_in_dim(part, at, size, 0) for part in self.parts], axis=1)

    def hop(self):
        to_right, to_left = self.moving
        if self.done > 0:
            s = self.top - self.done
            a, b = self.piece(s), self.piece(-s)
            if self.done == 1:
                half = self.rows // 2
                to_right = jnp.concatenate([a[:half] + to_right, a[half:]], axis=0)
                to_left = jnp.concatenate([b[:half], b[half:] + to_left], axis=0)
            else:
                to_right, to_left = a + to_right, b + to_left
        self.moving = (lax.ppermute(to_right, self.axis, self.right), lax.ppermute(to_left, self.axis, self.left))
        self.done += 1

    def before(self, *values):
        held = lax.optimization_barrier((self.moving,) + values)
        self.moving = held[0]
        return held[1] if len(values) == 1 else held[1:]

    def finish(self):
        while self.done < self.top:
            self.hop()
        return self.piece(0).astype(f32) + self.moving[0].astype(f32) + self.moving[1].astype(f32)


def tp_sum(x):
    count = lax.axis_size("tp")
    me = lax.axis_index("tp")
    pieces = [x] + [lax.ppermute(x, "tp", [(i, (i + s) % count) for i in range(count)]) for s in range(1, count)]
    stacked = jnp.stack(pieces)
    slots = (me - jnp.arange(count, dtype=jnp.int32)) % count
    total = jnp.zeros_like(x)
    for r in range(count):
        total = total + jnp.sum(jnp.where((slots == r)[:, None, None], stacked, 0.0), axis=0)
    return total


SLOTS = (0, 2, 1, 3)


def across(x):
    return lax.ppermute(x, "tp", [(i, i ^ 2) for i in range(4)])


def beside(x):
    return lax.ppermute(x, "tp", [(i, i ^ 1) for i in range(4)])


def share(rows):
    size = rows.shape[0] // 4
    other = beside(rows[2 * size :])
    pair = rows[: 2 * size].astype(f32) + other.astype(f32)
    return pair[:size], across(pair[size:].astype(bf16))


def spread(x):
    pair = jnp.concatenate([x, across(x)], axis=0)
    return jnp.concatenate([pair, beside(pair)], axis=0)


def together(*values):
    return lax.optimization_barrier(values)


def local(
    tokens,
    cotangent,
    w_query,
    w_key,
    w_value,
    w_house,
    w_beta,
    w_out,
    w_gate,
    w_up,
    w_down,
    gain_attn,
    gain_ffn,
    pack_index,
    seq_start,
):
    packing, begins = pack_index[0], seq_start[0]
    bins, bin_rows = packing.shape
    per_bin = bin_rows // BLOCK
    streams = range(bins)
    width = w_query.shape[1]
    heads = w_beta.shape[1]
    hidden_width = w_gate.shape[1]
    shard = w_query.shape[0]
    ranks = 4
    assert lax.axis_size("tp") == ranks
    half = bin_rows // ranks
    per_half = half // BLOCK
    me = lax.axis_index("tp")

    given = packing[:, ::BLOCK] // BLOCK
    per_own = bins * per_half
    table = given
    first = begins[:, ::BLOCK] // BLOCK
    spots = jnp.arange(per_bin, dtype=jnp.int32)
    last = jnp.max(jnp.where(first[:, :, None] == first[:, None, :], spots[None, None, :], 0), axis=2)
    away = me ^ (spots // per_half)
    slot = ((away // 2) + 2 * (away % 2)) * per_half + spots % per_half
    places = jnp.arange(bins, dtype=jnp.int32)[:, None] * per_bin + slot[None, :]
    blocks = jnp.arange(bins * per_bin, dtype=jnp.int32)
    inverse = jnp.sum(jnp.where(given.reshape(-1)[:, None] == blocks[None, :], places.reshape(-1)[:, None], 0), axis=0)
    slotted = jnp.sum(jnp.where(slot[None, :, None] == spots[None, None, :], given[:, :, None], 0), axis=1)
    packed = jnp.sum(jnp.where(given.reshape(-1)[:, None] == blocks[None, :], blocks[:, None], 0), axis=0)
    mine = (blocks // per_own == me) & (blocks >= 0)
    pull = jnp.arange(per_own, dtype=jnp.int32)[:, None] == jnp.where(mine, blocks % per_own, -1)[None, :]
    own_places = jnp.sum(jnp.where(pull, inverse[None, :], 0), axis=1)
    own_packed = jnp.sum(jnp.where(pull, packed[None, :], 0), axis=1)
    origin = me ^ (own_packed % per_bin // per_half)
    own_spots = ((origin // 2) + 2 * (origin % 2)) * per_own + own_packed // per_bin * per_half + own_packed % per_half
    tables = (table.astype(jnp.int32), first, last, slot, slotted, own_places, own_spots)

    extras = jnp.concatenate(
        [w_beta, gain_attn[:, None], gain_ffn[:, None], jnp.zeros((shard, BLOCK - heads - 2), bf16)], axis=1
    )
    attn_pack = jnp.concatenate([w_query, w_key, w_value, w_house, extras], axis=1)
    ffn_pack = jnp.concatenate([w_gate, w_up, w_down], axis=1)
    full_tokens = lax.all_gather(tokens, "tp", axis=0, tiled=True)
    attn_ring = RingGather(attn_pack, "fsdp")
    attn_ring.hop()
    table, first, last, slot, slotted, own_places, own_spots = attn_ring.before(*tables)
    while len(attn_ring.hops) < attn_ring.count // 2 - 1:
        attn_ring.hop()
    full_tokens, out_shard, cotangent = attn_ring.before(full_tokens, w_out, cotangent)
    w_in, ffn_pack, out_shard, cotangent = together(attn_ring.finish(), ffn_pack, out_shard, cotangent)
    ffn_ring = RingGather(ffn_pack, "fsdp", True)
    ffn_ring.hop()
    x_rows = gather_blocks(full_tokens, slotted[:, :per_half], per_half)
    full_out = lax.all_gather(out_shard, "fsdp", axis=0, tiled=True)
    full_cot = lax.all_gather(cotangent, "tp", axis=0, tiled=True)
    pick = (jnp.arange(BLOCK)[None, :] == heads + jnp.arange(8)[:, None]).astype(bf16)
    gain_rows = cols_contract(pick, w_in[:, 4 * width :])
    gain_one, gain_two = gain_rows[0], gain_rows[1]

    all_unit, _ = unit_rows(full_tokens.astype(f32))
    normed = (all_unit * gain_one).astype(bf16)
    proj = jnp.dot(normed, w_in, preferred_element_type=f32).astype(bf16)

    def attend(m):
        prep = attention_prep(proj, table[m], heads)
        return prep, lambda prep: attention_fwd(proj, prep, first[m], table[m], slot, heads)

    preps, saved, hidden_in, unit_two, scale_two, normed_two = [], [], [], [], [], []

    def close(m, own, far):
        hidden_in.append(x_rows[m].astype(f32) + own + far.astype(f32))
        unit, scale = unit_rows(hidden_in[m])
        unit_two.append(unit)
        scale_two.append(scale)
        return (unit * gain_two).astype(bf16)

    prep, run = attend(0)
    prep = list(prep)
    prep[0] = ffn_ring.before(prep[0])
    ffn_ring.hop()
    preps.append(prep)
    saved.append(list(run(prep)))
    rows = ffn_ring.before(cols_contract(saved[0][0], full_out).astype(bf16))
    ffn_ring.hop()
    attn_own, attn_far = share(rows)
    proj, attn_own = together(proj, attn_own)
    prep, run = attend(1)
    prep = list(prep)
    prep[0], attn_far = ffn_ring.before(prep[0], attn_far)
    while len(ffn_ring.hops) < ffn_ring.count // 2:
        ffn_ring.hop()
    preps.append(prep)
    normed_own = close(0, attn_own, attn_far)
    normed_far = across(normed_own)
    prep[0], normed_own = together(prep[0], normed_own)
    saved.append(list(run(prep)))
    saved[1][0], normed_far, full_cot = together(saved[1][0], normed_far, full_cot)
    pair = jnp.concatenate([normed_own, normed_far], axis=0)
    normed_two.append(jnp.concatenate([pair, beside(pair)], axis=0))
    attn_own, attn_far = share(cols_contract(saved[1][0], full_out).astype(bf16))
    attn_own, full_cot, ffn_ring.x = together(attn_own, full_cot, ffn_ring.x)
    ffn_full = ffn_ring.finish()
    cot_rows = list(gather_blocks(full_cot, slotted, 4))

    full_gate, full_up = ffn_full[:, :hidden_width], ffn_full[:, hidden_width : 2 * hidden_width]
    full_gate_up, full_down = ffn_full[:, : 2 * hidden_width], ffn_full[:, 2 * hidden_width :]
    hidden, gate_up, back = [], [], []

    def ffn(m, rows, middle):
        gate_pre = jnp.dot(rows, full_gate, preferred_element_type=f32)
        up_part = jnp.dot(rows, full_up, preferred_element_type=f32)
        cot_rows[m] = middle(cot_rows[m])
        hidden.append((jax.nn.silu(gate_pre) * up_part).astype(bf16))
        grad_hidden = jnp.dot(cot_rows[m], full_down, preferred_element_type=f32)
        sigma = jax.nn.sigmoid(gate_pre)
        grad_gate = (grad_hidden * up_part * sigma * (1.0 + gate_pre * (1.0 - sigma))).astype(bf16)
        grad_up = (grad_hidden * jax.nn.silu(gate_pre)).astype(bf16)
        gate_up.append(jnp.concatenate([grad_gate, grad_up], axis=1))

    def ffn_back_rows(m):
        return cols_contract(gate_up[m], full_gate_up).astype(bf16)

    flying = {}

    def middle(rows):
        rows, own, far = together(rows, attn_own, attn_far)
        mine = close(1, own, far)
        flying[0], flying[1] = mine, across(mine)
        return rows

    ffn(0, normed_two[0], middle)
    normed_own, normed_far = flying[0], flying[1]
    rows, normed_own, normed_far = together(ffn_back_rows(0), normed_own, normed_far)
    back_own, back_far = share(rows)
    pair = jnp.concatenate([normed_own, normed_far], axis=0)
    normed_two.append(jnp.concatenate([pair, beside(pair)], axis=0))
    grad_attn = []

    def close_back(m, own, far):
        norm_two_grad = norm_back(own + far.astype(f32), unit_two[m], scale_two[m], gain_two)
        cot_own = cot_rows[m][:half].astype(f32)
        return (cot_own + norm_two_grad).astype(bf16)

    def middle_back(rows):
        rows, own, far = together(rows, back_own, back_far)
        mine = close_back(0, own, far)
        flying[0], flying[1] = mine, across(mine)
        return rows

    ffn(1, normed_two[1], middle_back)
    dh_own, dh_far = flying[0], flying[1]
    rows, dh_own, dh_far = together(ffn_back_rows(1), dh_own, dh_far)
    back_own, back_far = share(rows)
    back_own, normed_two[0], normed_two[1] = together(back_own, *normed_two)
    grads_in = sum(rows_contract(normed_two[m], gate_up[m]) for m in streams)
    grads_in, dh_far = together(grads_in.astype(bf16), dh_far)
    pair = jnp.concatenate([dh_own, dh_far], axis=0)
    grad_attn.append(jnp.concatenate([pair, beside(pair)], axis=0))
    grads_down = sum(rows_contract(cot_rows[m], hidden[m]) for m in streams).astype(bf16)
    grads_down, back_far = together(grads_down, back_far)
    ffn_back = RingScatter([grads_in, grads_down], "fsdp")
    ffn_back.hop()
    dh_own = close_back(1, back_own, back_far)
    dh_far = across(dh_own)
    hidden[0], hidden[1], dh_own = together(*hidden, dh_own)
    y_parts = list(ffn_back.before(*[cols_contract(hidden[m], full_down).astype(bf16) for m in streams]))
    ffn_back.hop()
    ffn_parts = [share(part) for part in y_parts]
    d_mixed = jnp.dot(grad_attn[0], full_out, preferred_element_type=f32).astype(bf16)
    y_own, y_far = [p[0] for p in ffn_parts], [p[1] for p in ffn_parts]
    d_mixed, y_own[0], y_own[1] = together(d_mixed, *y_own)
    d_proj = attention_bwd(proj, preps[0], saved[0], d_mixed, last[0], table[0], slot, heads, None)
    d_proj, dh_far, y_far[0], y_far[1] = ffn_back.before(d_proj, dh_far, *y_far)
    ffn_back.hop()
    pair = jnp.concatenate([dh_own, dh_far], axis=0)
    grad_attn.append(jnp.concatenate([pair, beside(pair)], axis=0))
    d_mixed = jnp.dot(grad_attn[1], full_out, preferred_element_type=f32).astype(bf16)
    y_rows = jnp.concatenate(
        [(hidden_in[m] + y_own[m] + y_far[m].astype(f32)).astype(bf16) for m in streams], axis=0
    )
    grad_out = sum(rows_contract(grad_attn[m], saved[m][0]) for m in streams).astype(bf16)
    d_mixed, grad_out, y_rows = together(d_mixed, grad_out, y_rows)
    y_across = across(y_rows)
    d_proj = attention_bwd(proj, preps[1], saved[1], d_mixed, last[1], table[1], slot, heads, d_proj)
    d_proj, y_across = ffn_back.before(d_proj, y_across)
    ffn_back.hop()
    attn_grads, d_proj, y_rows = together(rows_contract(normed, d_proj).astype(bf16), d_proj, y_rows)
    attn_back = RingScatter([attn_grads, grad_out], "fsdp")
    attn_back.hop()
    y_pair = jnp.concatenate([y_rows, y_across], axis=0)
    rows_one, y_other = attn_back.before(cols_contract(d_proj, w_in).astype(bf16), beside(y_pair))
    grad_one = lax.psum_scatter(rows_one, "tp", scatter_dimension=0, tiled=True).astype(f32)
    ffn_sum = ffn_back.finish()
    attn_back.hop()
    ffn_sum = attn_back.before(ffn_sum)
    attn_back.hop()
    out_y = pick_blocks([y_rows, y_across, y_other], own_spots)
    grad_one = attn_back.before(grad_one)
    attn_sum = attn_back.finish()
    unit_one, scale_one = unit_rows(tokens.astype(f32))
    norm_one_grad = norm_back(grad_one, unit_one, scale_one, gain_one)
    out_dx = (pick_blocks(grad_attn, own_places).astype(f32) + norm_one_grad).astype(bf16)
    dots = lambda grads, weights: jnp.sum(grads * weights.astype(f32), axis=1)
    own_one = dots(attn_sum[:, : 4 * width], attn_pack[:, : 4 * width]) + dots(
        attn_sum[:, 4 * width : 4 * width + heads], w_beta
    )
    own_two = dots(ffn_sum[:, : 2 * hidden_width], ffn_pack[:, : 2 * hidden_width])
    gains = tp_sum(jnp.stack([own_one, own_two])) / jnp.stack([gain_attn, gain_ffn]).astype(f32)
    return (
        out_y,
        out_dx,
        attn_sum[:, :width],
        attn_sum[:, width : 2 * width],
        attn_sum[:, 2 * width : 3 * width],
        attn_sum[:, 3 * width : 4 * width],
        attn_sum[:, 4 * width : 4 * width + heads],
        attn_sum[:, 4 * width + BLOCK :],
        ffn_sum[:, :hidden_width],
        ffn_sum[:, hidden_width : 2 * hidden_width],
        ffn_sum[:, 2 * hidden_width :],
        gains[0],
        gains[1],
    )


def solution(mesh):
    rows = P(("fsdp", "tp"), None)
    weight = P("fsdp", "tp")
    return jax.shard_map(
        local,
        mesh=mesh,
        in_specs=(rows, rows) + (weight,) * 9 + (P("fsdp"), P("fsdp"), P("fsdp", None, None), P("fsdp", None, None)),
        out_specs=(rows, rows) + (weight,) * 9 + (P("fsdp"), P("fsdp")),
        check_vma=False,
    )
```

```python
import functools

import jax
import jax.numpy as jnp
from jax import lax
from jax.experimental import pallas as pl
from jax.experimental.pallas import tpu as pltpu
from jax.sharding import PartitionSpec as P

BLOCK = 128
epsilon = 1e-06
bf16 = jnp.bfloat16
f32 = jnp.float32


def mm(a, b):
    return lax.dot_general(a, b, (((1,), (0,)), ((), ())), preferred_element_type=f32)


def mm_rt(a, b):
    return lax.dot_general(a, b, (((1,), (1,)), ((), ())), preferred_element_type=f32)


def mm_lt(a, b):
    return lax.dot_general(a, b, (((0,), (0,)), ((), ())), preferred_element_type=f32)


def iotas():
    rows = lax.broadcasted_iota(jnp.int32, (BLOCK, BLOCK), 0)
    cols = lax.broadcasted_iota(jnp.int32, (BLOCK, BLOCK), 1)
    return rows, cols


def lockstep(tasks):
    tasks = list(tasks)
    while tasks:
        tasks = [task for task in tasks if next(task, None) is not None]


def strengths(u, r_col):
    uf = u.astype(f32)
    inv_sq = 1.0 / (jnp.sum(uf * uf, axis=1, keepdims=True) + epsilon)
    beta = 2.0 / (1.0 + jnp.exp(-r_col))
    return beta, inv_sq


def prep_kernel(heads, chunks, table_ref, *refs):
    q_refs, k_refs, u_refs, r_refs = (refs[n * chunks : (n + 1) * chunks] for n in range(4))
    near_ref, q0_ref, kp_ref, inv_ref, t_ref = refs[4 * chunks :]
    rows, cols = iotas()
    strict = rows > cols
    lower = rows >= cols
    diff = rows ^ cols
    eye = jnp.where(rows == cols, 1.0, 0.0).astype(f32)
    eye_b = eye.astype(bf16)
    items = [(c, h) for c in range(chunks) for h in range(heads)]
    state = []
    for c, h in items:
        cs = pl.ds(h * BLOCK, BLOCK)
        q, k, u = q_refs[c][:, cs], k_refs[c][:, cs], u_refs[c][:, cs]
        beta, inv_sq = strengths(u, r_refs[c][:, h : h + 1].astype(f32))
        bp = beta * inv_sq
        big = mm_rt(jnp.concatenate([u, q], axis=0), jnp.concatenate([u, k], axis=0))
        gram = big[:BLOCK, :BLOCK]
        e_s = jnp.where(strict, big[:BLOCK, BLOCK:], 0.0)
        a_s = jnp.where(lower, big[BLOCK:, :BLOCK], 0.0)
        n0 = big[BLOCK:, BLOCK:]
        low = jnp.where(strict, gram * bp, 0.0)
        eu = jnp.concatenate([e_s * bp, u.astype(f32) * bp], axis=1).astype(bf16)
        state.append([q, k, u, a_s.astype(bf16), n0, low, eu, eye - jnp.where(diff < 2, low, 0.0)])
    size = 2
    while size < BLOCK:
        sel = (diff >= size) & (diff < 2 * size)
        prods = []
        for st in state:
            xb = st[7].astype(bf16)
            prods.append((xb, mm(jnp.where(sel, st[5], 0.0).astype(bf16), xb)))
        for st, (xb, y) in zip(state, prods):
            st[7] = st[7] - mm(xb, y.astype(bf16))
        size *= 2
    for (c, h), (q, k, u, a_b, n0, low, eu, x) in zip(items, state):
        rs, cs = pl.ds(c * BLOCK, BLOCK), pl.ds(h * BLOCK, BLOCK)
        xb = x.astype(bf16)
        t = mm(xb, eu).astype(bf16)
        top = mm(a_b, t)
        bot = mm_lt(u, t)
        inv_ref[c, h] = xb
        t_ref[c, h] = t
        near_ref[c, h] = n0 - top[:, :BLOCK]
        q0_ref[rs, cs] = (q.astype(f32) - top[:, BLOCK:]).astype(bf16)
        ket = mm_rt(eye_b, k) - bot[:, :BLOCK]
        kp_ref[c, h] = jnp.concatenate([ket, eye - bot[:, BLOCK:]], axis=1).astype(bf16)


def fwd_kernel(
    heads, depth, scale, first_ref, table_ref, slot_ref, q0_ref, near_ref, kp_ref, v_ref, o_ref, linv_ref, e_ref, cur_ref, s_ref, m_ref, acc_ref
):
    i = pl.program_id(0)
    first = first_ref[i]
    rows, cols = iotas()
    lower = rows >= cols
    neg = jnp.float32(-1e30)
    for h in range(heads):
        s0 = jnp.where(lower, near_ref[0, h], neg)
        s_ref[0, h] = s0
        m_ref[h] = s0
        cur_ref[0, 0, h] = q0_ref[:, h * BLOCK : (h + 1) * BLOCK]
    for d in range(1, depth):

        @pl.when(i - d >= first)
        def _():
            j = i - d
            for h in range(heads):
                both = mm(cur_ref[0, d - 1, h], kp_ref[j, h])
                s = both[:, :BLOCK]
                s_ref[d, h] = s
                m_ref[h] = jnp.maximum(m_ref[h], s)
                if d + 1 < depth:
                    cur_ref[0, d, h] = both[:, BLOCK:].astype(bf16)

    peaks = []
    for h in range(heads):
        peak = jnp.max(m_ref[h], axis=1, keepdims=True)
        peaks.append(peak)
        e0 = jnp.exp((s_ref[0, h] - peak) * scale)
        m_ref[h] = e0
        eb = e0.astype(bf16)
        e_ref[0, 0, h] = eb
        v = v_ref[pl.ds(pl.multiple_of(table_ref[i] * BLOCK, BLOCK), BLOCK), h * BLOCK : (h + 1) * BLOCK]
        acc_ref[h] = mm(eb, v)
    for d in range(1, depth):

        @pl.when(i - d >= first)
        def _():
            j = i - d
            for h in range(heads):
                e = jnp.exp((s_ref[d, h] - peaks[h]) * scale)
                m_ref[h] = m_ref[h] + e
                eb = e.astype(bf16)
                e_ref[0, d, h] = eb
                v = v_ref[pl.ds(pl.multiple_of(table_ref[j] * BLOCK, BLOCK), BLOCK), h * BLOCK : (h + 1) * BLOCK]
                acc_ref[h] = acc_ref[h] + mm(eb, v)

    for h in range(heads):
        linv = 1.0 / jnp.sum(m_ref[h], axis=1, keepdims=True)
        cs = slice(h * BLOCK, (h + 1) * BLOCK)
        o_ref[:, cs] = (acc_ref[h] * linv).astype(bf16)
        linv_ref[:, cs] = jnp.broadcast_to(linv, (BLOCK, BLOCK))


def bwd_kernel(heads, depth, scale, last_ref, table_ref, slot_ref, *refs):
    (do_ref, o_ref, linv_ref, q_ref, k_ref, v_ref, u_ref, r_ref, kp_ref, inv_ref, t_ref) = refs[:11]
    e_refs = refs[11 : 11 + depth]
    cur_refs = refs[11 + depth : 10 + 2 * depth]
    out_ref, dop_ref, del_ref, g_ref, dv_ref, acc_ref = refs[-6:]
    j = pl.program_id(0)
    last = last_ref[j]
    rows, cols = iotas()
    strict = rows > cols
    lower = rows >= cols
    upper = rows <= cols
    total = dop_ref.shape[0]

    @pl.when(j == 0)
    def _():
        for c in range(total // BLOCK):
            rs = pl.ds(c * BLOCK, BLOCK)
            for h in range(heads):
                cs = slice(h * BLOCK, (h + 1) * BLOCK)
                there = pl.ds(pl.multiple_of(slot_ref[c] * BLOCK, BLOCK), BLOCK)
                dop = do_ref[there, cs].astype(f32) * linv_ref[rs, cs]
                delta = jnp.sum(dop * o_ref[there, cs].astype(f32), axis=1, keepdims=True)
                dop_ref[rs, cs] = dop.astype(bf16)
                del_ref[rs, cs] = jnp.broadcast_to(delta, (BLOCK, BLOCK))
                g_ref[c, h] = jnp.zeros((BLOCK, BLOCK), bf16)

    here = pl.ds(pl.multiple_of(j * BLOCK, BLOCK), BLOCK)
    near = []
    for h in range(heads):
        cs = slice(h * BLOCK, (h + 1) * BLOCK)
        dop = dop_ref[here, cs]
        e = e_refs[0][0, 0, h]
        dp = mm_rt(dop, v_ref[:, cs])
        near.append((e.astype(f32) * (dp - del_ref[here, cs]) * scale).astype(bf16))
        dv_ref[h] = mm_lt(e, dop)
        acc_ref[h] = jnp.zeros((BLOCK, 2 * BLOCK), f32)
    for d in range(1, depth):

        @pl.when(j + d <= last)
        def _():
            i = j + d
            there = pl.ds(pl.multiple_of(i * BLOCK, BLOCK), BLOCK)
            def far(h):
                cs = slice(h * BLOCK, (h + 1) * BLOCK)
                dop = dop_ref[there, cs]
                e = e_refs[d][0, 0, h]
                dp = mm_rt(dop, v_ref[:, cs])
                yield 1
                dv_ref[h] = dv_ref[h] + mm_lt(e, dop)
                yield 1
                ds = (e.astype(f32) * (dp - del_ref[there, cs]) * scale).astype(bf16)
                dsg = jnp.concatenate([ds, g_ref[i, h]], axis=1)
                yield 1
                acc_ref[h] = acc_ref[h] + mm_lt(cur_refs[d - 1][0, 0, h], dsg)
                yield 1
                g_ref[i, h] = mm_rt(dsg, kp_ref[0, h]).astype(bf16)

            lockstep(far(h) for h in range(heads))

    lane = cols
    dr_all = jnp.zeros((BLOCK, BLOCK), f32)
    width = heads * BLOCK
    drs = {}

    def local_part(h):
        cs = slice(h * BLOCK, (h + 1) * BLOCK)
        q, k, u = q_ref[:, cs], k_ref[:, cs], u_ref[:, cs]
        kq = mm_rt(u, jnp.concatenate([k, q], axis=0))
        yield 1
        e_s = jnp.where(strict, kq[:, :BLOCK], 0.0).astype(bf16)
        a_t = jnp.where(upper, kq[:, BLOCK:], 0.0).astype(bf16)
        dn = near[h]
        acc = acc_ref[h]
        bmat = jnp.concatenate([jnp.concatenate([dn, g_ref[j, h]], axis=1), acc.astype(bf16)], axis=0)
        yz = mm(jnp.concatenate([a_t, u], axis=1), bmat).astype(bf16)
        yield 1
        ru = mm_rt(jnp.concatenate([e_s, u], axis=1), bmat)
        beta, inv_sq = strengths(u, r_ref[:, h : h + 1].astype(f32))
        bp = beta * inv_sq
        yield 1
        inv = inv_ref[0, h]
        left = mm_lt(inv, yz) * (-bp)
        yield 1
        right = -mm(inv, (ru * bp).astype(bf16))
        yield 1
        d_s = jnp.where(strict, -mm_rt(left.astype(bf16), t_ref[0, h]), 0.0).astype(bf16)
        d_e = jnp.where(strict, left[:, :BLOCK], 0.0).astype(bf16)
        d_at = jnp.where(upper, right[:, :BLOCK], 0.0).astype(bf16)
        du = left[:, BLOCK:] + right[:, BLOCK:]
        yield 1
        d_a = d_at.astype(f32).T.astype(bf16)
        uk = jnp.concatenate([u, k], axis=0)
        dq_o = g_ref[j, h].astype(f32) + mm(jnp.concatenate([d_a, dn], axis=1), uk)
        out_ref[:, cs] = dq_o.astype(bf16)
        yield 1
        uq = jnp.concatenate([u, q], axis=0)
        dk_o = acc_ref[h][:, :BLOCK].T + mm_lt(jnp.concatenate([d_e, dn], axis=0), uq)
        out_ref[:, width + h * BLOCK : width + (h + 1) * BLOCK] = dk_o.astype(bf16)
        yield 1
        du = du + mm(jnp.concatenate([d_s, d_e], axis=1), uk)
        d_st = d_s.astype(f32).T.astype(bf16)
        du = du + mm(jnp.concatenate([d_st, d_at], axis=1), uq)
        yield 1
        uf = u.astype(f32)
        rad = jnp.sum(uf * du, axis=1, keepdims=True)
        du = du - (inv_sq * rad) * uf
        drs[h] = 0.5 * rad * (1.0 - 0.5 * beta)
        out_ref[:, 2 * width + h * BLOCK : 2 * width + (h + 1) * BLOCK] = dv_ref[h].astype(bf16)
        out_ref[:, 3 * width + h * BLOCK : 3 * width + (h + 1) * BLOCK] = du.astype(bf16)

    lockstep(local_part(h) for h in range(heads))
    for h in range(heads):
        dr_all = jnp.where(lane == h, drs[h], dr_all)
    out_ref[:, 4 * width :] = dr_all.astype(bf16)


def attention_prep(proj, table, heads):
    count = table.shape[0]
    width = heads * BLOCK
    step = 2

    def rows(c, n, col):
        return pl.BlockSpec((BLOCK, n), lambda i, t: (t[i * step + c], col))

    tile = lambda n: pl.BlockSpec((step, heads, BLOCK, n), lambda i, t: (i, 0, 0, 0))
    shape = lambda n, t: jax.ShapeDtypeStruct((count, heads, BLOCK, n), t)
    spec = pltpu.PrefetchScalarGridSpec(
        num_scalar_prefetch=1,
        grid=(count // step,),
        in_specs=[rows(c, width, col) for col in (0, 1, 3) for c in range(step)]
        + [rows(c, BLOCK, 4 * heads) for c in range(step)],
        out_specs=[
            tile(BLOCK),
            pl.BlockSpec((step * BLOCK, width), lambda i, t: (i, 0)),
            tile(2 * BLOCK),
            tile(BLOCK),
            tile(2 * BLOCK),
        ],
    )
    return pl.pallas_call(
        functools.partial(prep_kernel, heads, step),
        grid_spec=spec,
        out_shape=[
            shape(BLOCK, f32),
            jax.ShapeDtypeStruct((count * BLOCK, width), bf16),
            shape(2 * BLOCK, bf16),
            shape(BLOCK, bf16),
            shape(2 * BLOCK, bf16),
        ],
        cost_estimate=pl.CostEstimate(
            flops=count * heads * 45 * BLOCK**3, bytes_accessed=6 * count * BLOCK * width, transcendentals=0
        ),
        name="attn_prep",
    )(table, *([proj] * (4 * step)))


def attention_fwd(proj, prep, first, table, slot, heads):
    near, q0, kp, _, _ = prep
    count = table.shape[0]
    depth = count
    width = heads * BLOCK
    scale = float(BLOCK) ** -0.5
    spec = pltpu.PrefetchScalarGridSpec(
        num_scalar_prefetch=3,
        grid=(count,),
        in_specs=[
            pl.BlockSpec((BLOCK, width), lambda i, f, t, w: (i, 0)),
            pl.BlockSpec((1, heads, BLOCK, BLOCK), lambda i, f, t, w: (i, 0, 0, 0)),
            pl.BlockSpec((count, heads, BLOCK, 2 * BLOCK), lambda i, f, t, w: (0, 0, 0, 0)),
            pl.BlockSpec((proj.shape[0], width), lambda i, f, t, w: (0, 2)),
        ],
        out_specs=[
            pl.BlockSpec((BLOCK, width), lambda i, f, t, w: (w[i], 0)),
            pl.BlockSpec((BLOCK, width), lambda i, f, t, w: (i, 0)),
            pl.BlockSpec((1, depth, heads, BLOCK, BLOCK), lambda i, f, t, w: (i, 0, 0, 0, 0)),
            pl.BlockSpec((1, depth - 1, heads, BLOCK, BLOCK), lambda i, f, t, w: (i, 0, 0, 0, 0)),
        ],
        scratch_shapes=[
            pltpu.VMEM((depth, heads, BLOCK, BLOCK), f32),
            pltpu.VMEM((heads, BLOCK, BLOCK), f32),
            pltpu.VMEM((heads, BLOCK, BLOCK), f32),
        ],
    )
    return pl.pallas_call(
        functools.partial(fwd_kernel, heads, depth, scale),
        grid_spec=spec,
        out_shape=[
            jax.ShapeDtypeStruct((count * BLOCK, width), bf16),
            jax.ShapeDtypeStruct((count * BLOCK, width), f32),
            jax.ShapeDtypeStruct((count, depth, heads, BLOCK, BLOCK), bf16),
            jax.ShapeDtypeStruct((count, depth - 1, heads, BLOCK, BLOCK), bf16),
        ],
        cost_estimate=pl.CostEstimate(
            flops=count * heads * 48 * BLOCK**3, bytes_accessed=6 * count * BLOCK * width, transcendentals=0
        ),
        name="attn_fwd",
    )(first, table, slot, q0, near, kp, proj)


def attention_bwd(proj, prep, saved, d_mixed, last, table, slot, heads, filled):
    _, _, kp, inv, t_all = prep
    mixed, linv, e_all, cur_all = saved
    count = table.shape[0]
    depth = count
    total = count * BLOCK
    width = heads * BLOCK
    scale = float(BLOCK) ** -0.5
    full = lambda: pl.BlockSpec((total, width), lambda j, f, t, w: (0, 0))
    wide = lambda col: pl.BlockSpec((BLOCK, width), lambda j, f, t, w: (t[j], col))
    tile = lambda n: pl.BlockSpec((1, heads, BLOCK, n), lambda j, f, t, w: (j, 0, 0, 0))

    def diagonal(d, slot):
        return pl.BlockSpec(
            (1, 1, heads, BLOCK, BLOCK), lambda j, f, t, w: (jnp.minimum(j + d, count - 1), slot, 0, 0, 0)
        )

    in_specs = [
        full(),
        full(),
        full(),
        wide(0),
        wide(1),
        wide(2),
        wide(3),
        pl.BlockSpec((BLOCK, BLOCK), lambda j, f, t, w: (t[j], 4 * heads)),
        tile(2 * BLOCK),
        tile(BLOCK),
        tile(2 * BLOCK),
    ]
    in_specs += [diagonal(d, d) for d in range(depth)] + [diagonal(d, d - 1) for d in range(1, depth)]
    operands = [last, table, slot, d_mixed, mixed, linv, proj, proj, proj, proj, proj, kp, inv, t_all]
    operands += [e_all] * depth + [cur_all] * (depth - 1)
    aliases = {}
    if filled is not None:
        aliases = {len(operands): 0}
        in_specs.append(pl.BlockSpec(memory_space=pl.ANY))
        operands.append(filled)
    spec = pltpu.PrefetchScalarGridSpec(
        num_scalar_prefetch=3,
        grid=(count,),
        in_specs=in_specs,
        out_specs=pl.BlockSpec((BLOCK, 4 * width + BLOCK), lambda j, f, t, w: (t[j], 0)),
        scratch_shapes=[
            pltpu.VMEM((total, width), bf16),
            pltpu.VMEM((total, width), f32),
            pltpu.VMEM((count, heads, BLOCK, BLOCK), bf16),
            pltpu.VMEM((heads, BLOCK, BLOCK), f32),
            pltpu.VMEM((heads, BLOCK, 2 * BLOCK), f32),
        ],
    )
    return pl.pallas_call(
        functools.partial(bwd_kernel, heads, depth, scale),
        grid_spec=spec,
        out_shape=jax.ShapeDtypeStruct((proj.shape[0], 4 * width + BLOCK), bf16),
        input_output_aliases=aliases,
        cost_estimate=pl.CostEstimate(
            flops=count * heads * 120 * BLOCK**3, bytes_accessed=8 * total * width, transcendentals=0
        ),
        name="attn_bwd",
    )(*operands)


def gather_kernel(group, table_ref, *refs):
    outs = refs[-(len(refs) // (group + 1)) :]
    for m, dst in enumerate(outs):
        for c in range(group):
            dst[c * BLOCK : (c + 1) * BLOCK, :] = refs[m * group + c][...]


def gather_blocks(x, tables, group):
    streams, count = tables.shape
    cols = x.shape[1]

    def source(m, c):
        return pl.BlockSpec((BLOCK, cols), lambda i, t: (t[m * count + i * group + c], 0))

    spec = pltpu.PrefetchScalarGridSpec(
        num_scalar_prefetch=1,
        grid=(count // group,),
        in_specs=[source(m, c) for m in range(streams) for c in range(group)],
        out_specs=[pl.BlockSpec((group * BLOCK, cols), lambda i, t: (i, 0))] * streams,
    )
    return pl.pallas_call(
        functools.partial(gather_kernel, group),
        grid_spec=spec,
        out_shape=[jax.ShapeDtypeStruct((count * BLOCK, cols), x.dtype)] * streams,
        cost_estimate=pl.CostEstimate(flops=0, bytes_accessed=4 * streams * count * BLOCK * cols, transcendentals=0),
        name="gather_blocks",
    )(tables.reshape(-1), *([x] * (group * streams)))


def pick_kernel(bounds, picks, table_ref, *refs):
    total = sum(len(part) for part in bounds)
    parts, outs = refs[:total], refs[total:-3]
    held, load_sem, store_sem = refs[-3:]
    stores = []
    base = 0
    for group, limits in enumerate(bounds):
        for n in range(picks):
            slot = group * picks + n
            at = table_ref[slot]
            for p, (low, high) in enumerate(limits):

                @pl.when((at >= low) & (at < high))
                def _():
                    rows = pl.ds(pl.multiple_of((at - low) * BLOCK, BLOCK), BLOCK)
                    pltpu.make_async_copy(parts[base + p].at[rows, :], held.at[slot], load_sem.at[slot]).start()

        base += len(limits)
    for group in range(len(bounds)):
        for n in range(picks):
            slot = group * picks + n
            rows = pl.ds(n * BLOCK, BLOCK)
            pltpu.make_async_copy(outs[group].at[rows, :], held.at[slot], load_sem.at[slot]).wait()
            stores.append(pltpu.make_async_copy(held.at[slot], outs[group].at[rows, :], store_sem.at[slot]))
            stores[-1].start()
    for store in stores:
        store.wait()


def pick_blocks(groups, tables):
    picks = tables[0].shape[0]
    cols = groups[0][0].shape[1]
    dtype = groups[0][0].dtype
    bounds = []
    for parts in groups:
        limits, low = [], 0
        for part in parts:
            limits.append((low, low + part.shape[0] // BLOCK))
            low = limits[-1][1]
        bounds.append(limits)
    flat = [part for parts in groups for part in parts]
    slots = picks * len(groups)
    spec = pltpu.PrefetchScalarGridSpec(
        num_scalar_prefetch=1,
        grid=(1,),
        in_specs=[pl.BlockSpec(memory_space=pl.ANY)] * len(flat),
        out_specs=[pl.BlockSpec(memory_space=pl.ANY)] * len(groups),
        scratch_shapes=[
            pltpu.VMEM((slots, BLOCK, cols), dtype),
            pltpu.SemaphoreType.DMA((slots,)),
            pltpu.SemaphoreType.DMA((slots,)),
        ],
    )
    return pl.pallas_call(
        functools.partial(pick_kernel, bounds, picks),
        grid_spec=spec,
        out_shape=[jax.ShapeDtypeStruct((picks * BLOCK, cols), dtype)] * len(groups),
        cost_estimate=pl.CostEstimate(flops=0, bytes_accessed=4 * slots * BLOCK * cols, transcendentals=0),
        name="pick_blocks",
    )(jnp.concatenate(tables).astype(jnp.int32), *flat)


def place_kernel(count, rows, spot_ref, *refs):
    pieces, out, bufs, sem_in, sem_out = refs[:count], refs[count], refs[count + 1], refs[count + 2], refs[count + 3]
    loads = [pltpu.make_async_copy(pieces[n], bufs.at[n], sem_in.at[n]) for n in range(count)]
    for load in loads:
        load.start()
    stores = []
    for n in range(count):
        loads[n].wait()
        to = out.at[pl.ds(pl.multiple_of(spot_ref[n] * rows, rows), rows), :]
        stores.append(pltpu.make_async_copy(bufs.at[n], to, sem_out.at[n]))
        stores[n].start()
    for store in stores:
        store.wait()


def place_pieces(pieces, spots, count):
    rows, cols = pieces[0].shape
    held = len(pieces)
    dtype = pieces[0].dtype
    spec = pltpu.PrefetchScalarGridSpec(
        num_scalar_prefetch=1,
        grid=(1,),
        in_specs=[pl.BlockSpec(memory_space=pl.ANY)] * held,
        out_specs=pl.BlockSpec(memory_space=pl.ANY),
        scratch_shapes=[
            pltpu.VMEM((held, rows, cols), dtype),
            pltpu.SemaphoreType.DMA((held,)),
            pltpu.SemaphoreType.DMA((held,)),
        ],
    )
    where = jnp.concatenate([jnp.reshape(spot, (1,)) for spot in spots]).astype(jnp.int32)
    return pl.pallas_call(
        functools.partial(place_kernel, held, rows),
        grid_spec=spec,
        out_shape=jax.ShapeDtypeStruct((count * rows, cols), dtype),
        cost_estimate=pl.CostEstimate(flops=0, bytes_accessed=4 * held * rows * cols, transcendentals=0),
        name="place_pieces",
    )(where, *pieces)


def open_kernel(spot_ref, x_ref, out_ref):
    out_ref[...] = x_ref[...]


def open_buffer(x, spot, count):
    rows, cols = x.shape
    spec = pltpu.PrefetchScalarGridSpec(
        num_scalar_prefetch=1,
        grid=(2,),
        in_specs=[pl.BlockSpec((rows // 2, cols), lambda i, t: (i, 0))],
        out_specs=pl.BlockSpec((rows // 2, cols), lambda i, t: (2 * t[0] + i, 0)),
    )
    return pl.pallas_call(
        open_kernel,
        grid_spec=spec,
        out_shape=jax.ShapeDtypeStruct((count * rows, cols), x.dtype),
        cost_estimate=pl.CostEstimate(flops=0, bytes_accessed=4 * rows * cols, transcendentals=0),
        name="open_buffer",
    )(jnp.reshape(spot, (1,)).astype(jnp.int32), x)


def rows_contract(a, b):
    return lax.dot_general(a, b, (((0,), (0,)), ((), ())), preferred_element_type=f32)


def cols_contract(a, b):
    return lax.dot_general(a, b, (((1,), (1,)), ((), ())), preferred_element_type=f32)


def unit_rows(x):
    scale = lax.rsqrt(jnp.mean(x * x, axis=1, keepdims=True) + epsilon)
    return x * scale, scale


def norm_back(grad_normed, unit, scale, gain):
    grad_unit = grad_normed * gain
    return scale * (grad_unit - unit * jnp.mean(grad_unit * unit, axis=1, keepdims=True))


def ring_order(count):
    return list(range(0, count, 2)) + list(range(1, count, 2))[::-1]


def ring_tables(axis):
    count = lax.axis_size(axis)
    order = ring_order(count)
    right = [(order[p], order[(p + 1) % count]) for p in range(count)]
    left = [(order[p], order[(p - 1) % count]) for p in range(count)]
    me = lax.axis_index(axis)
    spot = jnp.where(me % 2 == 0, me // 2, count - 1 - me // 2)

    def owner(shift):
        at = (spot + shift + count) % count
        return jnp.where(at < count // 2, 2 * at, 2 * (count - 1 - at) + 1)

    return count, right, left, owner


class RingGather:
    def __init__(self, x, axis, whole=False):
        self.axis, self.x, self.whole = axis, x, whole
        self.count, self.right, self.left, self.owner = ring_tables(axis)
        self.moving = (x, x)
        self.hops = []

    def hop(self):
        from_left, from_right = self.moving
        if len(self.hops) == self.count // 2 - 1:
            half = self.x.shape[0] // 2
            from_left, from_right = from_left[:half], from_right[half:]
        self.moving = (
            lax.ppermute(from_left, self.axis, self.right),
            lax.ppermute(from_right, self.axis, self.left),
        )
        self.hops.append(self.moving)

    def before(self, *values):
        held = lax.optimization_barrier((self.moving,) + values)
        self.moving = held[0]
        self.hops[-1] = self.moving
        return held[1] if len(values) == 1 else held[1:]

    def finish(self):
        while len(self.hops) < self.count // 2:
            self.hop()
        rows = self.x.shape[0]
        put = lax.dynamic_update_slice_in_dim
        pieces, spots = [self.x], [self.owner(0)]
        for s, (from_left, from_right) in enumerate(self.hops[:-1], 1):
            pieces += [from_left, from_right]
            spots += [self.owner(-s), self.owner(s)]
        if self.whole:
            out = place_pieces(pieces, spots, self.count)
        else:
            out = open_buffer(self.x, spots[0], self.count)
            for piece, spot in zip(pieces[1:], spots[1:]):
                out = put(out, piece, spot * rows, 0)
        far = self.owner(self.count // 2) * rows
        out = put(out, self.hops[-1][0], far, 0)
        return put(out, self.hops[-1][1], far + rows // 2, 0)


class RingScatter:
    def __init__(self, parts, axis):
        self.axis, self.parts = axis, parts
        self.count, self.right, self.left, self.owner = ring_tables(axis)
        self.rows = parts[0].shape[0] // self.count
        self.top = self.count // 2
        self.done = 0
        half = self.rows // 2
        self.moving = (self.piece(self.top, 0, half), self.piece(-self.top, half, half))

    def piece(self, shift, start=0, size=None):
        size = self.rows if size is None else size
        at = self.owner(shift) * self.rows + start
        return jnp.concatenate([lax.dynamic_slice_in_dim(part, at, size, 0) for part in self.parts], axis=1)

    def hop(self):
        to_right, to_left = self.moving
        if self.done > 0:
            s = self.top - self.done
            a, b = self.piece(s), self.piece(-s)
            if self.done == 1:
                half = self.rows // 2
                to_right = jnp.concatenate([a[:half] + to_right, a[half:]], axis=0)
                to_left = jnp.concatenate([b[:half], b[half:] + to_left], axis=0)
            else:
                to_right, to_left = a + to_right, b + to_left
        self.moving = (lax.ppermute(to_right, self.axis, self.right), lax.ppermute(to_left, self.axis, self.left))
        self.done += 1

    def before(self, *values):
        held = lax.optimization_barrier((self.moving,) + values)
        self.moving = held[0]
        return held[1] if len(values) == 1 else held[1:]

    def finish(self):
        while self.done < self.top:
            self.hop()
        return self.piece(0).astype(f32) + self.moving[0].astype(f32) + self.moving[1].astype(f32)


def ring_kernel(axis, count, rows, widths, *refs):
    held = len(widths)
    parts, outs = refs[:held], refs[held : 2 * held]
    own_buf, send_buf, recv_buf, load_sem, send_sem, recv_sem = refs[2 * held :]
    me = lax.axis_index(axis)
    odd = me % 2
    spot = (1 - odd) * (me // 2) + odd * (count - 1 - me // 2)

    def owner(shift):
        at = (spot + shift + count) % count
        upper = at // (count // 2)
        return (1 - upper) * (2 * at) + upper * (2 * (count - 1 - at) + 1)

    top = count // 2
    cut = rows // 32 * 16
    ways = ((1, owner(1)), (-1, owner(-1)))
    barrier = pltpu.get_barrier_semaphore()
    for _, peer in ways:
        pl.semaphore_signal(barrier, inc=1, device_id={axis: peer}, device_id_type=pl.DeviceIdType.MESH)

    def load(shift, slot):
        copies = []
        at = pl.multiple_of(owner(shift) * rows, rows)
        col = 0
        for n, width in enumerate(widths):
            copies.append(
                pltpu.make_async_copy(
                    parts[n].at[pl.ds(at, rows), :],
                    own_buf.at[slot, :, pl.ds(col, width)],
                    load_sem.at[slot, n],
                )
            )
            col += width
        for copy in copies:
            copy.start()
        return copies

    slots = {top: 0, 0: 2 * top - 1}
    for s in range(1, top):
        slots[s], slots[-s] = 2 * s - 1, 2 * s
    loads = {}
    for shift in [top] + [t * s for s in range(top - 1, 0, -1) for t in (1, -1)] + [0]:
        loads[shift] = load(shift, slots[shift])
    for copy in loads[top]:
        copy.wait()
    pl.semaphore_wait(barrier, 2)
    halves = ((0, cut), (cut, rows - cut))
    sent = []

    def push(way, hop, part, src):
        start, size = halves[part]
        copy = pltpu.make_async_remote_copy(
            src_ref=src,
            dst_ref=recv_buf.at[way, hop, pl.ds(start, size), :],
            send_sem=send_sem.at[way, hop, part],
            recv_sem=recv_sem.at[way, hop, part],
            device_id={axis: ways[way][1]},
            device_id_type=pl.DeviceIdType.MESH,
        )
        copy.start()
        sent.append(copy)
        return copy

    flying = {}
    for way in range(2):
        start, size = halves[way]
        flying[way, way] = push(way, 0, way, own_buf.at[slots[top], pl.ds(start, size), :])
    for hop in range(1, top):
        shift = top - hop
        order = [(way, 1 - way) for way in range(2)] + [(way, way) for way in range(2)]
        for way, part in order:
            sign = ways[way][0]
            start, size = halves[part]
            slot = slots[sign * shift]
            if part == 1 - way:
                for copy in loads[sign * shift]:
                    copy.wait()
            area = pl.ds(start, size)
            if hop == 1 and part == 1 - way:
                flying[way, part] = push(way, hop, part, own_buf.at[slot, area, :])
                continue
            flying[way, part].wait_recv()
            total = own_buf[slot, area, :].astype(f32) + recv_buf[way, hop - 1, area, :].astype(f32)
            send_buf[way, hop - 1, area, :] = total.astype(bf16)
            flying[way, part] = push(way, hop, part, send_buf.at[way, hop - 1, area, :])
    for copy in loads[0]:
        copy.wait()
    for part in range(2):
        start, size = halves[part]
        area = pl.ds(start, size)
        for way in range(2):
            flying[way, part].wait_recv()
        col = 0
        for n, width in enumerate(widths):
            cols = pl.ds(col, width)
            outs[n][area, :] = (
                own_buf[slots[0], area, cols].astype(f32)
                + recv_buf[0, top - 1, area, cols].astype(f32)
                + recv_buf[1, top - 1, area, cols].astype(f32)
            )
            col += width
    for copy in sent:
        copy.wait_send()


def ring_sum(parts, axis):
    count = lax.axis_size(axis)
    rows = parts[0].shape[0] // count
    widths = [part.shape[1] for part in parts]
    cols = sum(widths)
    top = count // 2
    sent = (2 * top - 1) * rows * cols * 2
    return pl.pallas_call(
        functools.partial(ring_kernel, axis, count, rows, widths),
        in_specs=[pl.BlockSpec(memory_space=pl.ANY)] * len(parts),
        out_specs=[pl.BlockSpec(memory_space=pltpu.VMEM)] * len(parts),
        out_shape=[jax.ShapeDtypeStruct((rows, width), f32) for width in widths],
        scratch_shapes=[
            pltpu.VMEM((count, rows, cols), bf16),
            pltpu.VMEM((2, top - 1, rows, cols), bf16),
            pltpu.VMEM((2, top, rows, cols), bf16),
            pltpu.SemaphoreType.DMA((count, len(parts))),
            pltpu.SemaphoreType.DMA((2, top, 2)),
            pltpu.SemaphoreType.DMA((2, top, 2)),
        ],
        compiler_params=pltpu.CompilerParams(collective_id=0, has_side_effects=True),
        cost_estimate=pl.CostEstimate(flops=0, bytes_accessed=4 * count * rows * cols, transcendentals=0),
        name="ring_sum",
    )(*parts)


def tp_sum(x):
    count = lax.axis_size("tp")
    me = lax.axis_index("tp")
    pieces = [x] + [lax.ppermute(x, "tp", [(i, (i + s) % count) for i in range(count)]) for s in range(1, count)]
    stacked = jnp.stack(pieces)
    slots = (me - jnp.arange(count, dtype=jnp.int32)) % count
    total = jnp.zeros_like(x)
    for r in range(count):
        total = total + jnp.sum(jnp.where((slots == r)[:, None, None], stacked, 0.0), axis=0)
    return total


SLOTS = (0, 2, 1, 3)


def across(x):
    return lax.ppermute(x, "tp", [(i, i ^ 2) for i in range(4)])


def beside(x):
    return lax.ppermute(x, "tp", [(i, i ^ 1) for i in range(4)])


def share(rows):
    size = rows.shape[0] // 4
    other = beside(rows[2 * size :])
    pair = rows[: 2 * size].astype(f32) + other.astype(f32)
    return pair[:size], across(pair[size:].astype(bf16))


def spread(x):
    pair = jnp.concatenate([x, across(x)], axis=0)
    return jnp.concatenate([pair, beside(pair)], axis=0)


def together(*values):
    return lax.optimization_barrier(values)


def local(
    tokens,
    cotangent,
    w_query,
    w_key,
    w_value,
    w_house,
    w_beta,
    w_out,
    w_gate,
    w_up,
    w_down,
    gain_attn,
    gain_ffn,
    pack_index,
    seq_start,
):
    packing, begins = pack_index[0], seq_start[0]
    bins, bin_rows = packing.shape
    per_bin = bin_rows // BLOCK
    streams = range(bins)
    width = w_query.shape[1]
    heads = w_beta.shape[1]
    hidden_width = w_gate.shape[1]
    shard = w_query.shape[0]
    ranks = 4
    assert lax.axis_size("tp") == ranks
    half = bin_rows // ranks
    per_half = half // BLOCK
    me = lax.axis_index("tp")

    given = packing[:, ::BLOCK] // BLOCK
    per_own = bins * per_half
    table = given
    first = begins[:, ::BLOCK] // BLOCK
    spots = jnp.arange(per_bin, dtype=jnp.int32)
    last = jnp.max(jnp.where(first[:, :, None] == first[:, None, :], spots[None, None, :], 0), axis=2)
    away = me ^ (spots // per_half)
    slot = ((away // 2) + 2 * (away % 2)) * per_half + spots % per_half
    places = jnp.arange(bins, dtype=jnp.int32)[:, None] * per_bin + slot[None, :]
    blocks = jnp.arange(bins * per_bin, dtype=jnp.int32)
    inverse = jnp.sum(jnp.where(given.reshape(-1)[:, None] == blocks[None, :], places.reshape(-1)[:, None], 0), axis=0)
    slotted = jnp.sum(jnp.where(slot[None, :, None] == spots[None, None, :], given[:, :, None], 0), axis=1)
    packed = jnp.sum(jnp.where(given.reshape(-1)[:, None] == blocks[None, :], blocks[:, None], 0), axis=0)
    mine = (blocks // per_own == me) & (blocks >= 0)
    pull = jnp.arange(per_own, dtype=jnp.int32)[:, None] == jnp.where(mine, blocks % per_own, -1)[None, :]
    own_places = jnp.sum(jnp.where(pull, inverse[None, :], 0), axis=1)
    own_packed = jnp.sum(jnp.where(pull, packed[None, :], 0), axis=1)
    origin = me ^ (own_packed % per_bin // per_half)
    own_spots = ((origin // 2) + 2 * (origin % 2)) * per_own + own_packed // per_bin * per_half + own_packed % per_half
    tables = (table.astype(jnp.int32), first, last, slot, slotted, own_places, own_spots)

    extras = jnp.concatenate(
        [w_beta, gain_attn[:, None], gain_ffn[:, None], jnp.zeros((shard, BLOCK - heads - 2), bf16)], axis=1
    )
    attn_pack = jnp.concatenate([w_query, w_key, w_value, w_house, extras], axis=1)
    ffn_pack = jnp.concatenate([w_gate, w_up], axis=1)
    full_tokens = lax.all_gather(tokens, "tp", axis=0, tiled=True)
    attn_ring = RingGather(attn_pack, "fsdp")
    attn_ring.hop()
    table, first, last, slot, slotted, own_places, own_spots = attn_ring.before(*tables)
    while len(attn_ring.hops) < attn_ring.count // 2 - 1:
        attn_ring.hop()
    full_tokens, out_shard, down_shard, cotangent = attn_ring.before(full_tokens, w_out, w_down, cotangent)
    w_in, ffn_pack, out_shard, down_shard, cotangent = together(
        attn_ring.finish(), ffn_pack, out_shard, down_shard, cotangent
    )
    ffn_ring = RingGather(ffn_pack, "fsdp", True)
    ffn_ring.hop()
    x_rows = gather_blocks(full_tokens, slotted[:, :per_half], per_half)
    full_out = lax.all_gather(out_shard, "fsdp", axis=0, tiled=True)
    full_down = lax.all_gather(down_shard, "fsdp", axis=0, tiled=True)
    full_cot = lax.all_gather(cotangent, "tp", axis=0, tiled=True)
    pick = (jnp.arange(BLOCK)[None, :] == heads + jnp.arange(8)[:, None]).astype(bf16)
    gain_rows = cols_contract(pick, w_in[:, 4 * width :])
    gain_one, gain_two = gain_rows[0], gain_rows[1]

    all_unit, _ = unit_rows(full_tokens.astype(f32))
    normed = (all_unit * gain_one).astype(bf16)
    proj = jnp.dot(normed, w_in, preferred_element_type=f32).astype(bf16)

    def attend(m):
        prep = attention_prep(proj, table[m], heads)
        return prep, lambda prep: attention_fwd(proj, prep, first[m], table[m], slot, heads)

    preps, saved, hidden_in, unit_two, scale_two, normed_two = [], [], [], [], [], []

    def close(m, own, far):
        hidden_in.append(x_rows[m].astype(f32) + own + far.astype(f32))
        unit, scale = unit_rows(hidden_in[m])
        unit_two.append(unit)
        scale_two.append(scale)
        return (unit * gain_two).astype(bf16)

    prep, run = attend(0)
    prep = list(prep)
    prep[0] = ffn_ring.before(prep[0])
    ffn_ring.hop()
    preps.append(prep)
    saved.append(list(run(prep)))
    rows = ffn_ring.before(cols_contract(saved[0][0], full_out).astype(bf16))
    ffn_ring.hop()
    attn_own, attn_far = share(rows)
    proj, attn_own = together(proj, attn_own)
    prep, run = attend(1)
    prep = list(prep)
    prep[0], attn_far = ffn_ring.before(prep[0], attn_far)
    while len(ffn_ring.hops) < ffn_ring.count // 2:
        ffn_ring.hop()
    preps.append(prep)
    normed_own = close(0, attn_own, attn_far)
    normed_far = across(normed_own)
    prep[0], normed_own = together(prep[0], normed_own)
    saved.append(list(run(prep)))
    saved[1][0], normed_far, full_cot = together(saved[1][0], normed_far, full_cot)
    pair = jnp.concatenate([normed_own, normed_far], axis=0)
    normed_two.append(jnp.concatenate([pair, beside(pair)], axis=0))
    attn_own, attn_far = share(cols_contract(saved[1][0], full_out).astype(bf16))
    attn_own, full_cot, ffn_ring.x = together(attn_own, full_cot, ffn_ring.x)
    ffn_full = ffn_ring.finish()
    cot_rows = list(gather_blocks(full_cot, slotted, 4))

    full_gate, full_up = ffn_full[:, :hidden_width], ffn_full[:, hidden_width : 2 * hidden_width]
    full_gate_up = ffn_full
    hidden, gate_up, back = [], [], []

    def ffn(m, rows, middle):
        gate_pre = jnp.dot(rows, full_gate, preferred_element_type=f32)
        up_part = jnp.dot(rows, full_up, preferred_element_type=f32)
        cot_rows[m] = middle(cot_rows[m])
        hidden.append((jax.nn.silu(gate_pre) * up_part).astype(bf16))
        grad_hidden = jnp.dot(cot_rows[m], full_down, preferred_element_type=f32)
        sigma = jax.nn.sigmoid(gate_pre)
        grad_gate = (grad_hidden * up_part * sigma * (1.0 + gate_pre * (1.0 - sigma))).astype(bf16)
        grad_up = (grad_hidden * jax.nn.silu(gate_pre)).astype(bf16)
        gate_up.append(jnp.concatenate([grad_gate, grad_up], axis=1))

    def ffn_back_rows(m):
        return cols_contract(gate_up[m], full_gate_up).astype(bf16)

    flying = {}

    def middle(rows):
        rows, own, far = together(rows, attn_own, attn_far)
        mine = close(1, own, far)
        flying[0], flying[1] = mine, across(mine)
        return rows

    ffn(0, normed_two[0], middle)
    normed_own, normed_far = flying[0], flying[1]
    rows, normed_own, normed_far = together(ffn_back_rows(0), normed_own, normed_far)
    back_own, back_far = share(rows)
    pair = jnp.concatenate([normed_own, normed_far], axis=0)
    normed_two.append(jnp.concatenate([pair, beside(pair)], axis=0))
    grad_attn = []

    def close_back(m, own, far):
        norm_two_grad = norm_back(own + far.astype(f32), unit_two[m], scale_two[m], gain_two)
        cot_own = cot_rows[m][:half].astype(f32)
        return (cot_own + norm_two_grad).astype(bf16)

    def middle_back(rows):
        rows, own, far = together(rows, back_own, back_far)
        mine = close_back(0, own, far)
        flying[0], flying[1] = mine, across(mine)
        return rows

    ffn(1, normed_two[1], middle_back)
    dh_own, dh_far = flying[0], flying[1]
    rows, dh_own, dh_far = together(ffn_back_rows(1), dh_own, dh_far)
    back_own, back_far = share(rows)
    back_own, normed_two[0], normed_two[1] = together(back_own, *normed_two)
    grads_down = sum(rows_contract(cot_rows[m], hidden[m]) for m in streams)
    grads_down, dh_far, gate_up[0], gate_up[1] = together(grads_down.astype(bf16), dh_far, *gate_up)
    sum_down = lax.psum_scatter(grads_down, "fsdp", scatter_dimension=0, tiled=True)
    pair = jnp.concatenate([dh_own, dh_far], axis=0)
    grad_attn.append(jnp.concatenate([pair, beside(pair)], axis=0))
    grads_in = sum(rows_contract(normed_two[m], gate_up[m]) for m in streams)
    grads_in, back_far = together(grads_in.astype(bf16), back_far)
    sum_in = lax.psum_scatter(grads_in, "fsdp", scatter_dimension=0, tiled=True)
    dh_own = close_back(1, back_own, back_far)
    dh_far = across(dh_own)
    hidden[0], hidden[1], dh_own = together(*hidden, dh_own)
    ffn_parts = [share(cols_contract(hidden[m], full_down).astype(bf16)) for m in streams]
    d_mixed = jnp.dot(grad_attn[0], full_out, preferred_element_type=f32).astype(bf16)
    y_own, y_far = [p[0] for p in ffn_parts], [p[1] for p in ffn_parts]
    d_mixed, y_own[0], y_own[1] = together(d_mixed, *y_own)
    d_proj = attention_bwd(proj, preps[0], saved[0], d_mixed, last[0], table[0], slot, heads, None)
    d_proj, dh_far, y_far[0], y_far[1] = together(d_proj, dh_far, *y_far)
    pair = jnp.concatenate([dh_own, dh_far], axis=0)
    grad_attn.append(jnp.concatenate([pair, beside(pair)], axis=0))
    d_mixed = jnp.dot(grad_attn[1], full_out, preferred_element_type=f32).astype(bf16)
    y_rows = jnp.concatenate(
        [(hidden_in[m] + y_own[m] + y_far[m].astype(f32)).astype(bf16) for m in streams], axis=0
    )
    grad_out = sum(rows_contract(grad_attn[m], saved[m][0]) for m in streams).astype(bf16)
    d_mixed, grad_out, y_rows = together(d_mixed, grad_out, y_rows)
    y_across = across(y_rows)
    d_proj = attention_bwd(proj, preps[1], saved[1], d_mixed, last[1], table[1], slot, heads, d_proj)
    d_proj, sum_down = together(d_proj, sum_down)
    attn_grads, d_proj, y_rows = together(rows_contract(normed, d_proj).astype(bf16), d_proj, y_rows)
    y_pair = jnp.concatenate([y_rows, y_across], axis=0)
    rows_one, y_other, attn_grads, sum_in = together(
        cols_contract(d_proj, w_in).astype(bf16), beside(y_pair), attn_grads, sum_in
    )
    grad_one = lax.psum_scatter(rows_one, "tp", scatter_dimension=0, tiled=True)
    dh_own, out_y = pick_blocks([grad_attn, [y_rows, y_across, y_other]], [own_places, own_spots])
    attn_grads, dh_own, out_y = together(attn_grads, dh_own, out_y)
    attn_sum, grad_out = ring_sum([attn_grads, grad_out], "fsdp")
    sum_in, sum_down = sum_in.astype(f32), sum_down.astype(f32)
    grad_one = grad_one.astype(f32)
    unit_one, scale_one = unit_rows(tokens.astype(f32))
    norm_one_grad = norm_back(grad_one, unit_one, scale_one, gain_one)
    out_dx = (dh_own.astype(f32) + norm_one_grad).astype(bf16)
    dots = lambda grads, weights: jnp.sum(grads * weights.astype(f32), axis=1)
    own_one = dots(attn_sum[:, : 4 * width], attn_pack[:, : 4 * width]) + dots(
        attn_sum[:, 4 * width : 4 * width + heads], w_beta
    )
    own_two = dots(sum_in, ffn_pack)
    gains = tp_sum(jnp.stack([own_one, own_two])) / jnp.stack([gain_attn, gain_ffn]).astype(f32)
    return (
        out_y,
        out_dx,
        attn_sum[:, :width],
        attn_sum[:, width : 2 * width],
        attn_sum[:, 2 * width : 3 * width],
        attn_sum[:, 3 * width : 4 * width],
        attn_sum[:, 4 * width : 4 * width + heads],
        grad_out,
        sum_in[:, :hidden_width],
        sum_in[:, hidden_width:],
        sum_down,
        gains[0],
        gains[1],
    )


def solution(mesh):
    rows = P(("fsdp", "tp"), None)
    weight = P("fsdp", "tp")
    return jax.shard_map(
        local,
        mesh=mesh,
        in_specs=(rows, rows) + (weight,) * 9 + (P("fsdp"), P("fsdp"), P("fsdp", None, None), P("fsdp", None, None)),
        out_specs=(rows, rows) + (weight,) * 9 + (P("fsdp"), P("fsdp")),
        check_vma=False,
    )
```

```python
import functools

import jax
import jax.numpy as jnp
from jax import lax
from jax.experimental import pallas as pl
from jax.experimental.pallas import tpu as pltpu
from jax.sharding import PartitionSpec as P

BLOCK = 128
epsilon = 1e-06
bf16 = jnp.bfloat16
f32 = jnp.float32


def mm(a, b):
    return lax.dot_general(a, b, (((1,), (0,)), ((), ())), preferred_element_type=f32)


def mm_rt(a, b):
    return lax.dot_general(a, b, (((1,), (1,)), ((), ())), preferred_element_type=f32)


def mm_lt(a, b):
    return lax.dot_general(a, b, (((0,), (0,)), ((), ())), preferred_element_type=f32)


def iotas():
    rows = lax.broadcasted_iota(jnp.int32, (BLOCK, BLOCK), 0)
    cols = lax.broadcasted_iota(jnp.int32, (BLOCK, BLOCK), 1)
    return rows, cols


def lockstep(tasks):
    tasks = list(tasks)
    while tasks:
        tasks = [task for task in tasks if next(task, None) is not None]


def strengths(u, r_col):
    uf = u.astype(f32)
    inv_sq = 1.0 / (jnp.sum(uf * uf, axis=1, keepdims=True) + epsilon)
    beta = 2.0 / (1.0 + jnp.exp(-r_col))
    return beta, inv_sq


def prep_kernel(heads, chunks, table_ref, *refs):
    q_refs, k_refs, u_refs, r_refs = (refs[n * chunks : (n + 1) * chunks] for n in range(4))
    near_ref, q0_ref, kp_ref, inv_ref, t_ref = refs[4 * chunks :]
    rows, cols = iotas()
    strict = rows > cols
    lower = rows >= cols
    diff = rows ^ cols
    eye = jnp.where(rows == cols, 1.0, 0.0).astype(f32)
    eye_b = eye.astype(bf16)
    items = [(c, h) for c in range(chunks) for h in range(heads)]
    state = []
    for c, h in items:
        cs = pl.ds(h * BLOCK, BLOCK)
        q, k, u = q_refs[c][:, cs], k_refs[c][:, cs], u_refs[c][:, cs]
        beta, inv_sq = strengths(u, r_refs[c][:, h : h + 1].astype(f32))
        bp = beta * inv_sq
        big = mm_rt(jnp.concatenate([u, q], axis=0), jnp.concatenate([u, k], axis=0))
        gram = big[:BLOCK, :BLOCK]
        e_s = jnp.where(strict, big[:BLOCK, BLOCK:], 0.0)
        a_s = jnp.where(lower, big[BLOCK:, :BLOCK], 0.0)
        n0 = big[BLOCK:, BLOCK:]
        low = jnp.where(strict, gram * bp, 0.0)
        eu = jnp.concatenate([e_s * bp, u.astype(f32) * bp], axis=1).astype(bf16)
        start = (eye - jnp.where(diff < 2, low, 0.0)).astype(bf16)
        state.append([q, k, u, a_s.astype(bf16), n0, low.astype(bf16), eu, start])
    def invert(st, delay):
        for _ in range(delay):
            yield 1
        size = 2
        while size < BLOCK:
            sel = jnp.where((diff >= size) & (diff < 2 * size), 1.0, 0.0).astype(bf16)
            if size < 16:
                y = mm(st[5] * sel, st[7]).astype(bf16)
                yield 1
                st[7] = st[7] - mm(st[7], y).astype(bf16)
            else:
                groups = range(size, BLOCK, 2 * size)
                odd = lambda x: jnp.concatenate([x[g : g + size] for g in groups], axis=0)
                blank = jnp.zeros((size, BLOCK), bf16)
                y = mm(odd(st[5]) * odd(sel), st[7]).astype(bf16)
                yield 1
                pieces = []
                for n in range(len(groups)):
                    pieces += [blank, y[n * size : (n + 1) * size]]
                rows_odd = odd(st[7])
                fresh = rows_odd - mm(rows_odd, jnp.concatenate(pieces, axis=0)).astype(bf16)
                pieces = []
                for n, g in enumerate(groups):
                    pieces += [st[7][g - size : g], fresh[n * size : (n + 1) * size]]
                st[7] = jnp.concatenate(pieces, axis=0)
            yield 1
            size *= 2

    lockstep(invert(st, n % 2) for n, st in enumerate(state))
    def close(item, st, delay):
        for _ in range(delay):
            yield 1
        c, h = item
        q, k, u, a_b, n0, low, eu, x = st
        rs, cs = pl.ds(c * BLOCK, BLOCK), pl.ds(h * BLOCK, BLOCK)
        t = mm(x, eu).astype(bf16)
        inv_ref[c, h] = x
        t_ref[c, h] = t
        yield 1
        top = mm(a_b, t)
        yield 1
        bot = mm_lt(u, t)
        near_ref[c, h] = n0 - top[:, :BLOCK]
        q0_ref[rs, cs] = (q.astype(f32) - top[:, BLOCK:]).astype(bf16)
        yield 1
        ket = mm_rt(eye_b, k) - bot[:, :BLOCK]
        kp_ref[c, h] = jnp.concatenate([ket, eye - bot[:, BLOCK:]], axis=1).astype(bf16)

    lockstep(close(item, st, 0) for n, (item, st) in enumerate(zip(items, state)))


def fwd_kernel(
    heads, depth, scale, first_ref, table_ref, slot_ref, q0_ref, near_ref, kp_ref, v_ref, o_ref, linv_ref, e_ref, cur_ref, s_ref, m_ref, acc_ref
):
    i = pl.program_id(0)
    first = first_ref[i]
    rows, cols = iotas()
    lower = rows >= cols
    neg = jnp.float32(-1e30)
    for h in range(heads):
        s0 = jnp.where(lower, near_ref[0, h], neg)
        s_ref[0, h] = s0
        m_ref[h] = s0
        cur_ref[0, 0, h] = q0_ref[:, h * BLOCK : (h + 1) * BLOCK]
    for d in range(1, depth):

        @pl.when(i - d >= first)
        def _():
            j = i - d
            for h in range(heads):
                both = mm(cur_ref[0, d - 1, h], kp_ref[j, h])
                s = both[:, :BLOCK]
                s_ref[d, h] = s
                m_ref[h] = jnp.maximum(m_ref[h], s)
                if d + 1 < depth:
                    cur_ref[0, d, h] = both[:, BLOCK:].astype(bf16)

    peaks = []
    for h in range(heads):
        peak = jnp.max(m_ref[h], axis=1, keepdims=True)
        peaks.append(peak)
        e0 = jnp.exp((s_ref[0, h] - peak) * scale)
        m_ref[h] = e0
        eb = e0.astype(bf16)
        e_ref[0, 0, h] = eb
        v = v_ref[pl.ds(pl.multiple_of(table_ref[i] * BLOCK, BLOCK), BLOCK), h * BLOCK : (h + 1) * BLOCK]
        acc_ref[h] = mm(eb, v)
    def weigh(d, carry):
        j = i - d
        at = pl.ds(pl.multiple_of(table_ref[j] * BLOCK, BLOCK), BLOCK)
        for h in range(heads):
            e = jnp.exp((s_ref[d, h] - peaks[h]) * scale)
            m_ref[h] = m_ref[h] + e
            eb = e.astype(bf16)
            e_ref[0, d, h] = eb
            acc_ref[h] = acc_ref[h] + mm(eb, v_ref[at, h * BLOCK : (h + 1) * BLOCK])
        return carry

    lax.fori_loop(1, i - first + 1, weigh, 0)

    for h in range(heads):
        linv = 1.0 / jnp.sum(m_ref[h], axis=1, keepdims=True)
        cs = slice(h * BLOCK, (h + 1) * BLOCK)
        o_ref[:, cs] = (acc_ref[h] * linv).astype(bf16)
        linv_ref[:, cs] = jnp.broadcast_to(linv, (BLOCK, BLOCK))


def bwd_kernel(heads, depth, scale, last_ref, table_ref, slot_ref, *refs):
    (do_ref, o_ref, linv_ref, q_ref, k_ref, v_ref, u_ref, r_ref, kp_ref, inv_ref, t_ref) = refs[:11]
    e_refs = refs[11 : 11 + depth]
    cur_refs = refs[11 + depth : 10 + 2 * depth]
    out_ref, dop_ref, del_ref, g_ref, dv_ref, acc_ref = refs[-6:]
    j = pl.program_id(0)
    last = last_ref[j]
    rows, cols = iotas()
    strict = rows > cols
    lower = rows >= cols
    upper = rows <= cols
    total = dop_ref.shape[0]

    @pl.when(j == 0)
    def _():
        for c in range(total // BLOCK):
            rs = pl.ds(c * BLOCK, BLOCK)
            for h in range(heads):
                cs = slice(h * BLOCK, (h + 1) * BLOCK)
                there = pl.ds(pl.multiple_of(slot_ref[c] * BLOCK, BLOCK), BLOCK)
                dop = do_ref[there, cs].astype(f32) * linv_ref[rs, cs]
                delta = jnp.sum(dop * o_ref[there, cs].astype(f32), axis=1, keepdims=True)
                dop_ref[rs, cs] = dop.astype(bf16)
                del_ref[rs, cs] = jnp.broadcast_to(delta, (BLOCK, BLOCK))
                g_ref[c, h] = jnp.zeros((BLOCK, BLOCK), bf16)

    here = pl.ds(pl.multiple_of(j * BLOCK, BLOCK), BLOCK)
    near = []
    for h in range(heads):
        cs = slice(h * BLOCK, (h + 1) * BLOCK)
        dop = dop_ref[here, cs]
        e = e_refs[0][0, 0, h]
        dp = mm_rt(dop, v_ref[:, cs])
        near.append((e.astype(f32) * (dp - del_ref[here, cs]) * scale).astype(bf16))
        dv_ref[h] = mm_lt(e, dop)
        acc_ref[h] = jnp.zeros((BLOCK, 2 * BLOCK), f32)
    for d in range(1, depth):

        @pl.when(j + d <= last)
        def _():
            i = j + d
            there = pl.ds(pl.multiple_of(i * BLOCK, BLOCK), BLOCK)
            def far(h):
                cs = slice(h * BLOCK, (h + 1) * BLOCK)
                dop = dop_ref[there, cs]
                e = e_refs[d][0, 0, h]
                dp = mm_rt(dop, v_ref[:, cs])
                yield 1
                dv_ref[h] = dv_ref[h] + mm_lt(e, dop)
                yield 1
                ds = (e.astype(f32) * (dp - del_ref[there, cs]) * scale).astype(bf16)
                dsg = jnp.concatenate([ds, g_ref[i, h]], axis=1)
                yield 1
                acc_ref[h] = acc_ref[h] + mm_lt(cur_refs[d - 1][0, 0, h], dsg)
                yield 1
                g_ref[i, h] = mm_rt(dsg, kp_ref[0, h]).astype(bf16)

            lockstep(far(h) for h in range(heads))

    lane = cols
    dr_all = jnp.zeros((BLOCK, BLOCK), f32)
    width = heads * BLOCK
    drs = {}

    def local_part(h):
        cs = slice(h * BLOCK, (h + 1) * BLOCK)
        q, k, u = q_ref[:, cs], k_ref[:, cs], u_ref[:, cs]
        kq = mm_rt(u, jnp.concatenate([k, q], axis=0))
        yield 1
        e_s = jnp.where(strict, kq[:, :BLOCK], 0.0).astype(bf16)
        a_t = jnp.where(upper, kq[:, BLOCK:], 0.0).astype(bf16)
        dn = near[h]
        acc = acc_ref[h]
        bmat = jnp.concatenate([jnp.concatenate([dn, g_ref[j, h]], axis=1), acc.astype(bf16)], axis=0)
        yz = mm(jnp.concatenate([a_t, u], axis=1), bmat).astype(bf16)
        yield 1
        ru = mm_rt(jnp.concatenate([e_s, u], axis=1), bmat)
        beta, inv_sq = strengths(u, r_ref[:, h : h + 1].astype(f32))
        bp = beta * inv_sq
        yield 1
        inv = inv_ref[0, h]
        left = mm_lt(inv, yz) * (-bp)
        yield 1
        right = -mm(inv, (ru * bp).astype(bf16))
        yield 1
        d_s = jnp.where(strict, -mm_rt(left.astype(bf16), t_ref[0, h]), 0.0).astype(bf16)
        d_e = jnp.where(strict, left[:, :BLOCK], 0.0).astype(bf16)
        d_at = jnp.where(upper, right[:, :BLOCK], 0.0).astype(bf16)
        du = left[:, BLOCK:] + right[:, BLOCK:]
        yield 1
        d_a = d_at.astype(f32).T.astype(bf16)
        uk = jnp.concatenate([u, k], axis=0)
        dq_o = g_ref[j, h].astype(f32) + mm(jnp.concatenate([d_a, dn], axis=1), uk)
        out_ref[:, cs] = dq_o.astype(bf16)
        yield 1
        uq = jnp.concatenate([u, q], axis=0)
        dk_o = acc_ref[h][:, :BLOCK].T + mm_lt(jnp.concatenate([d_e, dn], axis=0), uq)
        out_ref[:, width + h * BLOCK : width + (h + 1) * BLOCK] = dk_o.astype(bf16)
        yield 1
        du = du + mm(jnp.concatenate([d_s, d_e], axis=1), uk)
        d_st = d_s.astype(f32).T.astype(bf16)
        du = du + mm(jnp.concatenate([d_st, d_at], axis=1), uq)
        yield 1
        uf = u.astype(f32)
        rad = jnp.sum(uf * du, axis=1, keepdims=True)
        du = du - (inv_sq * rad) * uf
        drs[h] = 0.5 * rad * (1.0 - 0.5 * beta)
        out_ref[:, 2 * width + h * BLOCK : 2 * width + (h + 1) * BLOCK] = dv_ref[h].astype(bf16)
        out_ref[:, 3 * width + h * BLOCK : 3 * width + (h + 1) * BLOCK] = du.astype(bf16)

    lockstep(local_part(h) for h in range(heads))
    for h in range(heads):
        dr_all = jnp.where(lane == h, drs[h], dr_all)
    out_ref[:, 4 * width :] = dr_all.astype(bf16)


def attention_prep(proj, table, heads):
    count = table.shape[0]
    width = heads * BLOCK
    step = 4

    def rows(c, n, col):
        return pl.BlockSpec((BLOCK, n), lambda i, t: (t[i * step + c], col))

    tile = lambda n: pl.BlockSpec((step, heads, BLOCK, n), lambda i, t: (i, 0, 0, 0))
    shape = lambda n, t: jax.ShapeDtypeStruct((count, heads, BLOCK, n), t)
    spec = pltpu.PrefetchScalarGridSpec(
        num_scalar_prefetch=1,
        grid=(count // step,),
        in_specs=[rows(c, width, col) for col in (0, 1, 3) for c in range(step)]
        + [rows(c, BLOCK, 4 * heads) for c in range(step)],
        out_specs=[
            tile(BLOCK),
            pl.BlockSpec((step * BLOCK, width), lambda i, t: (i, 0)),
            tile(2 * BLOCK),
            tile(BLOCK),
            tile(2 * BLOCK),
        ],
    )
    return pl.pallas_call(
        functools.partial(prep_kernel, heads, step),
        grid_spec=spec,
        out_shape=[
            shape(BLOCK, f32),
            jax.ShapeDtypeStruct((count * BLOCK, width), bf16),
            shape(2 * BLOCK, bf16),
            shape(BLOCK, bf16),
            shape(2 * BLOCK, bf16),
        ],
        cost_estimate=pl.CostEstimate(
            flops=count * heads * 45 * BLOCK**3, bytes_accessed=6 * count * BLOCK * width, transcendentals=0
        ),
        name="attn_prep",
    )(table, *([proj] * (4 * step)))


def attention_fwd(proj, prep, first, table, slot, heads):
    near, q0, kp, _, _ = prep
    count = table.shape[0]
    depth = count
    width = heads * BLOCK
    scale = float(BLOCK) ** -0.5
    spec = pltpu.PrefetchScalarGridSpec(
        num_scalar_prefetch=3,
        grid=(count,),
        in_specs=[
            pl.BlockSpec((BLOCK, width), lambda i, f, t, w: (i, 0)),
            pl.BlockSpec((1, heads, BLOCK, BLOCK), lambda i, f, t, w: (i, 0, 0, 0)),
            pl.BlockSpec((count, heads, BLOCK, 2 * BLOCK), lambda i, f, t, w: (0, 0, 0, 0)),
            pl.BlockSpec((proj.shape[0], width), lambda i, f, t, w: (0, 2)),
        ],
        out_specs=[
            pl.BlockSpec((BLOCK, width), lambda i, f, t, w: (w[i], 0)),
            pl.BlockSpec((BLOCK, width), lambda i, f, t, w: (i, 0)),
            pl.BlockSpec((1, depth, heads, BLOCK, BLOCK), lambda i, f, t, w: (i, 0, 0, 0, 0)),
            pl.BlockSpec((1, depth - 1, heads, BLOCK, BLOCK), lambda i, f, t, w: (i, 0, 0, 0, 0)),
        ],
        scratch_shapes=[
            pltpu.VMEM((depth, heads, BLOCK, BLOCK), f32),
            pltpu.VMEM((heads, BLOCK, BLOCK), f32),
            pltpu.VMEM((heads, BLOCK, BLOCK), f32),
        ],
    )
    return pl.pallas_call(
        functools.partial(fwd_kernel, heads, depth, scale),
        grid_spec=spec,
        out_shape=[
            jax.ShapeDtypeStruct((count * BLOCK, width), bf16),
            jax.ShapeDtypeStruct((count * BLOCK, width), f32),
            jax.ShapeDtypeStruct((count, depth, heads, BLOCK, BLOCK), bf16),
            jax.ShapeDtypeStruct((count, depth - 1, heads, BLOCK, BLOCK), bf16),
        ],
        cost_estimate=pl.CostEstimate(
            flops=count * heads * 48 * BLOCK**3, bytes_accessed=6 * count * BLOCK * width, transcendentals=0
        ),
        name="attn_fwd",
    )(first, table, slot, q0, near, kp, proj)


def attention_bwd(proj, prep, saved, d_mixed, last, table, slot, heads, filled):
    _, _, kp, inv, t_all = prep
    mixed, linv, e_all, cur_all = saved
    count = table.shape[0]
    depth = count
    total = count * BLOCK
    width = heads * BLOCK
    scale = float(BLOCK) ** -0.5
    full = lambda: pl.BlockSpec((total, width), lambda j, f, t, w: (0, 0))
    wide = lambda col: pl.BlockSpec((BLOCK, width), lambda j, f, t, w: (t[j], col))
    tile = lambda n: pl.BlockSpec((1, heads, BLOCK, n), lambda j, f, t, w: (j, 0, 0, 0))

    def diagonal(d, slot):
        return pl.BlockSpec(
            (1, 1, heads, BLOCK, BLOCK), lambda j, f, t, w: (jnp.minimum(j + d, count - 1), slot, 0, 0, 0)
        )

    in_specs = [
        full(),
        full(),
        full(),
        wide(0),
        wide(1),
        wide(2),
        wide(3),
        pl.BlockSpec((BLOCK, BLOCK), lambda j, f, t, w: (t[j], 4 * heads)),
        tile(2 * BLOCK),
        tile(BLOCK),
        tile(2 * BLOCK),
    ]
    in_specs += [diagonal(d, d) for d in range(depth)] + [diagonal(d, d - 1) for d in range(1, depth)]
    operands = [last, table, slot, d_mixed, mixed, linv, proj, proj, proj, proj, proj, kp, inv, t_all]
    operands += [e_all] * depth + [cur_all] * (depth - 1)
    aliases = {}
    if filled is not None:
        aliases = {len(operands): 0}
        in_specs.append(pl.BlockSpec(memory_space=pl.ANY))
        operands.append(filled)
    spec = pltpu.PrefetchScalarGridSpec(
        num_scalar_prefetch=3,
        grid=(count,),
        in_specs=in_specs,
        out_specs=pl.BlockSpec((BLOCK, 4 * width + BLOCK), lambda j, f, t, w: (t[j], 0)),
        scratch_shapes=[
            pltpu.VMEM((total, width), bf16),
            pltpu.VMEM((total, width), f32),
            pltpu.VMEM((count, heads, BLOCK, BLOCK), bf16),
            pltpu.VMEM((heads, BLOCK, BLOCK), f32),
            pltpu.VMEM((heads, BLOCK, 2 * BLOCK), f32),
        ],
    )
    return pl.pallas_call(
        functools.partial(bwd_kernel, heads, depth, scale),
        grid_spec=spec,
        out_shape=jax.ShapeDtypeStruct((proj.shape[0], 4 * width + BLOCK), bf16),
        input_output_aliases=aliases,
        cost_estimate=pl.CostEstimate(
            flops=count * heads * 120 * BLOCK**3, bytes_accessed=8 * total * width, transcendentals=0
        ),
        name="attn_bwd",
    )(*operands)


def gather_kernel(group, table_ref, *refs):
    outs = refs[-(len(refs) // (group + 1)) :]
    for m, dst in enumerate(outs):
        for c in range(group):
            dst[c * BLOCK : (c + 1) * BLOCK, :] = refs[m * group + c][...]


def gather_blocks(x, tables, group):
    streams, count = tables.shape
    cols = x.shape[1]

    def source(m, c):
        return pl.BlockSpec((BLOCK, cols), lambda i, t: (t[m * count + i * group + c], 0))

    spec = pltpu.PrefetchScalarGridSpec(
        num_scalar_prefetch=1,
        grid=(count // group,),
        in_specs=[source(m, c) for m in range(streams) for c in range(group)],
        out_specs=[pl.BlockSpec((group * BLOCK, cols), lambda i, t: (i, 0))] * streams,
    )
    return pl.pallas_call(
        functools.partial(gather_kernel, group),
        grid_spec=spec,
        out_shape=[jax.ShapeDtypeStruct((count * BLOCK, cols), x.dtype)] * streams,
        cost_estimate=pl.CostEstimate(flops=0, bytes_accessed=4 * streams * count * BLOCK * cols, transcendentals=0),
        name="gather_blocks",
    )(tables.reshape(-1), *([x] * (group * streams)))


def pick_kernel(bounds, picks, table_ref, *refs):
    total = sum(len(part) for part in bounds)
    parts, outs = refs[:total], refs[total:-3]
    held, load_sem, store_sem = refs[-3:]
    stores = []
    base = 0
    for group, limits in enumerate(bounds):
        for n in range(picks):
            slot = group * picks + n
            at = table_ref[slot]
            for p, (low, high) in enumerate(limits):

                @pl.when((at >= low) & (at < high))
                def _():
                    rows = pl.ds(pl.multiple_of((at - low) * BLOCK, BLOCK), BLOCK)
                    pltpu.make_async_copy(parts[base + p].at[rows, :], held.at[slot], load_sem.at[slot]).start()

        base += len(limits)
    for group in range(len(bounds)):
        for n in range(picks):
            slot = group * picks + n
            rows = pl.ds(n * BLOCK, BLOCK)
            pltpu.make_async_copy(outs[group].at[rows, :], held.at[slot], load_sem.at[slot]).wait()
            stores.append(pltpu.make_async_copy(held.at[slot], outs[group].at[rows, :], store_sem.at[slot]))
            stores[-1].start()
    for store in stores:
        store.wait()


def pick_blocks(groups, tables):
    picks = tables[0].shape[0]
    cols = groups[0][0].shape[1]
    dtype = groups[0][0].dtype
    bounds = []
    for parts in groups:
        limits, low = [], 0
        for part in parts:
            limits.append((low, low + part.shape[0] // BLOCK))
            low = limits[-1][1]
        bounds.append(limits)
    flat = [part for parts in groups for part in parts]
    slots = picks * len(groups)
    spec = pltpu.PrefetchScalarGridSpec(
        num_scalar_prefetch=1,
        grid=(1,),
        in_specs=[pl.BlockSpec(memory_space=pl.ANY)] * len(flat),
        out_specs=[pl.BlockSpec(memory_space=pl.ANY)] * len(groups),
        scratch_shapes=[
            pltpu.VMEM((slots, BLOCK, cols), dtype),
            pltpu.SemaphoreType.DMA((slots,)),
            pltpu.SemaphoreType.DMA((slots,)),
        ],
    )
    return pl.pallas_call(
        functools.partial(pick_kernel, bounds, picks),
        grid_spec=spec,
        out_shape=[jax.ShapeDtypeStruct((picks * BLOCK, cols), dtype)] * len(groups),
        cost_estimate=pl.CostEstimate(flops=0, bytes_accessed=4 * slots * BLOCK * cols, transcendentals=0),
        name="pick_blocks",
    )(jnp.concatenate(tables).astype(jnp.int32), *flat)


def place_kernel(count, rows, spot_ref, *refs):
    pieces, out, bufs, sem_in, sem_out = refs[:count], refs[count], refs[count + 1], refs[count + 2], refs[count + 3]
    loads = [pltpu.make_async_copy(pieces[n], bufs.at[n], sem_in.at[n]) for n in range(count)]
    for load in loads:
        load.start()
    stores = []
    for n in range(count):
        loads[n].wait()
        to = out.at[pl.ds(pl.multiple_of(spot_ref[n] * rows, rows), rows), :]
        stores.append(pltpu.make_async_copy(bufs.at[n], to, sem_out.at[n]))
        stores[n].start()
    for store in stores:
        store.wait()


def place_pieces(pieces, spots, count):
    rows, cols = pieces[0].shape
    held = len(pieces)
    dtype = pieces[0].dtype
    spec = pltpu.PrefetchScalarGridSpec(
        num_scalar_prefetch=1,
        grid=(1,),
        in_specs=[pl.BlockSpec(memory_space=pl.ANY)] * held,
        out_specs=pl.BlockSpec(memory_space=pl.ANY),
        scratch_shapes=[
            pltpu.VMEM((held, rows, cols), dtype),
            pltpu.SemaphoreType.DMA((held,)),
            pltpu.SemaphoreType.DMA((held,)),
        ],
    )
    where = jnp.concatenate([jnp.reshape(spot, (1,)) for spot in spots]).astype(jnp.int32)
    return pl.pallas_call(
        functools.partial(place_kernel, held, rows),
        grid_spec=spec,
        out_shape=jax.ShapeDtypeStruct((count * rows, cols), dtype),
        cost_estimate=pl.CostEstimate(flops=0, bytes_accessed=4 * held * rows * cols, transcendentals=0),
        name="place_pieces",
    )(where, *pieces)


def open_kernel(spot_ref, x_ref, out_ref):
    out_ref[...] = x_ref[...]


def open_buffer(x, spot, count):
    rows, cols = x.shape
    spec = pltpu.PrefetchScalarGridSpec(
        num_scalar_prefetch=1,
        grid=(2,),
        in_specs=[pl.BlockSpec((rows // 2, cols), lambda i, t: (i, 0))],
        out_specs=pl.BlockSpec((rows // 2, cols), lambda i, t: (2 * t[0] + i, 0)),
    )
    return pl.pallas_call(
        open_kernel,
        grid_spec=spec,
        out_shape=jax.ShapeDtypeStruct((count * rows, cols), x.dtype),
        cost_estimate=pl.CostEstimate(flops=0, bytes_accessed=4 * rows * cols, transcendentals=0),
        name="open_buffer",
    )(jnp.reshape(spot, (1,)).astype(jnp.int32), x)


def rows_contract(a, b):
    return lax.dot_general(a, b, (((0,), (0,)), ((), ())), preferred_element_type=f32)


def cols_contract(a, b):
    return lax.dot_general(a, b, (((1,), (1,)), ((), ())), preferred_element_type=f32)


def unit_rows(x):
    scale = lax.rsqrt(jnp.mean(x * x, axis=1, keepdims=True) + epsilon)
    return x * scale, scale


def norm_back(grad_normed, unit, scale, gain):
    grad_unit = grad_normed * gain
    return scale * (grad_unit - unit * jnp.mean(grad_unit * unit, axis=1, keepdims=True))


def ring_order(count):
    return list(range(0, count, 2)) + list(range(1, count, 2))[::-1]


def ring_tables(axis):
    count = lax.axis_size(axis)
    order = ring_order(count)
    right = [(order[p], order[(p + 1) % count]) for p in range(count)]
    left = [(order[p], order[(p - 1) % count]) for p in range(count)]
    me = lax.axis_index(axis)
    spot = jnp.where(me % 2 == 0, me // 2, count - 1 - me // 2)

    def owner(shift):
        at = (spot + shift + count) % count
        return jnp.where(at < count // 2, 2 * at, 2 * (count - 1 - at) + 1)

    return count, right, left, owner


class RingGather:
    def __init__(self, x, axis, whole=False):
        self.axis, self.x, self.whole = axis, x, whole
        self.count, self.right, self.left, self.owner = ring_tables(axis)
        self.moving = (x, x)
        self.hops = []

    def hop(self):
        from_left, from_right = self.moving
        if len(self.hops) == self.count // 2 - 1:
            half = self.x.shape[0] // 2
            from_left, from_right = from_left[:half], from_right[half:]
        self.moving = (
            lax.ppermute(from_left, self.axis, self.right),
            lax.ppermute(from_right, self.axis, self.left),
        )
        self.hops.append(self.moving)

    def before(self, *values):
        held = lax.optimization_barrier((self.moving,) + values)
        self.moving = held[0]
        self.hops[-1] = self.moving
        return held[1] if len(values) == 1 else held[1:]

    def finish(self):
        while len(self.hops) < self.count // 2:
            self.hop()
        rows = self.x.shape[0]
        put = lax.dynamic_update_slice_in_dim
        pieces, spots = [self.x], [self.owner(0)]
        for s, (from_left, from_right) in enumerate(self.hops[:-1], 1):
            pieces += [from_left, from_right]
            spots += [self.owner(-s), self.owner(s)]
        if self.whole:
            out = place_pieces(pieces, spots, self.count)
        else:
            out = open_buffer(self.x, spots[0], self.count)
            for piece, spot in zip(pieces[1:], spots[1:]):
                out = put(out, piece, spot * rows, 0)
        far = self.owner(self.count // 2) * rows
        out = put(out, self.hops[-1][0], far, 0)
        return put(out, self.hops[-1][1], far + rows // 2, 0)


class RingScatter:
    def __init__(self, parts, axis):
        self.axis, self.parts = axis, parts
        self.count, self.right, self.left, self.owner = ring_tables(axis)
        self.rows = parts[0].shape[0] // self.count
        self.top = self.count // 2
        self.done = 0
        half = self.rows // 2
        self.moving = (self.piece(self.top, 0, half), self.piece(-self.top, half, half))

    def piece(self, shift, start=0, size=None):
        size = self.rows if size is None else size
        at = self.owner(shift) * self.rows + start
        return jnp.concatenate([lax.dynamic_slice_in_dim(part, at, size, 0) for part in self.parts], axis=1)

    def hop(self):
        to_right, to_left = self.moving
        if self.done > 0:
            s = self.top - self.done
            a, b = self.piece(s), self.piece(-s)
            if self.done == 1:
                half = self.rows // 2
                to_right = jnp.concatenate([a[:half] + to_right, a[half:]], axis=0)
                to_left = jnp.concatenate([b[:half], b[half:] + to_left], axis=0)
            else:
                to_right, to_left = a + to_right, b + to_left
        self.moving = (lax.ppermute(to_right, self.axis, self.right), lax.ppermute(to_left, self.axis, self.left))
        self.done += 1

    def before(self, *values):
        held = lax.optimization_barrier((self.moving,) + values)
        self.moving = held[0]
        return held[1] if len(values) == 1 else held[1:]

    def finish(self):
        while self.done < self.top:
            self.hop()
        return self.piece(0).astype(f32) + self.moving[0].astype(f32) + self.moving[1].astype(f32)


def ring_kernel(axis, count, rows, widths, *refs):
    held = len(widths)
    parts, outs = refs[:held], refs[held : 2 * held]
    own_buf, send_buf, recv_buf, load_sem, send_sem, recv_sem = refs[2 * held :]
    me = lax.axis_index(axis)
    odd = me % 2
    spot = (1 - odd) * (me // 2) + odd * (count - 1 - me // 2)

    def owner(shift):
        at = (spot + shift + count) % count
        upper = at // (count // 2)
        return (1 - upper) * (2 * at) + upper * (2 * (count - 1 - at) + 1)

    top = count // 2
    cut = rows // 32 * 16
    ways = ((1, owner(1)), (-1, owner(-1)))
    barrier = pltpu.get_barrier_semaphore()
    for _, peer in ways:
        pl.semaphore_signal(barrier, inc=1, device_id={axis: peer}, device_id_type=pl.DeviceIdType.MESH)

    def load(shift, slot):
        copies = []
        at = pl.multiple_of(owner(shift) * rows, rows)
        col = 0
        for n, width in enumerate(widths):
            copies.append(
                pltpu.make_async_copy(
                    parts[n].at[pl.ds(at, rows), :],
                    own_buf.at[slot, :, pl.ds(col, width)],
                    load_sem.at[slot, n],
                )
            )
            col += width
        for copy in copies:
            copy.start()
        return copies

    slots = {top: 0, 0: 2 * top - 1}
    for s in range(1, top):
        slots[s], slots[-s] = 2 * s - 1, 2 * s
    loads = {}
    for shift in [top] + [t * s for s in range(top - 1, 0, -1) for t in (1, -1)] + [0]:
        loads[shift] = load(shift, slots[shift])
    for copy in loads[top]:
        copy.wait()
    pl.semaphore_wait(barrier, 2)
    halves = ((0, cut), (cut, rows - cut))
    sent = []

    def push(way, hop, part, src):
        start, size = halves[part]
        copy = pltpu.make_async_remote_copy(
            src_ref=src,
            dst_ref=recv_buf.at[way, hop, pl.ds(start, size), :],
            send_sem=send_sem.at[way, hop, part],
            recv_sem=recv_sem.at[way, hop, part],
            device_id={axis: ways[way][1]},
            device_id_type=pl.DeviceIdType.MESH,
        )
        copy.start()
        sent.append(copy)
        return copy

    flying = {}
    for way in range(2):
        start, size = halves[way]
        flying[way, way] = push(way, 0, way, own_buf.at[slots[top], pl.ds(start, size), :])
    for hop in range(1, top):
        shift = top - hop
        order = [(way, 1 - way) for way in range(2)] + [(way, way) for way in range(2)]
        for way, part in order:
            sign = ways[way][0]
            start, size = halves[part]
            slot = slots[sign * shift]
            if part == 1 - way:
                for copy in loads[sign * shift]:
                    copy.wait()
            area = pl.ds(start, size)
            if hop == 1 and part == 1 - way:
                flying[way, part] = push(way, hop, part, own_buf.at[slot, area, :])
                continue
            flying[way, part].wait_recv()
            total = own_buf[slot, area, :].astype(f32) + recv_buf[way, hop - 1, area, :].astype(f32)
            send_buf[way, hop - 1, area, :] = total.astype(bf16)
            flying[way, part] = push(way, hop, part, send_buf.at[way, hop - 1, area, :])
    for copy in loads[0]:
        copy.wait()
    for part in range(2):
        start, size = halves[part]
        area = pl.ds(start, size)
        for way in range(2):
            flying[way, part].wait_recv()
        col = 0
        for n, width in enumerate(widths):
            cols = pl.ds(col, width)
            outs[n][area, :] = (
                own_buf[slots[0], area, cols].astype(f32)
                + recv_buf[0, top - 1, area, cols].astype(f32)
                + recv_buf[1, top - 1, area, cols].astype(f32)
            )
            col += width
    for copy in sent:
        copy.wait_send()


def spread_kernel(axis, count, rows, widths, *refs):
    held = len(widths)
    parts, out = refs[:held], refs[held]
    own_buf, left_buf, right_buf, load_sem, store_sem, send_sem, recv_sem = refs[held + 1 :]
    me = lax.axis_index(axis)
    odd = me % 2
    spot = (1 - odd) * (me // 2) + odd * (count - 1 - me // 2)

    def owner(shift):
        at = (spot + shift + count) % count
        upper = at // (count // 2)
        return (1 - upper) * (2 * at) + upper * (2 * (count - 1 - at) + 1)

    top = count // 2
    cut = rows // 32 * 16
    halves = ((0, cut), (cut, rows - cut))
    peers = (owner(1), owner(-1))
    barrier = pltpu.get_barrier_semaphore()
    for peer in peers:
        pl.semaphore_signal(barrier, inc=1, device_id={axis: peer}, device_id_type=pl.DeviceIdType.MESH)
    loads, col = [], 0
    for n, width in enumerate(widths):
        loads.append(pltpu.make_async_copy(parts[n], own_buf.at[:, pl.ds(col, width)], load_sem.at[n]))
        loads[-1].start()
        col += width
    for load in loads:
        load.wait()
    pl.semaphore_wait(barrier, 2)
    bufs = (left_buf, right_buf)
    flying, sent, stores = {}, [], []

    def push(way, hop, part, src):
        start, size = halves[part]
        copy = pltpu.make_async_remote_copy(
            src_ref=src,
            dst_ref=bufs[way].at[hop, pl.ds(start, size), :],
            send_sem=send_sem.at[way, hop, part],
            recv_sem=recv_sem.at[way, hop, part],
            device_id={axis: peers[way]},
            device_id_type=pl.DeviceIdType.MESH,
        )
        copy.start()
        sent.append(copy)
        flying[way, hop, part] = copy

    def store(src, shift, part, sem):
        start, size = halves[part]
        at = pl.multiple_of(owner(shift) * rows + start, 16)
        stores.append(pltpu.make_async_copy(src, out.at[pl.ds(at, size), :], sem))
        stores[-1].start()

    for part in range(2):
        for way in range(2):
            start, size = halves[part]
            push(way, 0, part, own_buf.at[pl.ds(start, size), :])
    for part in range(2):
        start, size = halves[part]
        store(own_buf.at[pl.ds(start, size), :], 0, part, store_sem.at[2, 0, part])
    for hop in range(top):
        for part in range(2):
            for way in range(2):
                if hop == top - 1 and part != way:
                    continue
                start, size = halves[part]
                here = bufs[way].at[hop, pl.ds(start, size), :]
                flying[way, hop, part].wait_recv()
                if hop + 1 < top - 1 or (hop + 1 == top - 1 and part == way):
                    push(way, hop + 1, part, here)
                store(here, -(hop + 1) if way == 0 else hop + 1, part, store_sem.at[way, hop, part])
    for copy in sent:
        copy.wait_send()
    for copy in stores:
        copy.wait()


def ring_spread(parts, axis):
    count = lax.axis_size(axis)
    rows = parts[0].shape[0]
    widths = [part.shape[1] for part in parts]
    cols = sum(widths)
    top = count // 2
    return pl.pallas_call(
        functools.partial(spread_kernel, axis, count, rows, widths),
        in_specs=[pl.BlockSpec(memory_space=pl.ANY)] * len(parts),
        out_specs=pl.BlockSpec(memory_space=pl.ANY),
        out_shape=jax.ShapeDtypeStruct((count * rows, cols), bf16),
        scratch_shapes=[
            pltpu.VMEM((rows, cols), bf16),
            pltpu.VMEM((top, rows, cols), bf16),
            pltpu.VMEM((top, rows, cols), bf16),
            pltpu.SemaphoreType.DMA((len(parts),)),
            pltpu.SemaphoreType.DMA((3, top, 2)),
            pltpu.SemaphoreType.DMA((2, top, 2)),
            pltpu.SemaphoreType.DMA((2, top, 2)),
        ],
        compiler_params=pltpu.CompilerParams(collective_id=1, has_side_effects=True),
        cost_estimate=pl.CostEstimate(flops=0, bytes_accessed=4 * count * rows * cols, transcendentals=0),
        name="ring_spread",
    )(*parts)


def ring_sum(parts, axis):
    count = lax.axis_size(axis)
    rows = parts[0].shape[0] // count
    widths = [part.shape[1] for part in parts]
    cols = sum(widths)
    top = count // 2
    sent = (2 * top - 1) * rows * cols * 2
    return pl.pallas_call(
        functools.partial(ring_kernel, axis, count, rows, widths),
        in_specs=[pl.BlockSpec(memory_space=pl.ANY)] * len(parts),
        out_specs=[pl.BlockSpec(memory_space=pltpu.VMEM)] * len(parts),
        out_shape=[jax.ShapeDtypeStruct((rows, width), f32) for width in widths],
        scratch_shapes=[
            pltpu.VMEM((count, rows, cols), bf16),
            pltpu.VMEM((2, top - 1, rows, cols), bf16),
            pltpu.VMEM((2, top, rows, cols), bf16),
            pltpu.SemaphoreType.DMA((count, len(parts))),
            pltpu.SemaphoreType.DMA((2, top, 2)),
            pltpu.SemaphoreType.DMA((2, top, 2)),
        ],
        compiler_params=pltpu.CompilerParams(collective_id=0, has_side_effects=True),
        cost_estimate=pl.CostEstimate(flops=0, bytes_accessed=4 * count * rows * cols, transcendentals=0),
        name="ring_sum",
    )(*parts)


def tp_sum(x):
    count = lax.axis_size("tp")
    me = lax.axis_index("tp")
    pieces = [x] + [lax.ppermute(x, "tp", [(i, (i + s) % count) for i in range(count)]) for s in range(1, count)]
    stacked = jnp.stack(pieces)
    slots = (me - jnp.arange(count, dtype=jnp.int32)) % count
    total = jnp.zeros_like(x)
    for r in range(count):
        total = total + jnp.sum(jnp.where((slots == r)[:, None, None], stacked, 0.0), axis=0)
    return total


SLOTS = (0, 2, 1, 3)


def across(x):
    return lax.ppermute(x, "tp", [(i, i ^ 2) for i in range(4)])


def beside(x):
    return lax.ppermute(x, "tp", [(i, i ^ 1) for i in range(4)])


def share(rows):
    size = rows.shape[0] // 4
    other = beside(rows[2 * size :])
    pair = rows[: 2 * size].astype(f32) + other.astype(f32)
    return pair[:size], across(pair[size:].astype(bf16))


def spread(x):
    pair = jnp.concatenate([x, across(x)], axis=0)
    return jnp.concatenate([pair, beside(pair)], axis=0)


def together(*values):
    return lax.optimization_barrier(values)


def local(
    tokens,
    cotangent,
    w_query,
    w_key,
    w_value,
    w_house,
    w_beta,
    w_out,
    w_gate,
    w_up,
    w_down,
    gain_attn,
    gain_ffn,
    pack_index,
    seq_start,
):
    packing, begins = pack_index[0], seq_start[0]
    bins, bin_rows = packing.shape
    per_bin = bin_rows // BLOCK
    streams = range(bins)
    width = w_query.shape[1]
    heads = w_beta.shape[1]
    hidden_width = w_gate.shape[1]
    shard = w_query.shape[0]
    ranks = 4
    assert lax.axis_size("tp") == ranks
    half = bin_rows // ranks
    per_half = half // BLOCK
    me = lax.axis_index("tp")

    given = packing[:, ::BLOCK] // BLOCK
    per_own = bins * per_half
    table = given
    first = begins[:, ::BLOCK] // BLOCK
    spots = jnp.arange(per_bin, dtype=jnp.int32)
    last = jnp.max(jnp.where(first[:, :, None] == first[:, None, :], spots[None, None, :], 0), axis=2)
    away = me ^ (spots // per_half)
    slot = ((away // 2) + 2 * (away % 2)) * per_half + spots % per_half
    places = jnp.arange(bins, dtype=jnp.int32)[:, None] * per_bin + slot[None, :]
    blocks = jnp.arange(bins * per_bin, dtype=jnp.int32)
    inverse = jnp.sum(jnp.where(given.reshape(-1)[:, None] == blocks[None, :], places.reshape(-1)[:, None], 0), axis=0)
    slotted = jnp.sum(jnp.where(slot[None, :, None] == spots[None, None, :], given[:, :, None], 0), axis=1)
    packed = jnp.sum(jnp.where(given.reshape(-1)[:, None] == blocks[None, :], blocks[:, None], 0), axis=0)
    mine = (blocks // per_own == me) & (blocks >= 0)
    pull = jnp.arange(per_own, dtype=jnp.int32)[:, None] == jnp.where(mine, blocks % per_own, -1)[None, :]
    own_places = jnp.sum(jnp.where(pull, inverse[None, :], 0), axis=1)
    own_packed = jnp.sum(jnp.where(pull, packed[None, :], 0), axis=1)
    origin = me ^ (own_packed % per_bin // per_half)
    own_spots = ((origin // 2) + 2 * (origin % 2)) * per_own + own_packed // per_bin * per_half + own_packed % per_half
    holder = me ^ (slotted // per_own)
    cot_table = ((holder // 2) + 2 * (holder % 2)) * per_own + slotted % per_own
    tables = (table.astype(jnp.int32), first, last, slot, slotted, own_places, own_spots, cot_table)

    extras = jnp.concatenate(
        [w_beta, gain_attn[:, None], gain_ffn[:, None], jnp.zeros((shard, BLOCK - heads - 2), bf16)], axis=1
    )
    ffn_pack = jnp.concatenate([w_gate, w_up], axis=1)
    full_tokens = lax.all_gather(tokens, "tp", axis=0, tiled=True)
    tables = together(*tables)
    table, first, last, slot, slotted, own_places, own_spots, cot_table = tables
    ffn_pack, slotted = together(ffn_pack, slotted)
    w_in = ring_spread([w_query, w_key, w_value, w_house, extras], "fsdp")
    full_tokens, w_in, ffn_pack, out_shard, down_shard, cotangent, table, first, last, slot, own_places, own_spots = together(
        full_tokens, w_in, ffn_pack, w_out, w_down, cotangent, table, first, last, slot, own_places, own_spots
    )
    ffn_ring = RingGather(ffn_pack, "fsdp", True)
    ffn_ring.hop()
    x_rows = gather_blocks(full_tokens, slotted[:, :per_half], per_half)
    full_out = lax.all_gather(out_shard, "fsdp", axis=0, tiled=True)
    full_down = lax.all_gather(down_shard, "fsdp", axis=0, tiled=True)
    cot_far = across(cotangent)
    pick = (jnp.arange(BLOCK)[None, :] == heads + jnp.arange(8)[:, None]).astype(bf16)
    gain_rows = cols_contract(pick, w_in[:, 4 * width :])
    gain_one, gain_two = gain_rows[0], gain_rows[1]

    all_unit, _ = unit_rows(full_tokens.astype(f32))
    normed = (all_unit * gain_one).astype(bf16)
    proj = jnp.dot(normed, w_in, preferred_element_type=f32).astype(bf16)

    def attend(m):
        prep = attention_prep(proj, table[m], heads)
        return prep, lambda prep: attention_fwd(proj, prep, first[m], table[m], slot, heads)

    preps, saved, hidden_in, unit_two, scale_two, normed_two = [], [], [], [], [], []

    def close(m, own, far):
        hidden_in.append(x_rows[m].astype(f32) + own + far.astype(f32))
        unit, scale = unit_rows(hidden_in[m])
        unit_two.append(unit)
        scale_two.append(scale)
        return (unit * gain_two).astype(bf16)

    prep, run = attend(0)
    prep = list(prep)
    prep[0] = ffn_ring.before(prep[0])
    ffn_ring.hop()
    preps.append(prep)
    saved.append(list(run(prep)))
    saved[0][0], cot_far = together(saved[0][0], cot_far)
    cot_parts = [cotangent, cot_far, beside(cotangent), beside(cot_far)]
    rows = ffn_ring.before(cols_contract(saved[0][0], full_out).astype(bf16))
    ffn_ring.hop()
    attn_own, attn_far = share(rows)
    proj, attn_own = together(proj, attn_own)
    prep, run = attend(1)
    prep = list(prep)
    prep[0], attn_far = ffn_ring.before(prep[0], attn_far)
    while len(ffn_ring.hops) < ffn_ring.count // 2:
        ffn_ring.hop()
    preps.append(prep)
    normed_own = close(0, attn_own, attn_far)
    normed_far = across(normed_own)
    prep[0], normed_own = together(prep[0], normed_own)
    saved.append(list(run(prep)))
    saved[1][0], normed_far, cot_parts[2], cot_parts[3] = together(saved[1][0], normed_far, *cot_parts[2:])
    pair = jnp.concatenate([normed_own, normed_far], axis=0)
    normed_two.append(jnp.concatenate([pair, beside(pair)], axis=0))
    attn_own, attn_far = share(cols_contract(saved[1][0], full_out).astype(bf16))
    attn_own, cot_parts[3], ffn_ring.x = together(attn_own, cot_parts[3], ffn_ring.x)
    ffn_full = ffn_ring.finish()
    cot_rows = list(pick_blocks([cot_parts] * bins, list(cot_table)))

    full_gate, full_up = ffn_full[:, :hidden_width], ffn_full[:, hidden_width : 2 * hidden_width]
    full_gate_up = ffn_full
    hidden, gate_up, back = [], [], []

    def ffn(m, rows, middle):
        gate_pre = jnp.dot(rows, full_gate, preferred_element_type=f32)
        up_part = jnp.dot(rows, full_up, preferred_element_type=f32)
        cot_rows[m] = middle(cot_rows[m])
        hidden.append((jax.nn.silu(gate_pre) * up_part).astype(bf16))
        grad_hidden = jnp.dot(cot_rows[m], full_down, preferred_element_type=f32)
        sigma = jax.nn.sigmoid(gate_pre)
        grad_gate = (grad_hidden * up_part * sigma * (1.0 + gate_pre * (1.0 - sigma))).astype(bf16)
        grad_up = (grad_hidden * jax.nn.silu(gate_pre)).astype(bf16)
        gate_up.append(jnp.concatenate([grad_gate, grad_up], axis=1))

    def ffn_back_rows(m):
        return cols_contract(gate_up[m], full_gate_up).astype(bf16)

    flying = {}

    def middle(rows):
        rows, own, far = together(rows, attn_own, attn_far)
        mine = close(1, own, far)
        flying[0], flying[1] = mine, across(mine)
        return rows

    ffn(0, normed_two[0], middle)
    normed_own, normed_far = flying[0], flying[1]
    rows, normed_own, normed_far = together(ffn_back_rows(0), normed_own, normed_far)
    back_own, back_far = share(rows)
    pair = jnp.concatenate([normed_own, normed_far], axis=0)
    normed_two.append(jnp.concatenate([pair, beside(pair)], axis=0))
    grad_attn = []

    def close_back(m, own, far):
        norm_two_grad = norm_back(own + far.astype(f32), unit_two[m], scale_two[m], gain_two)
        cot_own = cot_rows[m][:half].astype(f32)
        return (cot_own + norm_two_grad).astype(bf16)

    ffn(1, normed_two[1], lambda rows: rows)
    gate_up[1], back_own, back_far = together(gate_up[1], back_own, back_far)
    dh_own = close_back(0, back_own, back_far)
    dh_far = across(dh_own)
    grads_down = sum(rows_contract(cot_rows[m], hidden[m]) for m in streams)
    grads_down, gate_up[1] = together(grads_down.astype(bf16), gate_up[1])
    sum_down = lax.psum_scatter(grads_down, "fsdp", scatter_dimension=0, tiled=True)
    rows, dh_own, dh_far = together(ffn_back_rows(1), dh_own, dh_far)
    back_own, back_far = share(rows)
    back_own, normed_two[0], normed_two[1] = together(back_own, *normed_two)
    pair = jnp.concatenate([dh_own, dh_far], axis=0)
    grad_attn.append(jnp.concatenate([pair, beside(pair)], axis=0))
    grads_in = sum(rows_contract(normed_two[m], gate_up[m]) for m in streams)
    grads_in, back_far = together(grads_in.astype(bf16), back_far)
    sum_in = lax.psum_scatter(grads_in, "fsdp", scatter_dimension=0, tiled=True)
    dh_own = close_back(1, back_own, back_far)
    dh_far = across(dh_own)
    hidden[0], hidden[1], dh_own = together(*hidden, dh_own)
    ffn_parts = [share(cols_contract(hidden[m], full_down).astype(bf16)) for m in streams]
    d_mixed = jnp.dot(grad_attn[0], full_out, preferred_element_type=f32).astype(bf16)
    y_own, y_far = [p[0] for p in ffn_parts], [p[1] for p in ffn_parts]
    d_mixed, y_own[0], y_own[1] = together(d_mixed, *y_own)
    d_proj = attention_bwd(proj, preps[0], saved[0], d_mixed, last[0], table[0], slot, heads, None)
    d_proj, dh_far, y_far[0] = together(d_proj, dh_far, y_far[0])
    pair = jnp.concatenate([dh_own, dh_far], axis=0)
    grad_attn.append(jnp.concatenate([pair, beside(pair)], axis=0))
    d_mixed = jnp.dot(grad_attn[1], full_out, preferred_element_type=f32).astype(bf16)
    finish_y = lambda m: (hidden_in[m] + y_own[m] + y_far[m].astype(f32)).astype(bf16)
    y_rows = [finish_y(0)]
    grad_out = sum(rows_contract(grad_attn[m], saved[m][0]) for m in streams).astype(bf16)
    d_mixed, grad_out, y_rows[0] = together(d_mixed, grad_out, y_rows[0])
    y_across = [across(y_rows[0])]
    d_proj = attention_bwd(proj, preps[1], saved[1], d_mixed, last[1], table[1], slot, heads, d_proj)
    d_proj, sum_down, y_across[0], y_far[1] = together(d_proj, sum_down, y_across[0], y_far[1])
    y_rows.append(finish_y(1))
    y_across.append(across(y_rows[1]))
    attn_grads, d_proj, y_across[1] = together(rows_contract(normed, d_proj).astype(bf16), d_proj, y_across[1])
    y_pair = jnp.concatenate([*y_rows, *y_across], axis=0)
    rows_one, y_other, attn_grads = together(
        cols_contract(d_proj, w_in).astype(bf16), beside(y_pair), attn_grads
    )
    grad_one = lax.psum_scatter(rows_one, "tp", scatter_dimension=0, tiled=True)
    dh_own, out_y = pick_blocks([grad_attn, [*y_rows, *y_across, y_other]], [own_places, own_spots])
    attn_grads, dh_own, out_y = together(attn_grads, dh_own, out_y)
    attn_sum, grad_out = ring_sum([attn_grads, grad_out], "fsdp")
    sum_in, sum_down = sum_in.astype(f32), sum_down.astype(f32)
    grad_one = grad_one.astype(f32)
    unit_one, scale_one = unit_rows(tokens.astype(f32))
    norm_one_grad = norm_back(grad_one, unit_one, scale_one, gain_one)
    out_dx = (dh_own.astype(f32) + norm_one_grad).astype(bf16)
    dots = lambda grads, weights: jnp.sum(grads * weights.astype(f32), axis=1)
    own_one = dots(attn_sum[:, 4 * width : 4 * width + heads], w_beta) + sum(
        dots(attn_sum[:, n * width : (n + 1) * width], weight)
        for n, weight in enumerate((w_query, w_key, w_value, w_house))
    )
    own_two = dots(sum_in, ffn_pack)
    gains = tp_sum(jnp.stack([own_one, own_two])) / jnp.stack([gain_attn, gain_ffn]).astype(f32)
    return (
        out_y,
        out_dx,
        attn_sum[:, :width],
        attn_sum[:, width : 2 * width],
        attn_sum[:, 2 * width : 3 * width],
        attn_sum[:, 3 * width : 4 * width],
        attn_sum[:, 4 * width : 4 * width + heads],
        grad_out,
        sum_in[:, :hidden_width],
        sum_in[:, hidden_width:],
        sum_down,
        gains[0],
        gains[1],
    )


def solution(mesh):
    rows = P(("fsdp", "tp"), None)
    weight = P("fsdp", "tp")
    return jax.shard_map(
        local,
        mesh=mesh,
        in_specs=(rows, rows) + (weight,) * 9 + (P("fsdp"), P("fsdp"), P("fsdp", None, None), P("fsdp", None, None)),
        out_specs=(rows, rows) + (weight,) * 9 + (P("fsdp"), P("fsdp")),
        check_vma=False,
    )
```

```python
import functools

import jax
import jax.numpy as jnp
from jax import lax
from jax.experimental import pallas as pl
from jax.experimental.pallas import tpu as pltpu
from jax.sharding import PartitionSpec as P

BLOCK = 128
epsilon = 1e-06
bf16 = jnp.bfloat16
f32 = jnp.float32


def mm(a, b):
    return lax.dot_general(a, b, (((1,), (0,)), ((), ())), preferred_element_type=f32)


def mm_rt(a, b):
    return lax.dot_general(a, b, (((1,), (1,)), ((), ())), preferred_element_type=f32)


def mm_lt(a, b):
    return lax.dot_general(a, b, (((0,), (0,)), ((), ())), preferred_element_type=f32)


def iotas():
    rows = lax.broadcasted_iota(jnp.int32, (BLOCK, BLOCK), 0)
    cols = lax.broadcasted_iota(jnp.int32, (BLOCK, BLOCK), 1)
    return rows, cols


def lockstep(tasks):
    tasks = list(tasks)
    while tasks:
        tasks = [task for task in tasks if next(task, None) is not None]


def strengths(u, r_col):
    uf = u.astype(f32)
    inv_sq = 1.0 / (jnp.sum(uf * uf, axis=1, keepdims=True) + epsilon)
    beta = 2.0 / (1.0 + jnp.exp(-r_col))
    return beta, inv_sq


def prep_kernel(heads, chunks, table_ref, *refs):
    q_refs, k_refs, u_refs, r_refs = (refs[n * chunks : (n + 1) * chunks] for n in range(4))
    near_ref, q0_ref, kp_ref, inv_ref, t_ref = refs[4 * chunks :]
    rows, cols = iotas()
    strict = rows > cols
    lower = rows >= cols
    diff = rows ^ cols
    eye = jnp.where(rows == cols, 1.0, 0.0).astype(f32)
    eye_b = eye.astype(bf16)
    items = [(c, h) for c in range(chunks) for h in range(heads)]
    state = []
    for c, h in items:
        cs = pl.ds(h * BLOCK, BLOCK)
        q, k, u = q_refs[c][:, cs], k_refs[c][:, cs], u_refs[c][:, cs]
        beta, inv_sq = strengths(u, r_refs[c][:, h : h + 1].astype(f32))
        bp = beta * inv_sq
        big = mm_rt(jnp.concatenate([u, q], axis=0), jnp.concatenate([u, k], axis=0))
        gram = big[:BLOCK, :BLOCK]
        e_s = jnp.where(strict, big[:BLOCK, BLOCK:], 0.0)
        a_s = jnp.where(lower, big[BLOCK:, :BLOCK], 0.0)
        n0 = big[BLOCK:, BLOCK:]
        low = jnp.where(strict, gram * bp, 0.0)
        eu = jnp.concatenate([e_s * bp, u.astype(f32) * bp], axis=1).astype(bf16)
        start = (eye - jnp.where(diff < 2, low, 0.0)).astype(bf16)
        state.append([q, k, u, a_s.astype(bf16), n0, low.astype(bf16), eu, start])
    def invert(st, delay):
        for _ in range(delay):
            yield 1
        size = 2
        while size < BLOCK:
            sel = jnp.where((diff >= size) & (diff < 2 * size), 1.0, 0.0).astype(bf16)
            if size < 16:
                y = mm(st[5] * sel, st[7]).astype(bf16)
                yield 1
                st[7] = st[7] - mm(st[7], y).astype(bf16)
            else:
                groups = range(size, BLOCK, 2 * size)
                odd = lambda x: jnp.concatenate([x[g : g + size] for g in groups], axis=0)
                blank = jnp.zeros((size, BLOCK), bf16)
                y = mm(odd(st[5]) * odd(sel), st[7]).astype(bf16)
                yield 1
                pieces = []
                for n in range(len(groups)):
                    pieces += [blank, y[n * size : (n + 1) * size]]
                rows_odd = odd(st[7])
                fresh = rows_odd - mm(rows_odd, jnp.concatenate(pieces, axis=0)).astype(bf16)
                pieces = []
                for n, g in enumerate(groups):
                    pieces += [st[7][g - size : g], fresh[n * size : (n + 1) * size]]
                st[7] = jnp.concatenate(pieces, axis=0)
            yield 1
            size *= 2

    lockstep(invert(st, n % 2) for n, st in enumerate(state))
    def close(item, st, delay):
        for _ in range(delay):
            yield 1
        c, h = item
        q, k, u, a_b, n0, low, eu, x = st
        rs, cs = pl.ds(c * BLOCK, BLOCK), pl.ds(h * BLOCK, BLOCK)
        t = mm(x, eu).astype(bf16)
        inv_ref[c, h] = x
        t_ref[c, h] = t
        yield 1
        top = mm(a_b, t)
        yield 1
        bot = mm_lt(u, t)
        near_ref[c, h] = n0 - top[:, :BLOCK]
        q0_ref[rs, cs] = (q.astype(f32) - top[:, BLOCK:]).astype(bf16)
        yield 1
        ket = mm_rt(eye_b, k) - bot[:, :BLOCK]
        kp_ref[c, h] = jnp.concatenate([ket, eye - bot[:, BLOCK:]], axis=1).astype(bf16)

    lockstep(close(item, st, 0) for n, (item, st) in enumerate(zip(items, state)))


def fwd_kernel(
    heads, depth, scale, first_ref, table_ref, slot_ref, q0_ref, near_ref, kp_ref, v_ref, o_ref, linv_ref, e_ref, cur_ref, s_ref, m_ref, acc_ref
):
    i = pl.program_id(0)
    first = first_ref[i]
    rows, cols = iotas()
    lower = rows >= cols
    neg = jnp.float32(-1e30)
    for h in range(heads):
        s0 = jnp.where(lower, near_ref[0, h], neg)
        s_ref[0, h] = s0
        m_ref[h] = s0
        cur_ref[0, 0, h] = q0_ref[:, h * BLOCK : (h + 1) * BLOCK]
    for d in range(1, depth):

        @pl.when(i - d >= first)
        def _():
            j = i - d
            for h in range(heads):
                both = mm(cur_ref[0, d - 1, h], kp_ref[j, h])
                s = both[:, :BLOCK]
                s_ref[d, h] = s
                m_ref[h] = jnp.maximum(m_ref[h], s)
                if d + 1 < depth:
                    cur_ref[0, d, h] = both[:, BLOCK:].astype(bf16)

    peaks = []
    for h in range(heads):
        peak = jnp.max(m_ref[h], axis=1, keepdims=True)
        peaks.append(peak)
        e0 = jnp.exp((s_ref[0, h] - peak) * scale)
        m_ref[h] = e0
        eb = e0.astype(bf16)
        e_ref[0, 0, h] = eb
        v = v_ref[pl.ds(pl.multiple_of(table_ref[i] * BLOCK, BLOCK), BLOCK), h * BLOCK : (h + 1) * BLOCK]
        acc_ref[h] = mm(eb, v)
    def weigh(d, carry):
        j = i - d
        at = pl.ds(pl.multiple_of(table_ref[j] * BLOCK, BLOCK), BLOCK)
        for h in range(heads):
            e = jnp.exp((s_ref[d, h] - peaks[h]) * scale)
            m_ref[h] = m_ref[h] + e
            eb = e.astype(bf16)
            e_ref[0, d, h] = eb
            acc_ref[h] = acc_ref[h] + mm(eb, v_ref[at, h * BLOCK : (h + 1) * BLOCK])
        return carry

    lax.fori_loop(1, i - first + 1, weigh, 0)

    for h in range(heads):
        linv = 1.0 / jnp.sum(m_ref[h], axis=1, keepdims=True)
        cs = slice(h * BLOCK, (h + 1) * BLOCK)
        o_ref[:, cs] = (acc_ref[h] * linv).astype(bf16)
        linv_ref[:, cs] = jnp.broadcast_to(linv, (BLOCK, BLOCK))


def bwd_kernel(heads, depth, scale, last_ref, table_ref, slot_ref, *refs):
    (do_ref, o_ref, linv_ref, q_ref, k_ref, v_ref, u_ref, r_ref, kp_ref, inv_ref, t_ref) = refs[:11]
    e_refs = refs[11 : 11 + depth]
    cur_refs = refs[11 + depth : 10 + 2 * depth]
    out_ref, dop_ref, del_ref, g_ref, dv_ref, acc_ref = refs[-6:]
    j = pl.program_id(0)
    last = last_ref[j]
    rows, cols = iotas()
    strict = rows > cols
    lower = rows >= cols
    upper = rows <= cols
    total = dop_ref.shape[0]

    @pl.when(j == 0)
    def _():
        for c in range(total // BLOCK):
            rs = pl.ds(c * BLOCK, BLOCK)
            for h in range(heads):
                cs = slice(h * BLOCK, (h + 1) * BLOCK)
                there = pl.ds(pl.multiple_of(slot_ref[c] * BLOCK, BLOCK), BLOCK)
                dop = do_ref[there, cs].astype(f32) * linv_ref[rs, cs]
                delta = jnp.sum(dop * o_ref[there, cs].astype(f32), axis=1, keepdims=True)
                dop_ref[rs, cs] = dop.astype(bf16)
                del_ref[rs, cs] = jnp.broadcast_to(delta, (BLOCK, BLOCK))
                g_ref[c, h] = jnp.zeros((BLOCK, BLOCK), bf16)

    here = pl.ds(pl.multiple_of(j * BLOCK, BLOCK), BLOCK)
    near = []
    for h in range(heads):
        cs = slice(h * BLOCK, (h + 1) * BLOCK)
        dop = dop_ref[here, cs]
        e = e_refs[0][0, 0, h]
        dp = mm_rt(dop, v_ref[:, cs])
        near.append((e.astype(f32) * (dp - del_ref[here, cs]) * scale).astype(bf16))
        dv_ref[h] = mm_lt(e, dop)
        acc_ref[h] = jnp.zeros((BLOCK, 2 * BLOCK), f32)
    for d in range(1, depth):

        @pl.when(j + d <= last)
        def _():
            i = j + d
            there = pl.ds(pl.multiple_of(i * BLOCK, BLOCK), BLOCK)
            def far(h):
                cs = slice(h * BLOCK, (h + 1) * BLOCK)
                dop = dop_ref[there, cs]
                e = e_refs[d][0, 0, h]
                dp = mm_rt(dop, v_ref[:, cs])
                yield 1
                dv_ref[h] = dv_ref[h] + mm_lt(e, dop)
                yield 1
                ds = (e.astype(f32) * (dp - del_ref[there, cs]) * scale).astype(bf16)
                dsg = jnp.concatenate([ds, g_ref[i, h]], axis=1)
                yield 1
                acc_ref[h] = acc_ref[h] + mm_lt(cur_refs[d - 1][0, 0, h], dsg)
                yield 1
                g_ref[i, h] = mm_rt(dsg, kp_ref[0, h]).astype(bf16)

            lockstep(far(h) for h in range(heads))

    lane = cols
    dr_all = jnp.zeros((BLOCK, BLOCK), f32)
    width = heads * BLOCK
    drs = {}

    def local_part(h):
        cs = slice(h * BLOCK, (h + 1) * BLOCK)
        q, k, u = q_ref[:, cs], k_ref[:, cs], u_ref[:, cs]
        kq = mm_rt(u, jnp.concatenate([k, q], axis=0))
        yield 1
        e_s = jnp.where(strict, kq[:, :BLOCK], 0.0).astype(bf16)
        a_t = jnp.where(upper, kq[:, BLOCK:], 0.0).astype(bf16)
        dn = near[h]
        acc = acc_ref[h]
        bmat = jnp.concatenate([jnp.concatenate([dn, g_ref[j, h]], axis=1), acc.astype(bf16)], axis=0)
        yz = mm(jnp.concatenate([a_t, u], axis=1), bmat).astype(bf16)
        yield 1
        ru = mm_rt(jnp.concatenate([e_s, u], axis=1), bmat)
        beta, inv_sq = strengths(u, r_ref[:, h : h + 1].astype(f32))
        bp = beta * inv_sq
        yield 1
        inv = inv_ref[0, h]
        left = mm_lt(inv, yz) * (-bp)
        yield 1
        right = -mm(inv, (ru * bp).astype(bf16))
        yield 1
        d_s = jnp.where(strict, -mm_rt(left.astype(bf16), t_ref[0, h]), 0.0).astype(bf16)
        d_e = jnp.where(strict, left[:, :BLOCK], 0.0).astype(bf16)
        d_at = jnp.where(upper, right[:, :BLOCK], 0.0).astype(bf16)
        du = left[:, BLOCK:] + right[:, BLOCK:]
        yield 1
        d_a = d_at.astype(f32).T.astype(bf16)
        uk = jnp.concatenate([u, k], axis=0)
        dq_o = g_ref[j, h].astype(f32) + mm(jnp.concatenate([d_a, dn], axis=1), uk)
        out_ref[:, cs] = dq_o.astype(bf16)
        yield 1
        uq = jnp.concatenate([u, q], axis=0)
        dk_o = acc_ref[h][:, :BLOCK].T + mm_lt(jnp.concatenate([d_e, dn], axis=0), uq)
        out_ref[:, width + h * BLOCK : width + (h + 1) * BLOCK] = dk_o.astype(bf16)
        yield 1
        du = du + mm(jnp.concatenate([d_s, d_e], axis=1), uk)
        d_st = d_s.astype(f32).T.astype(bf16)
        du = du + mm(jnp.concatenate([d_st, d_at], axis=1), uq)
        yield 1
        uf = u.astype(f32)
        rad = jnp.sum(uf * du, axis=1, keepdims=True)
        du = du - (inv_sq * rad) * uf
        drs[h] = 0.5 * rad * (1.0 - 0.5 * beta)
        out_ref[:, 2 * width + h * BLOCK : 2 * width + (h + 1) * BLOCK] = dv_ref[h].astype(bf16)
        out_ref[:, 3 * width + h * BLOCK : 3 * width + (h + 1) * BLOCK] = du.astype(bf16)

    lockstep(local_part(h) for h in range(heads))
    for h in range(heads):
        dr_all = jnp.where(lane == h, drs[h], dr_all)
    out_ref[:, 4 * width :] = dr_all.astype(bf16)


def attention_prep(proj, table, heads):
    count = table.shape[0]
    width = heads * BLOCK
    step = 4

    def rows(c, n, col):
        return pl.BlockSpec((BLOCK, n), lambda i, t: (t[i * step + c], col))

    tile = lambda n: pl.BlockSpec((step, heads, BLOCK, n), lambda i, t: (i, 0, 0, 0))
    shape = lambda n, t: jax.ShapeDtypeStruct((count, heads, BLOCK, n), t)
    spec = pltpu.PrefetchScalarGridSpec(
        num_scalar_prefetch=1,
        grid=(count // step,),
        in_specs=[rows(c, width, col) for col in (0, 1, 3) for c in range(step)]
        + [rows(c, BLOCK, 4 * heads) for c in range(step)],
        out_specs=[
            tile(BLOCK),
            pl.BlockSpec((step * BLOCK, width), lambda i, t: (i, 0)),
            tile(2 * BLOCK),
            tile(BLOCK),
            tile(2 * BLOCK),
        ],
    )
    return pl.pallas_call(
        functools.partial(prep_kernel, heads, step),
        grid_spec=spec,
        out_shape=[
            shape(BLOCK, f32),
            jax.ShapeDtypeStruct((count * BLOCK, width), bf16),
            shape(2 * BLOCK, bf16),
            shape(BLOCK, bf16),
            shape(2 * BLOCK, bf16),
        ],
        cost_estimate=pl.CostEstimate(
            flops=count * heads * 45 * BLOCK**3, bytes_accessed=6 * count * BLOCK * width, transcendentals=0
        ),
        name="attn_prep",
    )(table, *([proj] * (4 * step)))


def attention_fwd(proj, prep, first, table, slot, heads):
    near, q0, kp, _, _ = prep
    count = table.shape[0]
    depth = count
    width = heads * BLOCK
    scale = float(BLOCK) ** -0.5
    spec = pltpu.PrefetchScalarGridSpec(
        num_scalar_prefetch=3,
        grid=(count,),
        in_specs=[
            pl.BlockSpec((BLOCK, width), lambda i, f, t, w: (i, 0)),
            pl.BlockSpec((1, heads, BLOCK, BLOCK), lambda i, f, t, w: (i, 0, 0, 0)),
            pl.BlockSpec((count, heads, BLOCK, 2 * BLOCK), lambda i, f, t, w: (0, 0, 0, 0)),
            pl.BlockSpec((proj.shape[0], width), lambda i, f, t, w: (0, 2)),
        ],
        out_specs=[
            pl.BlockSpec((BLOCK, width), lambda i, f, t, w: (w[i], 0)),
            pl.BlockSpec((BLOCK, width), lambda i, f, t, w: (i, 0)),
            pl.BlockSpec((1, depth, heads, BLOCK, BLOCK), lambda i, f, t, w: (i, 0, 0, 0, 0)),
            pl.BlockSpec((1, depth - 1, heads, BLOCK, BLOCK), lambda i, f, t, w: (i, 0, 0, 0, 0)),
        ],
        scratch_shapes=[
            pltpu.VMEM((depth, heads, BLOCK, BLOCK), f32),
            pltpu.VMEM((heads, BLOCK, BLOCK), f32),
            pltpu.VMEM((heads, BLOCK, BLOCK), f32),
        ],
    )
    return pl.pallas_call(
        functools.partial(fwd_kernel, heads, depth, scale),
        grid_spec=spec,
        out_shape=[
            jax.ShapeDtypeStruct((count * BLOCK, width), bf16),
            jax.ShapeDtypeStruct((count * BLOCK, width), f32),
            jax.ShapeDtypeStruct((count, depth, heads, BLOCK, BLOCK), bf16),
            jax.ShapeDtypeStruct((count, depth - 1, heads, BLOCK, BLOCK), bf16),
        ],
        cost_estimate=pl.CostEstimate(
            flops=count * heads * 48 * BLOCK**3, bytes_accessed=6 * count * BLOCK * width, transcendentals=0
        ),
        name="attn_fwd",
    )(first, table, slot, q0, near, kp, proj)


def attention_bwd(proj, prep, saved, d_mixed, last, table, slot, heads, filled):
    _, _, kp, inv, t_all = prep
    mixed, linv, e_all, cur_all = saved
    count = table.shape[0]
    depth = count
    total = count * BLOCK
    width = heads * BLOCK
    scale = float(BLOCK) ** -0.5
    full = lambda: pl.BlockSpec((total, width), lambda j, f, t, w: (0, 0))
    wide = lambda col: pl.BlockSpec((BLOCK, width), lambda j, f, t, w: (t[j], col))
    tile = lambda n: pl.BlockSpec((1, heads, BLOCK, n), lambda j, f, t, w: (j, 0, 0, 0))

    def diagonal(d, slot):
        return pl.BlockSpec(
            (1, 1, heads, BLOCK, BLOCK), lambda j, f, t, w: (jnp.minimum(j + d, count - 1), slot, 0, 0, 0)
        )

    in_specs = [
        full(),
        full(),
        full(),
        wide(0),
        wide(1),
        wide(2),
        wide(3),
        pl.BlockSpec((BLOCK, BLOCK), lambda j, f, t, w: (t[j], 4 * heads)),
        tile(2 * BLOCK),
        tile(BLOCK),
        tile(2 * BLOCK),
    ]
    in_specs += [diagonal(d, d) for d in range(depth)] + [diagonal(d, d - 1) for d in range(1, depth)]
    operands = [last, table, slot, d_mixed, mixed, linv, proj, proj, proj, proj, proj, kp, inv, t_all]
    operands += [e_all] * depth + [cur_all] * (depth - 1)
    aliases = {}
    if filled is not None:
        aliases = {len(operands): 0}
        in_specs.append(pl.BlockSpec(memory_space=pl.ANY))
        operands.append(filled)
    spec = pltpu.PrefetchScalarGridSpec(
        num_scalar_prefetch=3,
        grid=(count,),
        in_specs=in_specs,
        out_specs=pl.BlockSpec((BLOCK, 4 * width + BLOCK), lambda j, f, t, w: (t[j], 0)),
        scratch_shapes=[
            pltpu.VMEM((total, width), bf16),
            pltpu.VMEM((total, width), f32),
            pltpu.VMEM((count, heads, BLOCK, BLOCK), bf16),
            pltpu.VMEM((heads, BLOCK, BLOCK), f32),
            pltpu.VMEM((heads, BLOCK, 2 * BLOCK), f32),
        ],
    )
    return pl.pallas_call(
        functools.partial(bwd_kernel, heads, depth, scale),
        grid_spec=spec,
        out_shape=jax.ShapeDtypeStruct((proj.shape[0], 4 * width + BLOCK), bf16),
        input_output_aliases=aliases,
        cost_estimate=pl.CostEstimate(
            flops=count * heads * 120 * BLOCK**3, bytes_accessed=8 * total * width, transcendentals=0
        ),
        name="attn_bwd",
    )(*operands)


def pick_kernel(bounds, picks, table_ref, *refs):
    total = sum(len(part) for part in bounds)
    parts, outs = refs[:total], refs[total:-3]
    held, load_sem, store_sem = refs[-3:]
    stores = []
    base = 0
    for group, limits in enumerate(bounds):
        for n in range(picks):
            slot = group * picks + n
            at = table_ref[slot]
            for p, (low, high) in enumerate(limits):

                @pl.when((at >= low) & (at < high))
                def _():
                    rows = pl.ds(pl.multiple_of((at - low) * BLOCK, BLOCK), BLOCK)
                    pltpu.make_async_copy(parts[base + p].at[rows, :], held.at[slot], load_sem.at[slot]).start()

        base += len(limits)
    for group in range(len(bounds)):
        for n in range(picks):
            slot = group * picks + n
            rows = pl.ds(n * BLOCK, BLOCK)
            pltpu.make_async_copy(outs[group].at[rows, :], held.at[slot], load_sem.at[slot]).wait()
            stores.append(pltpu.make_async_copy(held.at[slot], outs[group].at[rows, :], store_sem.at[slot]))
            stores[-1].start()
    for store in stores:
        store.wait()


def pick_blocks(groups, table):
    picks = table.shape[0] // len(groups)
    cols = groups[0][0].shape[1]
    dtype = groups[0][0].dtype
    bounds = []
    for parts in groups:
        limits, low = [], 0
        for part in parts:
            limits.append((low, low + part.shape[0] // BLOCK))
            low = limits[-1][1]
        bounds.append(limits)
    flat = [part for parts in groups for part in parts]
    slots = picks * len(groups)
    spec = pltpu.PrefetchScalarGridSpec(
        num_scalar_prefetch=1,
        grid=(1,),
        in_specs=[pl.BlockSpec(memory_space=pl.ANY)] * len(flat),
        out_specs=[pl.BlockSpec(memory_space=pl.ANY)] * len(groups),
        scratch_shapes=[
            pltpu.VMEM((slots, BLOCK, cols), dtype),
            pltpu.SemaphoreType.DMA((slots,)),
            pltpu.SemaphoreType.DMA((slots,)),
        ],
    )
    return pl.pallas_call(
        functools.partial(pick_kernel, bounds, picks),
        grid_spec=spec,
        out_shape=[jax.ShapeDtypeStruct((picks * BLOCK, cols), dtype)] * len(groups),
        cost_estimate=pl.CostEstimate(flops=0, bytes_accessed=4 * slots * BLOCK * cols, transcendentals=0),
        name="pick_blocks",
    )(table, *flat)


def place_kernel(count, rows, spot_ref, *refs):
    pieces, out, bufs, sem_in, sem_out = refs[:count], refs[count], refs[count + 1], refs[count + 2], refs[count + 3]
    loads = [pltpu.make_async_copy(pieces[n], bufs.at[n], sem_in.at[n]) for n in range(count)]
    for load in loads:
        load.start()
    stores = []
    for n in range(count):
        loads[n].wait()
        to = out.at[pl.ds(pl.multiple_of(spot_ref[n] * rows, rows), rows), :]
        stores.append(pltpu.make_async_copy(bufs.at[n], to, sem_out.at[n]))
        stores[n].start()
    for store in stores:
        store.wait()


def place_pieces(pieces, spots, count):
    rows, cols = pieces[0].shape
    held = len(pieces)
    dtype = pieces[0].dtype
    spec = pltpu.PrefetchScalarGridSpec(
        num_scalar_prefetch=1,
        grid=(1,),
        in_specs=[pl.BlockSpec(memory_space=pl.ANY)] * held,
        out_specs=pl.BlockSpec(memory_space=pl.ANY),
        scratch_shapes=[
            pltpu.VMEM((held, rows, cols), dtype),
            pltpu.SemaphoreType.DMA((held,)),
            pltpu.SemaphoreType.DMA((held,)),
        ],
    )
    where = jnp.concatenate([jnp.reshape(spot, (1,)) for spot in spots]).astype(jnp.int32)
    return pl.pallas_call(
        functools.partial(place_kernel, held, rows),
        grid_spec=spec,
        out_shape=jax.ShapeDtypeStruct((count * rows, cols), dtype),
        cost_estimate=pl.CostEstimate(flops=0, bytes_accessed=4 * held * rows * cols, transcendentals=0),
        name="place_pieces",
    )(where, *pieces)


def open_kernel(spot_ref, x_ref, out_ref):
    out_ref[...] = x_ref[...]


def open_buffer(x, spot, count):
    rows, cols = x.shape
    spec = pltpu.PrefetchScalarGridSpec(
        num_scalar_prefetch=1,
        grid=(2,),
        in_specs=[pl.BlockSpec((rows // 2, cols), lambda i, t: (i, 0))],
        out_specs=pl.BlockSpec((rows // 2, cols), lambda i, t: (2 * t[0] + i, 0)),
    )
    return pl.pallas_call(
        open_kernel,
        grid_spec=spec,
        out_shape=jax.ShapeDtypeStruct((count * rows, cols), x.dtype),
        cost_estimate=pl.CostEstimate(flops=0, bytes_accessed=4 * rows * cols, transcendentals=0),
        name="open_buffer",
    )(jnp.reshape(spot, (1,)).astype(jnp.int32), x)


def rows_contract(a, b):
    return lax.dot_general(a, b, (((0,), (0,)), ((), ())), preferred_element_type=f32)


def cols_contract(a, b):
    return lax.dot_general(a, b, (((1,), (1,)), ((), ())), preferred_element_type=f32)


def unit_rows(x):
    scale = lax.rsqrt(jnp.mean(x * x, axis=1, keepdims=True) + epsilon)
    return x * scale, scale


def norm_back(grad_normed, unit, scale, gain):
    grad_unit = grad_normed * gain
    return scale * (grad_unit - unit * jnp.mean(grad_unit * unit, axis=1, keepdims=True))


def ring_order(count):
    return list(range(0, count, 2)) + list(range(1, count, 2))[::-1]


def ring_tables(axis):
    count = lax.axis_size(axis)
    order = ring_order(count)
    right = [(order[p], order[(p + 1) % count]) for p in range(count)]
    left = [(order[p], order[(p - 1) % count]) for p in range(count)]
    me = lax.axis_index(axis)
    spot = jnp.where(me % 2 == 0, me // 2, count - 1 - me // 2)

    def owner(shift):
        at = (spot + shift + count) % count
        return jnp.where(at < count // 2, 2 * at, 2 * (count - 1 - at) + 1)

    return count, right, left, owner


class RingGather:
    def __init__(self, x, axis, whole=False):
        self.axis, self.x, self.whole = axis, x, whole
        self.count, self.right, self.left, self.owner = ring_tables(axis)
        self.moving = (x, x)
        self.hops = []

    def hop(self):
        from_left, from_right = self.moving
        if len(self.hops) == self.count // 2 - 1:
            half = self.x.shape[0] // 2
            from_left, from_right = from_left[:half], from_right[half:]
        self.moving = (
            lax.ppermute(from_left, self.axis, self.right),
            lax.ppermute(from_right, self.axis, self.left),
        )
        self.hops.append(self.moving)

    def before(self, *values):
        held = lax.optimization_barrier((self.moving,) + values)
        self.moving = held[0]
        self.hops[-1] = self.moving
        return held[1] if len(values) == 1 else held[1:]

    def finish(self):
        while len(self.hops) < self.count // 2:
            self.hop()
        rows = self.x.shape[0]
        put = lax.dynamic_update_slice_in_dim
        pieces, spots = [self.x], [self.owner(0)]
        for s, (from_left, from_right) in enumerate(self.hops[:-1], 1):
            pieces += [from_left, from_right]
            spots += [self.owner(-s), self.owner(s)]
        if self.whole:
            out = place_pieces(pieces, spots, self.count)
        else:
            out = open_buffer(self.x, spots[0], self.count)
            for piece, spot in zip(pieces[1:], spots[1:]):
                out = put(out, piece, spot * rows, 0)
        far = self.owner(self.count // 2) * rows
        out = put(out, self.hops[-1][0], far, 0)
        return put(out, self.hops[-1][1], far + rows // 2, 0)


class RingScatter:
    def __init__(self, parts, axis):
        self.axis, self.parts = axis, parts
        self.count, self.right, self.left, self.owner = ring_tables(axis)
        self.rows = parts[0].shape[0] // self.count
        self.top = self.count // 2
        self.done = 0
        half = self.rows // 2
        self.moving = (self.piece(self.top, 0, half), self.piece(-self.top, half, half))

    def piece(self, shift, start=0, size=None):
        size = self.rows if size is None else size
        at = self.owner(shift) * self.rows + start
        return jnp.concatenate([lax.dynamic_slice_in_dim(part, at, size, 0) for part in self.parts], axis=1)

    def hop(self):
        to_right, to_left = self.moving
        if self.done > 0:
            s = self.top - self.done
            a, b = self.piece(s), self.piece(-s)
            if self.done == 1:
                half = self.rows // 2
                to_right = jnp.concatenate([a[:half] + to_right, a[half:]], axis=0)
                to_left = jnp.concatenate([b[:half], b[half:] + to_left], axis=0)
            else:
                to_right, to_left = a + to_right, b + to_left
        self.moving = (lax.ppermute(to_right, self.axis, self.right), lax.ppermute(to_left, self.axis, self.left))
        self.done += 1

    def before(self, *values):
        held = lax.optimization_barrier((self.moving,) + values)
        self.moving = held[0]
        return held[1] if len(values) == 1 else held[1:]

    def finish(self):
        while self.done < self.top:
            self.hop()
        return self.piece(0).astype(f32) + self.moving[0].astype(f32) + self.moving[1].astype(f32)


def ring_kernel(axis, count, rows, widths, *refs):
    held = len(widths)
    parts, outs = refs[:held], refs[held : 2 * held]
    own_buf, send_buf, recv_buf, load_sem, send_sem, recv_sem = refs[2 * held :]
    me = lax.axis_index(axis)
    odd = me % 2
    spot = (1 - odd) * (me // 2) + odd * (count - 1 - me // 2)

    def owner(shift):
        at = (spot + shift + count) % count
        upper = at // (count // 2)
        return (1 - upper) * (2 * at) + upper * (2 * (count - 1 - at) + 1)

    top = count // 2
    cut = rows // 32 * 16
    ways = ((1, owner(1)), (-1, owner(-1)))
    barrier = pltpu.get_barrier_semaphore()
    for _, peer in ways:
        pl.semaphore_signal(barrier, inc=1, device_id={axis: peer}, device_id_type=pl.DeviceIdType.MESH)

    def load(shift, slot):
        copies = []
        at = pl.multiple_of(owner(shift) * rows, rows)
        col = 0
        for n, width in enumerate(widths):
            copies.append(
                pltpu.make_async_copy(
                    parts[n].at[pl.ds(at, rows), :],
                    own_buf.at[slot, :, pl.ds(col, width)],
                    load_sem.at[slot, n],
                )
            )
            col += width
        for copy in copies:
            copy.start()
        return copies

    slots = {top: 0, 0: 2 * top - 1}
    for s in range(1, top):
        slots[s], slots[-s] = 2 * s - 1, 2 * s
    loads = {}
    for shift in [top] + [t * s for s in range(top - 1, 0, -1) for t in (1, -1)] + [0]:
        loads[shift] = load(shift, slots[shift])
    for copy in loads[top]:
        copy.wait()
    pl.semaphore_wait(barrier, 2)
    halves = ((0, cut), (cut, rows - cut))
    sent = []

    def push(way, hop, part, src):
        start, size = halves[part]
        copy = pltpu.make_async_remote_copy(
            src_ref=src,
            dst_ref=recv_buf.at[way, hop, pl.ds(start, size), :],
            send_sem=send_sem.at[way, hop, part],
            recv_sem=recv_sem.at[way, hop, part],
            device_id={axis: ways[way][1]},
            device_id_type=pl.DeviceIdType.MESH,
        )
        copy.start()
        sent.append(copy)
        return copy

    flying = {}
    for way in range(2):
        start, size = halves[way]
        flying[way, way] = push(way, 0, way, own_buf.at[slots[top], pl.ds(start, size), :])
    for hop in range(1, top):
        shift = top - hop
        order = [(way, 1 - way) for way in range(2)] + [(way, way) for way in range(2)]
        for way, part in order:
            sign = ways[way][0]
            start, size = halves[part]
            slot = slots[sign * shift]
            if part == 1 - way:
                for copy in loads[sign * shift]:
                    copy.wait()
            area = pl.ds(start, size)
            if hop == 1 and part == 1 - way:
                flying[way, part] = push(way, hop, part, own_buf.at[slot, area, :])
                continue
            flying[way, part].wait_recv()
            total = own_buf[slot, area, :].astype(f32) + recv_buf[way, hop - 1, area, :].astype(f32)
            send_buf[way, hop - 1, area, :] = total.astype(bf16)
            flying[way, part] = push(way, hop, part, send_buf.at[way, hop - 1, area, :])
    for copy in loads[0]:
        copy.wait()
    for part in range(2):
        start, size = halves[part]
        area = pl.ds(start, size)
        for way in range(2):
            flying[way, part].wait_recv()
        col = 0
        for n, width in enumerate(widths):
            cols = pl.ds(col, width)
            outs[n][area, :] = (
                own_buf[slots[0], area, cols].astype(f32)
                + recv_buf[0, top - 1, area, cols].astype(f32)
                + recv_buf[1, top - 1, area, cols].astype(f32)
            )
            col += width
    for copy in sent:
        copy.wait_send()


def spread_kernel(axis, count, rows, widths, *refs):
    held = len(widths)
    parts, out = refs[:held], refs[held]
    own_buf, left_buf, right_buf, load_sem, store_sem, send_sem, recv_sem = refs[held + 1 :]
    me = lax.axis_index(axis)
    odd = me % 2
    spot = (1 - odd) * (me // 2) + odd * (count - 1 - me // 2)

    def owner(shift):
        at = (spot + shift + count) % count
        upper = at // (count // 2)
        return (1 - upper) * (2 * at) + upper * (2 * (count - 1 - at) + 1)

    top = count // 2
    cut = rows // 32 * 16
    halves = ((0, cut), (cut, rows - cut))
    peers = (owner(1), owner(-1))
    barrier = pltpu.get_barrier_semaphore()
    for peer in peers:
        pl.semaphore_signal(barrier, inc=1, device_id={axis: peer}, device_id_type=pl.DeviceIdType.MESH)
    loads, col = [], 0
    for n, width in enumerate(widths):
        loads.append(pltpu.make_async_copy(parts[n], own_buf.at[:, pl.ds(col, width)], load_sem.at[n]))
        loads[-1].start()
        col += width
    for load in loads:
        load.wait()
    pl.semaphore_wait(barrier, 2)
    bufs = (left_buf, right_buf)
    flying, sent, stores = {}, [], []

    def push(way, hop, part, src):
        start, size = halves[part]
        copy = pltpu.make_async_remote_copy(
            src_ref=src,
            dst_ref=bufs[way].at[hop, pl.ds(start, size), :],
            send_sem=send_sem.at[way, hop, part],
            recv_sem=recv_sem.at[way, hop, part],
            device_id={axis: peers[way]},
            device_id_type=pl.DeviceIdType.MESH,
        )
        copy.start()
        sent.append(copy)
        flying[way, hop, part] = copy

    def store(src, shift, part, sem):
        start, size = halves[part]
        at = pl.multiple_of(owner(shift) * rows + start, 16)
        stores.append(pltpu.make_async_copy(src, out.at[pl.ds(at, size), :], sem))
        stores[-1].start()

    for part in range(2):
        for way in range(2):
            start, size = halves[part]
            push(way, 0, part, own_buf.at[pl.ds(start, size), :])
    for part in range(2):
        start, size = halves[part]
        store(own_buf.at[pl.ds(start, size), :], 0, part, store_sem.at[2, 0, part])
    for hop in range(top):
        for part in range(2):
            for way in range(2):
                if hop == top - 1 and part != way:
                    continue
                start, size = halves[part]
                here = bufs[way].at[hop, pl.ds(start, size), :]
                flying[way, hop, part].wait_recv()
                if hop + 1 < top - 1 or (hop + 1 == top - 1 and part == way):
                    push(way, hop + 1, part, here)
                store(here, -(hop + 1) if way == 0 else hop + 1, part, store_sem.at[way, hop, part])
    for copy in sent:
        copy.wait_send()
    for copy in stores:
        copy.wait()


def ring_spread(parts, axis):
    count = lax.axis_size(axis)
    rows = parts[0].shape[0]
    widths = [part.shape[1] for part in parts]
    cols = sum(widths)
    top = count // 2
    return pl.pallas_call(
        functools.partial(spread_kernel, axis, count, rows, widths),
        in_specs=[pl.BlockSpec(memory_space=pl.ANY)] * len(parts),
        out_specs=pl.BlockSpec(memory_space=pl.ANY),
        out_shape=jax.ShapeDtypeStruct((count * rows, cols), bf16),
        scratch_shapes=[
            pltpu.VMEM((rows, cols), bf16),
            pltpu.VMEM((top, rows, cols), bf16),
            pltpu.VMEM((top, rows, cols), bf16),
            pltpu.SemaphoreType.DMA((len(parts),)),
            pltpu.SemaphoreType.DMA((3, top, 2)),
            pltpu.SemaphoreType.DMA((2, top, 2)),
            pltpu.SemaphoreType.DMA((2, top, 2)),
        ],
        compiler_params=pltpu.CompilerParams(collective_id=1, has_side_effects=True),
        cost_estimate=pl.CostEstimate(flops=0, bytes_accessed=4 * count * rows * cols, transcendentals=0),
        name="ring_spread",
    )(*parts)


def ring_sum(parts, axis):
    count = lax.axis_size(axis)
    rows = parts[0].shape[0] // count
    widths = [part.shape[1] for part in parts]
    cols = sum(widths)
    top = count // 2
    sent = (2 * top - 1) * rows * cols * 2
    return pl.pallas_call(
        functools.partial(ring_kernel, axis, count, rows, widths),
        in_specs=[pl.BlockSpec(memory_space=pl.ANY)] * len(parts),
        out_specs=[pl.BlockSpec(memory_space=pltpu.VMEM)] * len(parts),
        out_shape=[jax.ShapeDtypeStruct((rows, width), f32) for width in widths],
        scratch_shapes=[
            pltpu.VMEM((count, rows, cols), bf16),
            pltpu.VMEM((2, top - 1, rows, cols), bf16),
            pltpu.VMEM((2, top, rows, cols), bf16),
            pltpu.SemaphoreType.DMA((count, len(parts))),
            pltpu.SemaphoreType.DMA((2, top, 2)),
            pltpu.SemaphoreType.DMA((2, top, 2)),
        ],
        compiler_params=pltpu.CompilerParams(collective_id=0, has_side_effects=True),
        cost_estimate=pl.CostEstimate(flops=0, bytes_accessed=4 * count * rows * cols, transcendentals=0),
        name="ring_sum",
    )(*parts)


def tp_sum(x):
    count = lax.axis_size("tp")
    me = lax.axis_index("tp")
    pieces = [x] + [lax.ppermute(x, "tp", [(i, (i + s) % count) for i in range(count)]) for s in range(1, count)]
    total = jnp.zeros_like(x)
    for r in range(count):
        chosen = pieces[0]
        for step in range(1, count):
            chosen = jnp.where((me - step) % count == r, pieces[step], chosen)
        total = total + chosen
    return total


SLOTS = (0, 2, 1, 3)


def across(x):
    return lax.ppermute(x, "tp", [(i, i ^ 2) for i in range(4)])


def beside(x):
    return lax.ppermute(x, "tp", [(i, i ^ 1) for i in range(4)])


def share(rows):
    size = rows.shape[0] // 4
    other = beside(rows[2 * size :])
    pair = rows[: 2 * size].astype(f32) + other.astype(f32)
    return pair[:size], across(pair[size:].astype(bf16))


def spread(x):
    pair = jnp.concatenate([x, across(x)], axis=0)
    return jnp.concatenate([pair, beside(pair)], axis=0)


def together(*values):
    return lax.optimization_barrier(values)


def local(
    tokens,
    cotangent,
    w_query,
    w_key,
    w_value,
    w_house,
    w_beta,
    w_out,
    w_gate,
    w_up,
    w_down,
    gain_attn,
    gain_ffn,
    pack_index,
    seq_start,
):
    packing, begins = pack_index[0], seq_start[0]
    bins, bin_rows = packing.shape
    per_bin = bin_rows // BLOCK
    streams = range(bins)
    width = w_query.shape[1]
    heads = w_beta.shape[1]
    hidden_width = w_gate.shape[1]
    shard = w_query.shape[0]
    ranks = 4
    assert lax.axis_size("tp") == ranks
    half = bin_rows // ranks
    per_half = half // BLOCK
    me = lax.axis_index("tp")

    given = packing[:, ::BLOCK] // BLOCK
    per_own = bins * per_half
    table = given
    first = begins[:, ::BLOCK] // BLOCK
    spots = jnp.arange(per_bin, dtype=jnp.int32)
    last = jnp.max(jnp.where(first[:, :, None] == first[:, None, :], spots[None, None, :], 0), axis=2)
    away = me ^ (spots // per_half)
    slot = ((away // 2) + 2 * (away % 2)) * per_half + spots % per_half
    places = jnp.arange(bins, dtype=jnp.int32)[:, None] * per_bin + slot[None, :]
    blocks = jnp.arange(bins * per_bin, dtype=jnp.int32)
    inverse = jnp.sum(jnp.where(given.reshape(-1)[:, None] == blocks[None, :], places.reshape(-1)[:, None], 0), axis=0)
    slotted = jnp.sum(jnp.where(slot[None, :, None] == spots[None, None, :], given[:, :, None], 0), axis=1)
    packed = jnp.sum(jnp.where(given.reshape(-1)[:, None] == blocks[None, :], blocks[:, None], 0), axis=0)
    mine = (blocks // per_own == me) & (blocks >= 0)
    pull = jnp.arange(per_own, dtype=jnp.int32)[:, None] == jnp.where(mine, blocks % per_own, -1)[None, :]
    own_places = jnp.sum(jnp.where(pull, inverse[None, :], 0), axis=1)
    own_packed = jnp.sum(jnp.where(pull, packed[None, :], 0), axis=1)
    origin = me ^ (own_packed % per_bin // per_half)
    own_spots = ((origin // 2) + 2 * (origin % 2)) * per_own + own_packed // per_bin * per_half + own_packed % per_half
    holder = me ^ (slotted // per_own)
    cot_table = ((holder // 2) + 2 * (holder % 2)) * per_own + slotted % per_own
    x_table = slotted[:, :per_half].reshape(-1)
    end_table = jnp.concatenate([own_places, own_spots]).astype(jnp.int32)
    tables = (table.astype(jnp.int32), first, last, slot, x_table, end_table, cot_table.reshape(-1))

    extras = jnp.concatenate(
        [w_beta, gain_attn[:, None], gain_ffn[:, None], jnp.zeros((shard, BLOCK - heads - 2), bf16)], axis=1
    )
    ffn_pack = jnp.concatenate([w_gate, w_up], axis=1)
    full_tokens = lax.all_gather(tokens, "tp", axis=0, tiled=True)
    tables = together(*tables)
    table, first, last, slot, x_table, end_table, cot_table = tables
    w_in = ring_spread([w_query, w_key, w_value, w_house, extras], "fsdp")
    full_tokens, w_in, ffn_pack, out_shard, down_shard, cotangent, *tables = together(
        full_tokens, w_in, ffn_pack, w_out, w_down, cotangent, *tables
    )
    table, first, last, slot, x_table, end_table, cot_table = tables
    ffn_ring = RingGather(ffn_pack, "fsdp", True)
    ffn_ring.hop()
    x_rows = pick_blocks([[full_tokens]] * bins, x_table)
    full_out = lax.all_gather(out_shard, "fsdp", axis=0, tiled=True)
    full_down = lax.all_gather(down_shard, "fsdp", axis=0, tiled=True)
    cot_far = across(cotangent)
    pick = (jnp.arange(BLOCK)[None, :] == heads + jnp.arange(8)[:, None]).astype(bf16)
    gain_rows = cols_contract(pick, w_in[:, 4 * width :])
    gain_one, gain_two = gain_rows[0], gain_rows[1]

    all_unit, _ = unit_rows(full_tokens.astype(f32))
    normed = (all_unit * gain_one).astype(bf16)
    proj = jnp.dot(normed, w_in, preferred_element_type=f32).astype(bf16)

    def attend(m):
        prep = attention_prep(proj, table[m], heads)
        return prep, lambda prep: attention_fwd(proj, prep, first[m], table[m], slot, heads)

    preps, saved, hidden_in, unit_two, scale_two, normed_two = [], [], [], [], [], []

    def close(m, own, far):
        hidden_in.append(x_rows[m].astype(f32) + own + far.astype(f32))
        unit, scale = unit_rows(hidden_in[m])
        unit_two.append(unit)
        scale_two.append(scale)
        return (unit * gain_two).astype(bf16)

    prep, run = attend(0)
    prep = list(prep)
    prep[0] = ffn_ring.before(prep[0])
    ffn_ring.hop()
    preps.append(prep)
    saved.append(list(run(prep)))
    saved[0][0], cot_far = together(saved[0][0], cot_far)
    cot_parts = [cotangent, cot_far, beside(cotangent), beside(cot_far)]
    rows = ffn_ring.before(cols_contract(saved[0][0], full_out).astype(bf16))
    ffn_ring.hop()
    attn_own, attn_far = share(rows)
    proj, attn_own = together(proj, attn_own)
    prep, run = attend(1)
    prep = list(prep)
    prep[0], attn_far = ffn_ring.before(prep[0], attn_far)
    while len(ffn_ring.hops) < ffn_ring.count // 2:
        ffn_ring.hop()
    preps.append(prep)
    normed_own = close(0, attn_own, attn_far)
    normed_far = across(normed_own)
    prep[0], normed_own = together(prep[0], normed_own)
    saved.append(list(run(prep)))
    saved[1][0], normed_far, cot_parts[2], cot_parts[3] = ffn_ring.before(saved[1][0], normed_far, *cot_parts[2:])
    pair = jnp.concatenate([normed_own, normed_far], axis=0)
    normed_two.append(jnp.concatenate([pair, beside(pair)], axis=0))
    attn_own, attn_far = share(cols_contract(saved[1][0], full_out).astype(bf16))
    attn_own, cot_parts[3], ffn_ring.x = together(attn_own, cot_parts[3], ffn_ring.x)
    ffn_full = ffn_ring.finish()
    cot_rows = list(pick_blocks([cot_parts] * bins, cot_table))

    full_gate, full_up = ffn_full[:, :hidden_width], ffn_full[:, hidden_width : 2 * hidden_width]
    full_gate_up = ffn_full
    hidden, gate_up, back = [], [], []

    def ffn(m, rows, middle):
        gate_pre = jnp.dot(rows, full_gate, preferred_element_type=f32)
        up_part = jnp.dot(rows, full_up, preferred_element_type=f32)
        cot_rows[m] = middle(cot_rows[m])
        hidden.append((jax.nn.silu(gate_pre) * up_part).astype(bf16))
        grad_hidden = jnp.dot(cot_rows[m], full_down, preferred_element_type=f32)
        sigma = jax.nn.sigmoid(gate_pre)
        grad_gate = (grad_hidden * up_part * sigma * (1.0 + gate_pre * (1.0 - sigma))).astype(bf16)
        grad_up = (grad_hidden * jax.nn.silu(gate_pre)).astype(bf16)
        gate_up.append(jnp.concatenate([grad_gate, grad_up], axis=1))

    def ffn_back_rows(m):
        return cols_contract(gate_up[m], full_gate_up).astype(bf16)

    flying = {}

    def middle(rows):
        rows, own, far = together(rows, attn_own, attn_far)
        mine = close(1, own, far)
        flying[0], flying[1] = mine, across(mine)
        return rows

    ffn(0, normed_two[0], middle)
    normed_own, normed_far = flying[0], flying[1]
    rows, normed_own, normed_far = together(ffn_back_rows(0), normed_own, normed_far)
    back_own, back_far = share(rows)
    pair = jnp.concatenate([normed_own, normed_far], axis=0)
    normed_two.append(jnp.concatenate([pair, beside(pair)], axis=0))
    grad_attn = []

    def close_back(m, own, far):
        norm_two_grad = norm_back(own + far.astype(f32), unit_two[m], scale_two[m], gain_two)
        cot_own = cot_rows[m][:half].astype(f32)
        return (cot_own + norm_two_grad).astype(bf16)

    ffn(1, normed_two[1], lambda rows: rows)
    gate_up[1], hidden[1], back_own, back_far = together(gate_up[1], hidden[1], back_own, back_far)
    dh_own = close_back(0, back_own, back_far)
    hidden[1], dh_own = together(hidden[1], dh_own)
    dh_far = across(dh_own)
    grads_down = sum(rows_contract(cot_rows[m], hidden[m]) for m in streams)
    grads_down, gate_up[1] = together(grads_down.astype(bf16), gate_up[1])
    sum_down = lax.psum_scatter(grads_down, "fsdp", scatter_dimension=0, tiled=True)
    rows, dh_own = together(ffn_back_rows(1), dh_own)
    back_own, back_far = share(rows)
    back_own, normed_two[0], normed_two[1] = together(back_own, *normed_two)
    grads_in = sum(rows_contract(normed_two[m], gate_up[m]) for m in streams)
    grads_in, back_far, dh_far = together(grads_in.astype(bf16), back_far, dh_far)
    pair = jnp.concatenate([dh_own, dh_far], axis=0)
    grad_attn.append(jnp.concatenate([pair, beside(pair)], axis=0))
    sum_in = lax.psum_scatter(grads_in, "fsdp", scatter_dimension=0, tiled=True)
    dh_own = close_back(1, back_own, back_far)
    dh_far = across(dh_own)
    hidden[0], hidden[1], dh_own = together(*hidden, dh_own)
    ffn_parts = [share(cols_contract(hidden[m], full_down).astype(bf16)) for m in streams]
    d_mixed = jnp.dot(grad_attn[0], full_out, preferred_element_type=f32).astype(bf16)
    y_own, y_far = [p[0] for p in ffn_parts], [p[1] for p in ffn_parts]
    d_mixed, y_own[0], y_own[1] = together(d_mixed, *y_own)
    d_proj = attention_bwd(proj, preps[0], saved[0], d_mixed, last[0], table[0], slot, heads, None)
    d_proj, dh_far, y_far[0] = together(d_proj, dh_far, y_far[0])
    pair = jnp.concatenate([dh_own, dh_far], axis=0)
    grad_attn.append(jnp.concatenate([pair, beside(pair)], axis=0))
    d_mixed = jnp.dot(grad_attn[1], full_out, preferred_element_type=f32).astype(bf16)
    finish_y = lambda m: (hidden_in[m] + y_own[m] + y_far[m].astype(f32)).astype(bf16)
    y_rows = [finish_y(0)]
    grad_out = sum(rows_contract(grad_attn[m], saved[m][0]) for m in streams).astype(bf16)
    d_mixed, grad_out, y_rows[0] = together(d_mixed, grad_out, y_rows[0])
    y_across = [across(y_rows[0])]
    d_proj = attention_bwd(proj, preps[1], saved[1], d_mixed, last[1], table[1], slot, heads, d_proj)
    d_proj, sum_down, y_across[0], y_far[1] = together(d_proj, sum_down, y_across[0], y_far[1])
    y_rows.append(finish_y(1))
    y_across.append(across(y_rows[1]))
    attn_grads, d_proj, y_across[1] = together(rows_contract(normed, d_proj).astype(bf16), d_proj, y_across[1])
    y_other = [beside(part) for part in (*y_rows, *y_across)]
    rows_one, attn_grads, *y_other = together(cols_contract(d_proj, w_in).astype(bf16), attn_grads, *y_other)
    grad_one = lax.psum_scatter(rows_one, "tp", scatter_dimension=0, tiled=True)
    dh_own, out_y = pick_blocks([grad_attn, [*y_rows, *y_across, *y_other]], end_table)
    attn_grads, dh_own, out_y = together(attn_grads, dh_own, out_y)
    attn_sum, grad_out = ring_sum([attn_grads, grad_out], "fsdp")
    sum_in, sum_down = sum_in.astype(f32), sum_down.astype(f32)
    grad_one = grad_one.astype(f32)
    unit_one, scale_one = unit_rows(tokens.astype(f32))
    norm_one_grad = norm_back(grad_one, unit_one, scale_one, gain_one)
    out_dx = (dh_own.astype(f32) + norm_one_grad).astype(bf16)
    dots = lambda grads, weights: jnp.sum(grads * weights.astype(f32), axis=1)
    own_one = dots(attn_sum[:, 4 * width : 4 * width + heads], w_beta) + sum(
        dots(attn_sum[:, n * width : (n + 1) * width], weight)
        for n, weight in enumerate((w_query, w_key, w_value, w_house))
    )
    own_two = dots(sum_in, ffn_pack)
    gains = tp_sum(jnp.stack([own_one, own_two])) / jnp.stack([gain_attn, gain_ffn]).astype(f32)
    return (
        out_y,
        out_dx,
        attn_sum[:, :width],
        attn_sum[:, width : 2 * width],
        attn_sum[:, 2 * width : 3 * width],
        attn_sum[:, 3 * width : 4 * width],
        attn_sum[:, 4 * width : 4 * width + heads],
        grad_out,
        sum_in[:, :hidden_width],
        sum_in[:, hidden_width:],
        sum_down,
        gains[0],
        gains[1],
    )


def solution(mesh):
    rows = P(("fsdp", "tp"), None)
    weight = P("fsdp", "tp")
    return jax.shard_map(
        local,
        mesh=mesh,
        in_specs=(rows, rows) + (weight,) * 9 + (P("fsdp"), P("fsdp"), P("fsdp", None, None), P("fsdp", None, None)),
        out_specs=(rows, rows) + (weight,) * 9 + (P("fsdp"), P("fsdp")),
        check_vma=False,
    )
```

```python
import functools

import jax
import jax.numpy as jnp
from jax import lax
from jax.experimental import pallas as pl
from jax.experimental.pallas import tpu as pltpu
from jax.sharding import PartitionSpec as P

BLOCK = 128
epsilon = 1e-06
bf16 = jnp.bfloat16
f32 = jnp.float32


def mm(a, b):
    return lax.dot_general(a, b, (((1,), (0,)), ((), ())), preferred_element_type=f32)


def mm_rt(a, b):
    return lax.dot_general(a, b, (((1,), (1,)), ((), ())), preferred_element_type=f32)


def mm_lt(a, b):
    return lax.dot_general(a, b, (((0,), (0,)), ((), ())), preferred_element_type=f32)


def iotas():
    rows = lax.broadcasted_iota(jnp.int32, (BLOCK, BLOCK), 0)
    cols = lax.broadcasted_iota(jnp.int32, (BLOCK, BLOCK), 1)
    return rows, cols


def lockstep(tasks):
    tasks = list(tasks)
    while tasks:
        tasks = [task for task in tasks if next(task, None) is not None]


def strengths(u, r_col):
    uf = u.astype(f32)
    inv_sq = 1.0 / (jnp.sum(uf * uf, axis=1, keepdims=True) + epsilon)
    beta = 2.0 / (1.0 + jnp.exp(-r_col))
    return beta, inv_sq


def prep_kernel(heads, chunks, table_ref, *refs):
    q_refs, k_refs, u_refs, r_refs = (refs[n * chunks : (n + 1) * chunks] for n in range(4))
    near_ref, q0_ref, kp_ref, inv_ref, t_ref = refs[4 * chunks :]
    rows, cols = iotas()
    strict = rows > cols
    lower = rows >= cols
    diff = rows ^ cols
    eye = jnp.where(rows == cols, 1.0, 0.0).astype(f32)
    eye_b = eye.astype(bf16)
    items = [(c, h) for c in range(chunks) for h in range(heads)]
    state = []
    for c, h in items:
        cs = pl.ds(h * BLOCK, BLOCK)
        q, k, u = q_refs[c][:, cs], k_refs[c][:, cs], u_refs[c][:, cs]
        beta, inv_sq = strengths(u, r_refs[c][:, h : h + 1].astype(f32))
        bp = beta * inv_sq
        big = mm_rt(jnp.concatenate([u, q], axis=0), jnp.concatenate([u, k], axis=0))
        gram = big[:BLOCK, :BLOCK]
        e_s = jnp.where(strict, big[:BLOCK, BLOCK:], 0.0)
        a_s = jnp.where(lower, big[BLOCK:, :BLOCK], 0.0)
        n0 = big[BLOCK:, BLOCK:]
        low = jnp.where(strict, gram * bp, 0.0)
        eu = jnp.concatenate([e_s * bp, u.astype(f32) * bp], axis=1).astype(bf16)
        start = (eye - jnp.where(diff < 2, low, 0.0)).astype(bf16)
        state.append([q, k, u, a_s.astype(bf16), n0, low.astype(bf16), eu, start])
    def invert(st, delay):
        for _ in range(delay):
            yield 1
        size = 2
        while size < BLOCK:
            sel = jnp.where((diff >= size) & (diff < 2 * size), 1.0, 0.0).astype(bf16)
            if size < 16:
                y = mm(st[5] * sel, st[7]).astype(bf16)
                yield 1
                st[7] = st[7] - mm(st[7], y).astype(bf16)
            else:
                groups = range(size, BLOCK, 2 * size)
                odd = lambda x: jnp.concatenate([x[g : g + size] for g in groups], axis=0)
                blank = jnp.zeros((size, BLOCK), bf16)
                y = mm(odd(st[5]) * odd(sel), st[7]).astype(bf16)
                yield 1
                pieces = []
                for n in range(len(groups)):
                    pieces += [blank, y[n * size : (n + 1) * size]]
                rows_odd = odd(st[7])
                fresh = rows_odd - mm(rows_odd, jnp.concatenate(pieces, axis=0)).astype(bf16)
                pieces = []
                for n, g in enumerate(groups):
                    pieces += [st[7][g - size : g], fresh[n * size : (n + 1) * size]]
                st[7] = jnp.concatenate(pieces, axis=0)
            yield 1
            size *= 2

    lockstep(invert(st, n % 2) for n, st in enumerate(state))
    def close(item, st, delay):
        for _ in range(delay):
            yield 1
        c, h = item
        q, k, u, a_b, n0, low, eu, x = st
        rs, cs = pl.ds(c * BLOCK, BLOCK), pl.ds(h * BLOCK, BLOCK)
        t = mm(x, eu).astype(bf16)
        inv_ref[c, h] = x
        t_ref[c, h] = t
        yield 1
        top = mm(a_b, t)
        yield 1
        bot = mm_lt(u, t)
        near_ref[c, h] = n0 - top[:, :BLOCK]
        q0_ref[rs, cs] = (q.astype(f32) - top[:, BLOCK:]).astype(bf16)
        yield 1
        ket = mm_rt(eye_b, k) - bot[:, :BLOCK]
        kp_ref[c, h] = jnp.concatenate([ket, eye - bot[:, BLOCK:]], axis=1).astype(bf16)

    lockstep(close(item, st, 0) for n, (item, st) in enumerate(zip(items, state)))


def fwd_kernel(
    heads, depth, scale, first_ref, table_ref, slot_ref, q0_ref, near_ref, kp_ref, v_ref, o_ref, linv_ref, e_ref, cur_ref, s_ref, m_ref, acc_ref
):
    i = pl.program_id(0)
    first = first_ref[i]
    rows, cols = iotas()
    lower = rows >= cols
    neg = jnp.float32(-1e30)
    for h in range(heads):
        s0 = jnp.where(lower, near_ref[0, h], neg)
        s_ref[0, h] = s0
        m_ref[h] = s0
        cur_ref[0, 0, h] = q0_ref[:, h * BLOCK : (h + 1) * BLOCK]
    for d in range(1, depth):

        @pl.when(i - d >= first)
        def _():
            j = i - d
            for h in range(heads):
                both = mm(cur_ref[0, d - 1, h], kp_ref[j, h])
                s = both[:, :BLOCK]
                s_ref[d, h] = s
                m_ref[h] = jnp.maximum(m_ref[h], s)
                if d + 1 < depth:
                    cur_ref[0, d, h] = both[:, BLOCK:].astype(bf16)

    peaks = []
    for h in range(heads):
        peak = jnp.max(m_ref[h], axis=1, keepdims=True)
        peaks.append(peak)
        e0 = jnp.exp((s_ref[0, h] - peak) * scale)
        m_ref[h] = e0
        eb = e0.astype(bf16)
        e_ref[0, 0, h] = eb
        v = v_ref[pl.ds(pl.multiple_of(table_ref[i] * BLOCK, BLOCK), BLOCK), h * BLOCK : (h + 1) * BLOCK]
        acc_ref[h] = mm(eb, v)
    def weigh(d, carry):
        j = i - d
        at = pl.ds(pl.multiple_of(table_ref[j] * BLOCK, BLOCK), BLOCK)
        for h in range(heads):
            e = jnp.exp((s_ref[d, h] - peaks[h]) * scale)
            m_ref[h] = m_ref[h] + e
            eb = e.astype(bf16)
            e_ref[0, d, h] = eb
            acc_ref[h] = acc_ref[h] + mm(eb, v_ref[at, h * BLOCK : (h + 1) * BLOCK])
        return carry

    lax.fori_loop(1, i - first + 1, weigh, 0)

    for h in range(heads):
        linv = 1.0 / jnp.sum(m_ref[h], axis=1, keepdims=True)
        cs = slice(h * BLOCK, (h + 1) * BLOCK)
        o_ref[:, cs] = (acc_ref[h] * linv).astype(bf16)
        linv_ref[:, cs] = jnp.broadcast_to(linv, (BLOCK, BLOCK))


def bwd_kernel(heads, depth, scale, last_ref, table_ref, slot_ref, *refs):
    (do_ref, o_ref, linv_ref, q_ref, k_ref, v_ref, u_ref, r_ref, kp_ref, inv_ref, t_ref) = refs[:11]
    e_refs = refs[11 : 11 + depth]
    cur_refs = refs[11 + depth : 10 + 2 * depth]
    out_ref, dop_ref, del_ref, g_ref, dv_ref, acc_ref = refs[-6:]
    j = pl.program_id(0)
    last = last_ref[j]
    rows, cols = iotas()
    strict = rows > cols
    lower = rows >= cols
    upper = rows <= cols
    total = dop_ref.shape[0]

    @pl.when(j == 0)
    def _():
        for c in range(total // BLOCK):
            rs = pl.ds(c * BLOCK, BLOCK)
            for h in range(heads):
                cs = slice(h * BLOCK, (h + 1) * BLOCK)
                there = pl.ds(pl.multiple_of(slot_ref[c] * BLOCK, BLOCK), BLOCK)
                dop = do_ref[there, cs].astype(f32) * linv_ref[rs, cs]
                delta = jnp.sum(dop * o_ref[there, cs].astype(f32), axis=1, keepdims=True)
                dop_ref[rs, cs] = dop.astype(bf16)
                del_ref[rs, cs] = jnp.broadcast_to(delta, (BLOCK, BLOCK))
                g_ref[c, h] = jnp.zeros((BLOCK, BLOCK), bf16)

    here = pl.ds(pl.multiple_of(j * BLOCK, BLOCK), BLOCK)
    near = []
    for h in range(heads):
        cs = slice(h * BLOCK, (h + 1) * BLOCK)
        dop = dop_ref[here, cs]
        e = e_refs[0][0, 0, h]
        dp = mm_rt(dop, v_ref[:, cs])
        near.append((e.astype(f32) * (dp - del_ref[here, cs]) * scale).astype(bf16))
        dv_ref[h] = mm_lt(e, dop)
        acc_ref[h] = jnp.zeros((BLOCK, 2 * BLOCK), f32)
    for d in range(1, depth):

        @pl.when(j + d <= last)
        def _():
            i = j + d
            there = pl.ds(pl.multiple_of(i * BLOCK, BLOCK), BLOCK)
            def far(h):
                cs = slice(h * BLOCK, (h + 1) * BLOCK)
                dop = dop_ref[there, cs]
                e = e_refs[d][0, 0, h]
                dp = mm_rt(dop, v_ref[:, cs])
                yield 1
                dv_ref[h] = dv_ref[h] + mm_lt(e, dop)
                yield 1
                ds = (e.astype(f32) * (dp - del_ref[there, cs]) * scale).astype(bf16)
                dsg = jnp.concatenate([ds, g_ref[i, h]], axis=1)
                yield 1
                acc_ref[h] = acc_ref[h] + mm_lt(cur_refs[d - 1][0, 0, h], dsg)
                yield 1
                g_ref[i, h] = mm_rt(dsg, kp_ref[0, h]).astype(bf16)

            lockstep(far(h) for h in range(heads))

    lane = cols
    dr_all = jnp.zeros((BLOCK, BLOCK), f32)
    width = heads * BLOCK
    drs = {}

    def local_part(h):
        cs = slice(h * BLOCK, (h + 1) * BLOCK)
        q, k, u = q_ref[:, cs], k_ref[:, cs], u_ref[:, cs]
        kq = mm_rt(u, jnp.concatenate([k, q], axis=0))
        yield 1
        e_s = jnp.where(strict, kq[:, :BLOCK], 0.0).astype(bf16)
        a_t = jnp.where(upper, kq[:, BLOCK:], 0.0).astype(bf16)
        dn = near[h]
        acc = acc_ref[h]
        bmat = jnp.concatenate([jnp.concatenate([dn, g_ref[j, h]], axis=1), acc.astype(bf16)], axis=0)
        yz = mm(jnp.concatenate([a_t, u], axis=1), bmat).astype(bf16)
        yield 1
        ru = mm_rt(jnp.concatenate([e_s, u], axis=1), bmat)
        beta, inv_sq = strengths(u, r_ref[:, h : h + 1].astype(f32))
        bp = beta * inv_sq
        yield 1
        inv = inv_ref[0, h]
        left = mm_lt(inv, yz) * (-bp)
        yield 1
        right = -mm(inv, (ru * bp).astype(bf16))
        yield 1
        d_s = jnp.where(strict, -mm_rt(left.astype(bf16), t_ref[0, h]), 0.0).astype(bf16)
        d_e = jnp.where(strict, left[:, :BLOCK], 0.0).astype(bf16)
        d_at = jnp.where(upper, right[:, :BLOCK], 0.0).astype(bf16)
        du = left[:, BLOCK:] + right[:, BLOCK:]
        yield 1
        d_a = d_at.astype(f32).T.astype(bf16)
        uk = jnp.concatenate([u, k], axis=0)
        dq_o = g_ref[j, h].astype(f32) + mm(jnp.concatenate([d_a, dn], axis=1), uk)
        out_ref[:, cs] = dq_o.astype(bf16)
        yield 1
        uq = jnp.concatenate([u, q], axis=0)
        dk_o = acc_ref[h][:, :BLOCK].T + mm_lt(jnp.concatenate([d_e, dn], axis=0), uq)
        out_ref[:, width + h * BLOCK : width + (h + 1) * BLOCK] = dk_o.astype(bf16)
        yield 1
        du = du + mm(jnp.concatenate([d_s, d_e], axis=1), uk)
        d_st = d_s.astype(f32).T.astype(bf16)
        du = du + mm(jnp.concatenate([d_st, d_at], axis=1), uq)
        yield 1
        uf = u.astype(f32)
        rad = jnp.sum(uf * du, axis=1, keepdims=True)
        du = du - (inv_sq * rad) * uf
        drs[h] = 0.5 * rad * (1.0 - 0.5 * beta)
        out_ref[:, 2 * width + h * BLOCK : 2 * width + (h + 1) * BLOCK] = dv_ref[h].astype(bf16)
        out_ref[:, 3 * width + h * BLOCK : 3 * width + (h + 1) * BLOCK] = du.astype(bf16)

    lockstep(local_part(h) for h in range(heads))
    for h in range(heads):
        dr_all = jnp.where(lane == h, drs[h], dr_all)
    out_ref[:, 4 * width :] = dr_all.astype(bf16)


def attention_prep(proj, table, heads):
    count = table.shape[0]
    width = heads * BLOCK
    step = 4

    def rows(c, n, col):
        return pl.BlockSpec((BLOCK, n), lambda i, t: (t[i * step + c], col))

    tile = lambda n: pl.BlockSpec((step, heads, BLOCK, n), lambda i, t: (i, 0, 0, 0))
    shape = lambda n, t: jax.ShapeDtypeStruct((count, heads, BLOCK, n), t)
    spec = pltpu.PrefetchScalarGridSpec(
        num_scalar_prefetch=1,
        grid=(count // step,),
        in_specs=[rows(c, width, col) for col in (0, 1, 3) for c in range(step)]
        + [rows(c, BLOCK, 4 * heads) for c in range(step)],
        out_specs=[
            tile(BLOCK),
            pl.BlockSpec((step * BLOCK, width), lambda i, t: (i, 0)),
            tile(2 * BLOCK),
            tile(BLOCK),
            tile(2 * BLOCK),
        ],
    )
    return pl.pallas_call(
        functools.partial(prep_kernel, heads, step),
        grid_spec=spec,
        out_shape=[
            shape(BLOCK, f32),
            jax.ShapeDtypeStruct((count * BLOCK, width), bf16),
            shape(2 * BLOCK, bf16),
            shape(BLOCK, bf16),
            shape(2 * BLOCK, bf16),
        ],
        cost_estimate=pl.CostEstimate(
            flops=count * heads * 45 * BLOCK**3, bytes_accessed=6 * count * BLOCK * width, transcendentals=0
        ),
        name="attn_prep",
    )(table, *([proj] * (4 * step)))


def attention_fwd(proj, prep, first, table, slot, heads):
    near, q0, kp, _, _ = prep
    count = table.shape[0]
    depth = count
    width = heads * BLOCK
    scale = float(BLOCK) ** -0.5
    spec = pltpu.PrefetchScalarGridSpec(
        num_scalar_prefetch=3,
        grid=(count,),
        in_specs=[
            pl.BlockSpec((BLOCK, width), lambda i, f, t, w: (i, 0)),
            pl.BlockSpec((1, heads, BLOCK, BLOCK), lambda i, f, t, w: (i, 0, 0, 0)),
            pl.BlockSpec((count, heads, BLOCK, 2 * BLOCK), lambda i, f, t, w: (0, 0, 0, 0)),
            pl.BlockSpec((proj.shape[0], width), lambda i, f, t, w: (0, 2)),
        ],
        out_specs=[
            pl.BlockSpec((BLOCK, width), lambda i, f, t, w: (w[i], 0)),
            pl.BlockSpec((BLOCK, width), lambda i, f, t, w: (i, 0)),
            pl.BlockSpec((1, depth, heads, BLOCK, BLOCK), lambda i, f, t, w: (i, 0, 0, 0, 0)),
            pl.BlockSpec((1, depth - 1, heads, BLOCK, BLOCK), lambda i, f, t, w: (i, 0, 0, 0, 0)),
        ],
        scratch_shapes=[
            pltpu.VMEM((depth, heads, BLOCK, BLOCK), f32),
            pltpu.VMEM((heads, BLOCK, BLOCK), f32),
            pltpu.VMEM((heads, BLOCK, BLOCK), f32),
        ],
    )
    return pl.pallas_call(
        functools.partial(fwd_kernel, heads, depth, scale),
        grid_spec=spec,
        out_shape=[
            jax.ShapeDtypeStruct((count * BLOCK, width), bf16),
            jax.ShapeDtypeStruct((count * BLOCK, width), f32),
            jax.ShapeDtypeStruct((count, depth, heads, BLOCK, BLOCK), bf16),
            jax.ShapeDtypeStruct((count, depth - 1, heads, BLOCK, BLOCK), bf16),
        ],
        cost_estimate=pl.CostEstimate(
            flops=count * heads * 48 * BLOCK**3, bytes_accessed=6 * count * BLOCK * width, transcendentals=0
        ),
        name="attn_fwd",
    )(first, table, slot, q0, near, kp, proj)


def attention_bwd(proj, prep, saved, d_mixed, last, table, slot, heads, filled):
    _, _, kp, inv, t_all = prep
    mixed, linv, e_all, cur_all = saved
    count = table.shape[0]
    depth = count
    total = count * BLOCK
    width = heads * BLOCK
    scale = float(BLOCK) ** -0.5
    full = lambda: pl.BlockSpec((total, width), lambda j, f, t, w: (0, 0))
    wide = lambda col: pl.BlockSpec((BLOCK, width), lambda j, f, t, w: (t[j], col))
    tile = lambda n: pl.BlockSpec((1, heads, BLOCK, n), lambda j, f, t, w: (j, 0, 0, 0))

    def diagonal(d, slot):
        return pl.BlockSpec(
            (1, 1, heads, BLOCK, BLOCK), lambda j, f, t, w: (jnp.minimum(j + d, count - 1), slot, 0, 0, 0)
        )

    in_specs = [
        full(),
        full(),
        full(),
        wide(0),
        wide(1),
        wide(2),
        wide(3),
        pl.BlockSpec((BLOCK, BLOCK), lambda j, f, t, w: (t[j], 4 * heads)),
        tile(2 * BLOCK),
        tile(BLOCK),
        tile(2 * BLOCK),
    ]
    in_specs += [diagonal(d, d) for d in range(depth)] + [diagonal(d, d - 1) for d in range(1, depth)]
    operands = [last, table, slot, d_mixed, mixed, linv, proj, proj, proj, proj, proj, kp, inv, t_all]
    operands += [e_all] * depth + [cur_all] * (depth - 1)
    aliases = {}
    if filled is not None:
        aliases = {len(operands): 0}
        in_specs.append(pl.BlockSpec(memory_space=pl.ANY))
        operands.append(filled)
    spec = pltpu.PrefetchScalarGridSpec(
        num_scalar_prefetch=3,
        grid=(count,),
        in_specs=in_specs,
        out_specs=pl.BlockSpec((BLOCK, 4 * width + BLOCK), lambda j, f, t, w: (t[j], 0)),
        scratch_shapes=[
            pltpu.VMEM((total, width), bf16),
            pltpu.VMEM((total, width), f32),
            pltpu.VMEM((count, heads, BLOCK, BLOCK), bf16),
            pltpu.VMEM((heads, BLOCK, BLOCK), f32),
            pltpu.VMEM((heads, BLOCK, 2 * BLOCK), f32),
        ],
    )
    return pl.pallas_call(
        functools.partial(bwd_kernel, heads, depth, scale),
        grid_spec=spec,
        out_shape=jax.ShapeDtypeStruct((proj.shape[0], 4 * width + BLOCK), bf16),
        input_output_aliases=aliases,
        cost_estimate=pl.CostEstimate(
            flops=count * heads * 120 * BLOCK**3, bytes_accessed=8 * total * width, transcendentals=0
        ),
        name="attn_bwd",
    )(*operands)


def pick_kernel(bounds, picks, table_ref, *refs):
    total = sum(len(part) for part in bounds)
    parts, outs = refs[:total], refs[total:-3]
    held, load_sem, store_sem = refs[-3:]
    stores = []
    base = 0
    for group, limits in enumerate(bounds):
        for n in range(picks):
            slot = group * picks + n
            at = table_ref[slot]
            for p, (low, high) in enumerate(limits):

                @pl.when((at >= low) & (at < high))
                def _():
                    rows = pl.ds(pl.multiple_of((at - low) * BLOCK, BLOCK), BLOCK)
                    pltpu.make_async_copy(parts[base + p].at[rows, :], held.at[slot], load_sem.at[slot]).start()

        base += len(limits)
    for group in range(len(bounds)):
        for n in range(picks):
            slot = group * picks + n
            rows = pl.ds(n * BLOCK, BLOCK)
            pltpu.make_async_copy(outs[group].at[rows, :], held.at[slot], load_sem.at[slot]).wait()
            stores.append(pltpu.make_async_copy(held.at[slot], outs[group].at[rows, :], store_sem.at[slot]))
            stores[-1].start()
    for store in stores:
        store.wait()


def pick_blocks(groups, table):
    picks = table.shape[0] // len(groups)
    cols = groups[0][0].shape[1]
    dtype = groups[0][0].dtype
    bounds = []
    for parts in groups:
        limits, low = [], 0
        for part in parts:
            limits.append((low, low + part.shape[0] // BLOCK))
            low = limits[-1][1]
        bounds.append(limits)
    flat = [part for parts in groups for part in parts]
    slots = picks * len(groups)
    spec = pltpu.PrefetchScalarGridSpec(
        num_scalar_prefetch=1,
        grid=(1,),
        in_specs=[pl.BlockSpec(memory_space=pl.ANY)] * len(flat),
        out_specs=[pl.BlockSpec(memory_space=pl.ANY)] * len(groups),
        scratch_shapes=[
            pltpu.VMEM((slots, BLOCK, cols), dtype),
            pltpu.SemaphoreType.DMA((slots,)),
            pltpu.SemaphoreType.DMA((slots,)),
        ],
    )
    return pl.pallas_call(
        functools.partial(pick_kernel, bounds, picks),
        grid_spec=spec,
        out_shape=[jax.ShapeDtypeStruct((picks * BLOCK, cols), dtype)] * len(groups),
        cost_estimate=pl.CostEstimate(flops=0, bytes_accessed=4 * slots * BLOCK * cols, transcendentals=0),
        name="pick_blocks",
    )(table, *flat)


def place_kernel(count, rows, spot_ref, *refs):
    pieces, out, bufs, sem_in, sem_out = refs[:count], refs[count], refs[count + 1], refs[count + 2], refs[count + 3]
    loads = [pltpu.make_async_copy(pieces[n], bufs.at[n], sem_in.at[n]) for n in range(count)]
    for load in loads:
        load.start()
    stores = []
    for n in range(count):
        loads[n].wait()
        to = out.at[pl.ds(pl.multiple_of(spot_ref[n] * rows, rows), rows), :]
        stores.append(pltpu.make_async_copy(bufs.at[n], to, sem_out.at[n]))
        stores[n].start()
    for store in stores:
        store.wait()


def place_pieces(pieces, spots, count):
    rows, cols = pieces[0].shape
    held = len(pieces)
    dtype = pieces[0].dtype
    spec = pltpu.PrefetchScalarGridSpec(
        num_scalar_prefetch=1,
        grid=(1,),
        in_specs=[pl.BlockSpec(memory_space=pl.ANY)] * held,
        out_specs=pl.BlockSpec(memory_space=pl.ANY),
        scratch_shapes=[
            pltpu.VMEM((held, rows, cols), dtype),
            pltpu.SemaphoreType.DMA((held,)),
            pltpu.SemaphoreType.DMA((held,)),
        ],
    )
    where = jnp.concatenate([jnp.reshape(spot, (1,)) for spot in spots]).astype(jnp.int32)
    return pl.pallas_call(
        functools.partial(place_kernel, held, rows),
        grid_spec=spec,
        out_shape=jax.ShapeDtypeStruct((count * rows, cols), dtype),
        cost_estimate=pl.CostEstimate(flops=0, bytes_accessed=4 * held * rows * cols, transcendentals=0),
        name="place_pieces",
    )(where, *pieces)


def open_kernel(spot_ref, x_ref, out_ref):
    out_ref[...] = x_ref[...]


def open_buffer(x, spot, count):
    rows, cols = x.shape
    spec = pltpu.PrefetchScalarGridSpec(
        num_scalar_prefetch=1,
        grid=(2,),
        in_specs=[pl.BlockSpec((rows // 2, cols), lambda i, t: (i, 0))],
        out_specs=pl.BlockSpec((rows // 2, cols), lambda i, t: (2 * t[0] + i, 0)),
    )
    return pl.pallas_call(
        open_kernel,
        grid_spec=spec,
        out_shape=jax.ShapeDtypeStruct((count * rows, cols), x.dtype),
        cost_estimate=pl.CostEstimate(flops=0, bytes_accessed=4 * rows * cols, transcendentals=0),
        name="open_buffer",
    )(jnp.reshape(spot, (1,)).astype(jnp.int32), x)


def rows_contract(a, b):
    return lax.dot_general(a, b, (((0,), (0,)), ((), ())), preferred_element_type=f32)


def cols_contract(a, b):
    return lax.dot_general(a, b, (((1,), (1,)), ((), ())), preferred_element_type=f32)


def unit_rows(x):
    scale = lax.rsqrt(jnp.mean(x * x, axis=1, keepdims=True) + epsilon)
    return x * scale, scale


def norm_back(grad_normed, unit, scale, gain):
    grad_unit = grad_normed * gain
    return scale * (grad_unit - unit * jnp.mean(grad_unit * unit, axis=1, keepdims=True))


def ring_order(count):
    return list(range(0, count, 2)) + list(range(1, count, 2))[::-1]


def ring_tables(axis):
    count = lax.axis_size(axis)
    order = ring_order(count)
    right = [(order[p], order[(p + 1) % count]) for p in range(count)]
    left = [(order[p], order[(p - 1) % count]) for p in range(count)]
    me = lax.axis_index(axis)
    spot = jnp.where(me % 2 == 0, me // 2, count - 1 - me // 2)

    def owner(shift):
        at = (spot + shift + count) % count
        return jnp.where(at < count // 2, 2 * at, 2 * (count - 1 - at) + 1)

    return count, right, left, owner


class RingGather:
    def __init__(self, x, axis, whole=False):
        self.axis, self.x, self.whole = axis, x, whole
        self.count, self.right, self.left, self.owner = ring_tables(axis)
        self.moving = (x, x)
        self.hops = []

    def hop(self):
        from_left, from_right = self.moving
        if len(self.hops) == self.count // 2 - 1:
            half = self.x.shape[0] // 2
            from_left, from_right = from_left[:half], from_right[half:]
        self.moving = (
            lax.ppermute(from_left, self.axis, self.right),
            lax.ppermute(from_right, self.axis, self.left),
        )
        self.hops.append(self.moving)

    def before(self, *values):
        held = lax.optimization_barrier((self.moving,) + values)
        self.moving = held[0]
        self.hops[-1] = self.moving
        return held[1] if len(values) == 1 else held[1:]

    def finish(self):
        while len(self.hops) < self.count // 2:
            self.hop()
        rows = self.x.shape[0]
        put = lax.dynamic_update_slice_in_dim
        pieces, spots = [self.x], [self.owner(0)]
        for s, (from_left, from_right) in enumerate(self.hops[:-1], 1):
            pieces += [from_left, from_right]
            spots += [self.owner(-s), self.owner(s)]
        if self.whole:
            out = place_pieces(pieces, spots, self.count)
        else:
            out = open_buffer(self.x, spots[0], self.count)
            for piece, spot in zip(pieces[1:], spots[1:]):
                out = put(out, piece, spot * rows, 0)
        far = self.owner(self.count // 2) * rows
        out = put(out, self.hops[-1][0], far, 0)
        return put(out, self.hops[-1][1], far + rows // 2, 0)


class RingScatter:
    def __init__(self, parts, axis):
        self.axis, self.parts = axis, parts
        self.count, self.right, self.left, self.owner = ring_tables(axis)
        self.rows = parts[0].shape[0] // self.count
        self.top = self.count // 2
        self.done = 0
        half = self.rows // 2
        self.moving = (self.piece(self.top, 0, half), self.piece(-self.top, half, half))

    def piece(self, shift, start=0, size=None):
        size = self.rows if size is None else size
        at = self.owner(shift) * self.rows + start
        return jnp.concatenate([lax.dynamic_slice_in_dim(part, at, size, 0) for part in self.parts], axis=1)

    def hop(self):
        to_right, to_left = self.moving
        if self.done > 0:
            s = self.top - self.done
            a, b = self.piece(s), self.piece(-s)
            if self.done == 1:
                half = self.rows // 2
                to_right = jnp.concatenate([a[:half] + to_right, a[half:]], axis=0)
                to_left = jnp.concatenate([b[:half], b[half:] + to_left], axis=0)
            else:
                to_right, to_left = a + to_right, b + to_left
        self.moving = (lax.ppermute(to_right, self.axis, self.right), lax.ppermute(to_left, self.axis, self.left))
        self.done += 1

    def before(self, *values):
        held = lax.optimization_barrier((self.moving,) + values)
        self.moving = held[0]
        return held[1] if len(values) == 1 else held[1:]

    def finish(self):
        while self.done < self.top:
            self.hop()
        return self.piece(0).astype(f32) + self.moving[0].astype(f32) + self.moving[1].astype(f32)


def ring_kernel(axis, count, rows, widths, *refs):
    held = len(widths)
    parts, outs = refs[:held], refs[held : 2 * held]
    own_buf, send_buf, recv_buf, load_sem, send_sem, recv_sem = refs[2 * held :]
    me = lax.axis_index(axis)
    odd = me % 2
    spot = (1 - odd) * (me // 2) + odd * (count - 1 - me // 2)

    def owner(shift):
        at = (spot + shift + count) % count
        upper = at // (count // 2)
        return (1 - upper) * (2 * at) + upper * (2 * (count - 1 - at) + 1)

    top = count // 2
    cut = rows // 32 * 16
    ways = ((1, owner(1)), (-1, owner(-1)))
    barrier = pltpu.get_barrier_semaphore()
    for _, peer in ways:
        pl.semaphore_signal(barrier, inc=1, device_id={axis: peer}, device_id_type=pl.DeviceIdType.MESH)

    def load(shift, slot):
        copies = []
        at = pl.multiple_of(owner(shift) * rows, rows)
        col = 0
        for n, width in enumerate(widths):
            copies.append(
                pltpu.make_async_copy(
                    parts[n].at[pl.ds(at, rows), :],
                    own_buf.at[slot, :, pl.ds(col, width)],
                    load_sem.at[slot, n],
                )
            )
            col += width
        for copy in copies:
            copy.start()
        return copies

    slots = {top: 0, 0: 2 * top - 1}
    for s in range(1, top):
        slots[s], slots[-s] = 2 * s - 1, 2 * s
    loads = {}
    for shift in [top] + [t * s for s in range(top - 1, 0, -1) for t in (1, -1)] + [0]:
        loads[shift] = load(shift, slots[shift])
    for copy in loads[top]:
        copy.wait()
    pl.semaphore_wait(barrier, 2)
    halves = ((0, cut), (cut, rows - cut))
    sent = []

    def push(way, hop, part, src):
        start, size = halves[part]
        copy = pltpu.make_async_remote_copy(
            src_ref=src,
            dst_ref=recv_buf.at[way, hop, pl.ds(start, size), :],
            send_sem=send_sem.at[way, hop, part],
            recv_sem=recv_sem.at[way, hop, part],
            device_id={axis: ways[way][1]},
            device_id_type=pl.DeviceIdType.MESH,
        )
        copy.start()
        sent.append(copy)
        return copy

    flying = {}
    for way in range(2):
        start, size = halves[way]
        flying[way, way] = push(way, 0, way, own_buf.at[slots[top], pl.ds(start, size), :])
    for hop in range(1, top):
        shift = top - hop
        order = [(way, 1 - way) for way in range(2)] + [(way, way) for way in range(2)]
        for way, part in order:
            sign = ways[way][0]
            start, size = halves[part]
            slot = slots[sign * shift]
            if part == 1 - way:
                for copy in loads[sign * shift]:
                    copy.wait()
            area = pl.ds(start, size)
            if hop == 1 and part == 1 - way:
                flying[way, part] = push(way, hop, part, own_buf.at[slot, area, :])
                continue
            flying[way, part].wait_recv()
            total = own_buf[slot, area, :].astype(f32) + recv_buf[way, hop - 1, area, :].astype(f32)
            send_buf[way, hop - 1, area, :] = total.astype(bf16)
            flying[way, part] = push(way, hop, part, send_buf.at[way, hop - 1, area, :])
    for copy in loads[0]:
        copy.wait()
    for part in range(2):
        start, size = halves[part]
        area = pl.ds(start, size)
        for way in range(2):
            flying[way, part].wait_recv()
        col = 0
        for n, width in enumerate(widths):
            cols = pl.ds(col, width)
            outs[n][area, :] = (
                own_buf[slots[0], area, cols].astype(f32)
                + recv_buf[0, top - 1, area, cols].astype(f32)
                + recv_buf[1, top - 1, area, cols].astype(f32)
            )
            col += width
    for copy in sent:
        copy.wait_send()


def spread_kernel(axis, count, rows, widths, *refs):
    held = len(widths)
    parts, out = refs[:held], refs[held]
    own_buf, left_buf, right_buf, load_sem, store_sem, send_sem, recv_sem = refs[held + 1 :]
    me = lax.axis_index(axis)
    odd = me % 2
    spot = (1 - odd) * (me // 2) + odd * (count - 1 - me // 2)

    def owner(shift):
        at = (spot + shift + count) % count
        upper = at // (count // 2)
        return (1 - upper) * (2 * at) + upper * (2 * (count - 1 - at) + 1)

    top = count // 2
    cut = rows // 32 * 16
    halves = ((0, cut), (cut, rows - cut))
    peers = (owner(1), owner(-1))
    barrier = pltpu.get_barrier_semaphore()
    for peer in peers:
        pl.semaphore_signal(barrier, inc=1, device_id={axis: peer}, device_id_type=pl.DeviceIdType.MESH)
    loads, col = [], 0
    for n, width in enumerate(widths):
        loads.append(pltpu.make_async_copy(parts[n], own_buf.at[:, pl.ds(col, width)], load_sem.at[n]))
        loads[-1].start()
        col += width
    for load in loads:
        load.wait()
    pl.semaphore_wait(barrier, 2)
    bufs = (left_buf, right_buf)
    flying, sent, stores = {}, [], []

    def push(way, hop, part, src):
        start, size = halves[part]
        copy = pltpu.make_async_remote_copy(
            src_ref=src,
            dst_ref=bufs[way].at[hop, pl.ds(start, size), :],
            send_sem=send_sem.at[way, hop, part],
            recv_sem=recv_sem.at[way, hop, part],
            device_id={axis: peers[way]},
            device_id_type=pl.DeviceIdType.MESH,
        )
        copy.start()
        sent.append(copy)
        flying[way, hop, part] = copy

    def store(src, shift, part, sem):
        start, size = halves[part]
        at = pl.multiple_of(owner(shift) * rows + start, 16)
        stores.append(pltpu.make_async_copy(src, out.at[pl.ds(at, size), :], sem))
        stores[-1].start()

    for part in range(2):
        for way in range(2):
            start, size = halves[part]
            push(way, 0, part, own_buf.at[pl.ds(start, size), :])
    for part in range(2):
        start, size = halves[part]
        store(own_buf.at[pl.ds(start, size), :], 0, part, store_sem.at[2, 0, part])
    for hop in range(top):
        for part in range(2):
            for way in range(2):
                if hop == top - 1 and part != way:
                    continue
                start, size = halves[part]
                here = bufs[way].at[hop, pl.ds(start, size), :]
                flying[way, hop, part].wait_recv()
                if hop + 1 < top - 1 or (hop + 1 == top - 1 and part == way):
                    push(way, hop + 1, part, here)
                store(here, -(hop + 1) if way == 0 else hop + 1, part, store_sem.at[way, hop, part])
    for copy in sent:
        copy.wait_send()
    for copy in stores:
        copy.wait()


def ring_spread(parts, axis):
    count = lax.axis_size(axis)
    rows = parts[0].shape[0]
    widths = [part.shape[1] for part in parts]
    cols = sum(widths)
    top = count // 2
    return pl.pallas_call(
        functools.partial(spread_kernel, axis, count, rows, widths),
        in_specs=[pl.BlockSpec(memory_space=pl.ANY)] * len(parts),
        out_specs=pl.BlockSpec(memory_space=pl.ANY),
        out_shape=jax.ShapeDtypeStruct((count * rows, cols), bf16),
        scratch_shapes=[
            pltpu.VMEM((rows, cols), bf16),
            pltpu.VMEM((top, rows, cols), bf16),
            pltpu.VMEM((top, rows, cols), bf16),
            pltpu.SemaphoreType.DMA((len(parts),)),
            pltpu.SemaphoreType.DMA((3, top, 2)),
            pltpu.SemaphoreType.DMA((2, top, 2)),
            pltpu.SemaphoreType.DMA((2, top, 2)),
        ],
        compiler_params=pltpu.CompilerParams(collective_id=1, has_side_effects=True),
        cost_estimate=pl.CostEstimate(flops=0, bytes_accessed=4 * count * rows * cols, transcendentals=0),
        name="ring_spread",
    )(*parts)


def ring_sum(parts, axis):
    count = lax.axis_size(axis)
    rows = parts[0].shape[0] // count
    widths = [part.shape[1] for part in parts]
    cols = sum(widths)
    top = count // 2
    sent = (2 * top - 1) * rows * cols * 2
    return pl.pallas_call(
        functools.partial(ring_kernel, axis, count, rows, widths),
        in_specs=[pl.BlockSpec(memory_space=pl.ANY)] * len(parts),
        out_specs=[pl.BlockSpec(memory_space=pltpu.VMEM)] * len(parts),
        out_shape=[jax.ShapeDtypeStruct((rows, width), f32) for width in widths],
        scratch_shapes=[
            pltpu.VMEM((count, rows, cols), bf16),
            pltpu.VMEM((2, top - 1, rows, cols), bf16),
            pltpu.VMEM((2, top, rows, cols), bf16),
            pltpu.SemaphoreType.DMA((count, len(parts))),
            pltpu.SemaphoreType.DMA((2, top, 2)),
            pltpu.SemaphoreType.DMA((2, top, 2)),
        ],
        compiler_params=pltpu.CompilerParams(collective_id=0, has_side_effects=True),
        cost_estimate=pl.CostEstimate(flops=0, bytes_accessed=4 * count * rows * cols, transcendentals=0),
        name="ring_sum",
    )(*parts)


def tp_sum(x):
    count = lax.axis_size("tp")
    me = lax.axis_index("tp")
    pieces = [x] + [lax.ppermute(x, "tp", [(i, (i + s) % count) for i in range(count)]) for s in range(1, count)]
    total = jnp.zeros_like(x)
    for r in range(count):
        chosen = pieces[0]
        for step in range(1, count):
            chosen = jnp.where((me - step) % count == r, pieces[step], chosen)
        total = total + chosen
    return total


SLOTS = (0, 2, 1, 3)


def across(x):
    return lax.ppermute(x, "tp", [(i, i ^ 2) for i in range(4)])


def beside(x):
    return lax.ppermute(x, "tp", [(i, i ^ 1) for i in range(4)])


def share(rows):
    size = rows.shape[0] // 4
    other = beside(rows[2 * size :])
    pair = rows[: 2 * size].astype(f32) + other.astype(f32)
    return pair[:size], across(pair[size:].astype(bf16))


def spread(x):
    pair = jnp.concatenate([x, across(x)], axis=0)
    return jnp.concatenate([pair, beside(pair)], axis=0)


def together(*values):
    return lax.optimization_barrier(values)


def local(
    tokens,
    cotangent,
    w_query,
    w_key,
    w_value,
    w_house,
    w_beta,
    w_out,
    w_gate,
    w_up,
    w_down,
    gain_attn,
    gain_ffn,
    pack_index,
    seq_start,
):
    packing, begins = pack_index[0], seq_start[0]
    bins, bin_rows = packing.shape
    per_bin = bin_rows // BLOCK
    streams = range(bins)
    width = w_query.shape[1]
    heads = w_beta.shape[1]
    hidden_width = w_gate.shape[1]
    shard = w_query.shape[0]
    ranks = 4
    assert lax.axis_size("tp") == ranks
    half = bin_rows // ranks
    per_half = half // BLOCK
    me = lax.axis_index("tp")

    given = packing[:, ::BLOCK] // BLOCK
    per_own = bins * per_half
    table = given
    first = begins[:, ::BLOCK] // BLOCK
    spots = jnp.arange(per_bin, dtype=jnp.int32)
    last = jnp.max(jnp.where(first[:, :, None] == first[:, None, :], spots[None, None, :], 0), axis=2)
    away = me ^ (spots // per_half)
    slot = ((away // 2) + 2 * (away % 2)) * per_half + spots % per_half
    places = jnp.arange(bins, dtype=jnp.int32)[:, None] * per_bin + slot[None, :]
    blocks = jnp.arange(bins * per_bin, dtype=jnp.int32)
    inverse = jnp.sum(jnp.where(given.reshape(-1)[:, None] == blocks[None, :], places.reshape(-1)[:, None], 0), axis=0)
    slotted = jnp.sum(jnp.where(slot[None, :, None] == spots[None, None, :], given[:, :, None], 0), axis=1)
    packed = jnp.sum(jnp.where(given.reshape(-1)[:, None] == blocks[None, :], blocks[:, None], 0), axis=0)
    mine = (blocks // per_own == me) & (blocks >= 0)
    pull = jnp.arange(per_own, dtype=jnp.int32)[:, None] == jnp.where(mine, blocks % per_own, -1)[None, :]
    own_places = jnp.sum(jnp.where(pull, inverse[None, :], 0), axis=1)
    own_packed = jnp.sum(jnp.where(pull, packed[None, :], 0), axis=1)
    origin = me ^ (own_packed % per_bin // per_half)
    own_spots = ((origin // 2) + 2 * (origin % 2)) * per_own + own_packed // per_bin * per_half + own_packed % per_half
    holder = me ^ (slotted // per_own)
    cot_table = ((holder // 2) + 2 * (holder % 2)) * per_own + slotted % per_own
    x_table = slotted[:, :per_half].reshape(-1)
    end_table = jnp.concatenate([own_places, own_spots]).astype(jnp.int32)
    tables = (table.astype(jnp.int32), first, last, slot, x_table, end_table, cot_table.reshape(-1))

    lanes = lax.broadcasted_iota(jnp.int32, (shard, BLOCK), 1)
    extras = jnp.pad(w_beta, ((0, 0), (0, BLOCK - heads)))
    extras = jnp.where(lanes == heads, gain_attn[:, None], extras)
    extras = jnp.where(lanes == heads + 1, gain_ffn[:, None], extras)
    ffn_pack = jnp.concatenate([w_gate, w_up], axis=1)
    full_tokens = lax.all_gather(tokens, "tp", axis=0, tiled=True)
    tables = together(*tables)
    table, first, last, slot, x_table, end_table, cot_table = tables
    w_in = ring_spread([w_query, w_key, w_value, w_house, extras], "fsdp")
    full_tokens, w_in, ffn_pack, out_shard, down_shard, cotangent, *tables = together(
        full_tokens, w_in, ffn_pack, w_out, w_down, cotangent, *tables
    )
    table, first, last, slot, x_table, end_table, cot_table = tables
    ffn_ring = RingGather(ffn_pack, "fsdp", True)
    ffn_ring.hop()
    x_rows = pick_blocks([[full_tokens]] * bins, x_table)
    full_out = lax.all_gather(out_shard, "fsdp", axis=0, tiled=True)
    full_down = lax.all_gather(down_shard, "fsdp", axis=0, tiled=True)
    cot_far = across(cotangent)
    pick = (jnp.arange(BLOCK)[None, :] == heads + jnp.arange(8)[:, None]).astype(bf16)
    gain_rows = cols_contract(pick, w_in[:, 4 * width :])
    gain_one, gain_two = gain_rows[0], gain_rows[1]

    all_unit, _ = unit_rows(full_tokens.astype(f32))
    normed = (all_unit * gain_one).astype(bf16)
    proj = jnp.dot(normed, w_in, preferred_element_type=f32).astype(bf16)

    def attend(m):
        prep = attention_prep(proj, table[m], heads)
        return prep, lambda prep: attention_fwd(proj, prep, first[m], table[m], slot, heads)

    preps, saved, hidden_in, unit_two, scale_two, normed_two = [], [], [], [], [], []

    def close(m, own, far):
        hidden_in.append(x_rows[m].astype(f32) + own + far.astype(f32))
        unit, scale = unit_rows(hidden_in[m])
        unit_two.append(unit)
        scale_two.append(scale)
        return (unit * gain_two).astype(bf16)

    prep, run = attend(0)
    prep = list(prep)
    prep[0] = ffn_ring.before(prep[0])
    ffn_ring.hop()
    preps.append(prep)
    saved.append(list(run(prep)))
    saved[0][0], cot_far = together(saved[0][0], cot_far)
    cot_parts = [cotangent, cot_far, beside(cotangent), beside(cot_far)]
    rows = ffn_ring.before(cols_contract(saved[0][0], full_out).astype(bf16))
    ffn_ring.hop()
    attn_own, attn_far = share(rows)
    proj, attn_own = together(proj, attn_own)
    prep, run = attend(1)
    prep = list(prep)
    prep[0], attn_far = ffn_ring.before(prep[0], attn_far)
    while len(ffn_ring.hops) < ffn_ring.count // 2:
        ffn_ring.hop()
    preps.append(prep)
    normed_own = close(0, attn_own, attn_far)
    normed_far = across(normed_own)
    prep[0], normed_own = together(prep[0], normed_own)
    saved.append(list(run(prep)))
    saved[1][0], normed_far, cot_parts[2], cot_parts[3] = ffn_ring.before(saved[1][0], normed_far, *cot_parts[2:])
    pair = jnp.concatenate([normed_own, normed_far], axis=0)
    normed_two.append(jnp.concatenate([pair, beside(pair)], axis=0))
    attn_own, attn_far = share(cols_contract(saved[1][0], full_out).astype(bf16))
    attn_own, cot_parts[3], ffn_ring.x = together(attn_own, cot_parts[3], ffn_ring.x)
    ffn_full = ffn_ring.finish()
    cot_rows = list(pick_blocks([cot_parts] * bins, cot_table))

    full_gate, full_up = ffn_full[:, :hidden_width], ffn_full[:, hidden_width : 2 * hidden_width]
    full_gate_up = ffn_full
    hidden, gate_up, back = [], [], []

    def ffn(m, rows, middle):
        gate_pre = jnp.dot(rows, full_gate, preferred_element_type=f32)
        up_part = jnp.dot(rows, full_up, preferred_element_type=f32)
        cot_rows[m] = middle(cot_rows[m])
        hidden.append((jax.nn.silu(gate_pre) * up_part).astype(bf16))
        grad_hidden = jnp.dot(cot_rows[m], full_down, preferred_element_type=f32)
        sigma = jax.nn.sigmoid(gate_pre)
        grad_gate = (grad_hidden * up_part * sigma * (1.0 + gate_pre * (1.0 - sigma))).astype(bf16)
        grad_up = (grad_hidden * jax.nn.silu(gate_pre)).astype(bf16)
        gate_up.append(jnp.concatenate([grad_gate, grad_up], axis=1))

    def ffn_back_rows(m):
        return cols_contract(gate_up[m], full_gate_up).astype(bf16)

    flying = {}

    def middle(rows):
        rows, own, far = together(rows, attn_own, attn_far)
        mine = close(1, own, far)
        flying[0], flying[1] = mine, across(mine)
        return rows

    ffn(0, normed_two[0], middle)
    normed_own, normed_far = flying[0], flying[1]
    rows, normed_own, normed_far = together(ffn_back_rows(0), normed_own, normed_far)
    back_own, back_far = share(rows)
    pair = jnp.concatenate([normed_own, normed_far], axis=0)
    normed_two.append(jnp.concatenate([pair, beside(pair)], axis=0))
    grad_attn = []

    def close_back(m, own, far):
        norm_two_grad = norm_back(own + far.astype(f32), unit_two[m], scale_two[m], gain_two)
        cot_own = cot_rows[m][:half].astype(f32)
        return (cot_own + norm_two_grad).astype(bf16)

    ffn(1, normed_two[1], lambda rows: rows)
    gate_up[1], hidden[1], back_own, back_far = together(gate_up[1], hidden[1], back_own, back_far)
    dh_own = close_back(0, back_own, back_far)
    hidden[1], dh_own = together(hidden[1], dh_own)
    grads_down = sum(rows_contract(cot_rows[m], hidden[m]) for m in streams)
    grads_down, gate_up[1] = together(grads_down.astype(bf16), gate_up[1])
    sum_down = lax.psum_scatter(grads_down, "fsdp", scatter_dimension=0, tiled=True)
    rows, dh_own = together(ffn_back_rows(1), dh_own)
    back_own, back_far = share(rows)
    back_own, normed_two[0], normed_two[1] = together(back_own, *normed_two)
    grads_in, dh_own = together(rows_contract(normed_two[0], gate_up[0]), dh_own)
    dh_far = across(dh_own)
    grads_in = grads_in + sum(rows_contract(normed_two[m], gate_up[m]) for m in streams[1:])
    grads_in, back_far = together(grads_in.astype(bf16), back_far)
    early_own, early_far = dh_own, dh_far
    sum_in = lax.psum_scatter(grads_in, "fsdp", scatter_dimension=0, tiled=True)
    dh_own = close_back(1, back_own, back_far)
    dh_far = across(dh_own)
    hidden[0], hidden[1], dh_own = together(*hidden, dh_own)
    y_parts = [cols_contract(hidden[m], full_down).astype(bf16) for m in streams]
    y_parts[0], y_parts[1], early_far = together(*y_parts, early_far)
    ffn_parts = [share(part) for part in y_parts]
    pair = jnp.concatenate([early_own, early_far], axis=0)
    grad_attn.append(jnp.concatenate([pair, beside(pair)], axis=0))
    d_mixed = jnp.dot(grad_attn[0], full_out, preferred_element_type=f32).astype(bf16)
    y_own, y_far = [p[0] for p in ffn_parts], [p[1] for p in ffn_parts]
    d_mixed, y_own[0], y_own[1] = together(d_mixed, *y_own)
    d_proj = attention_bwd(proj, preps[0], saved[0], d_mixed, last[0], table[0], slot, heads, None)
    d_proj, dh_far, y_far[0] = together(d_proj, dh_far, y_far[0])
    pair = jnp.concatenate([dh_own, dh_far], axis=0)
    grad_attn.append(jnp.concatenate([pair, beside(pair)], axis=0))
    d_mixed = jnp.dot(grad_attn[1], full_out, preferred_element_type=f32).astype(bf16)
    finish_y = lambda m: (hidden_in[m] + y_own[m] + y_far[m].astype(f32)).astype(bf16)
    y_rows = [finish_y(0)]
    grad_out = sum(rows_contract(grad_attn[m], saved[m][0]) for m in streams).astype(bf16)
    d_mixed, grad_out, y_rows[0] = together(d_mixed, grad_out, y_rows[0])
    y_across = [across(y_rows[0])]
    d_proj = attention_bwd(proj, preps[1], saved[1], d_mixed, last[1], table[1], slot, heads, d_proj)
    d_proj, sum_down, y_across[0], y_far[1] = together(d_proj, sum_down, y_across[0], y_far[1])
    y_rows.append(finish_y(1))
    y_across.append(across(y_rows[1]))
    attn_grads, d_proj, y_across[1] = together(rows_contract(normed, d_proj).astype(bf16), d_proj, y_across[1])
    y_other = [beside(part) for part in (*y_rows, *y_across)]
    rows_one, attn_grads, *y_other = together(cols_contract(d_proj, w_in).astype(bf16), attn_grads, *y_other)
    grad_one = lax.psum_scatter(rows_one, "tp", scatter_dimension=0, tiled=True)
    dh_own, out_y = pick_blocks([grad_attn, [*y_rows, *y_across, *y_other]], end_table)
    attn_grads, dh_own, out_y = together(attn_grads, dh_own, out_y)
    attn_sum, grad_out = ring_sum([attn_grads, grad_out], "fsdp")
    sum_in, sum_down = sum_in.astype(f32), sum_down.astype(f32)
    grad_one = grad_one.astype(f32)
    unit_one, scale_one = unit_rows(tokens.astype(f32))
    norm_one_grad = norm_back(grad_one, unit_one, scale_one, gain_one)
    out_dx = (dh_own.astype(f32) + norm_one_grad).astype(bf16)
    dots = lambda grads, weights: jnp.sum(grads * weights.astype(f32), axis=1)
    own_one = dots(attn_sum[:, 4 * width : 4 * width + heads], w_beta) + sum(
        dots(attn_sum[:, n * width : (n + 1) * width], weight)
        for n, weight in enumerate((w_query, w_key, w_value, w_house))
    )
    own_two = dots(sum_in, ffn_pack)
    gains = tp_sum(jnp.stack([own_one, own_two])) / jnp.stack([gain_attn, gain_ffn]).astype(f32)
    return (
        out_y,
        out_dx,
        attn_sum[:, :width],
        attn_sum[:, width : 2 * width],
        attn_sum[:, 2 * width : 3 * width],
        attn_sum[:, 3 * width : 4 * width],
        attn_sum[:, 4 * width : 4 * width + heads],
        grad_out,
        sum_in[:, :hidden_width],
        sum_in[:, hidden_width:],
        sum_down,
        gains[0],
        gains[1],
    )


def solution(mesh):
    rows = P(("fsdp", "tp"), None)
    weight = P("fsdp", "tp")
    return jax.shard_map(
        local,
        mesh=mesh,
        in_specs=(rows, rows) + (weight,) * 9 + (P("fsdp"), P("fsdp"), P("fsdp", None, None), P("fsdp", None, None)),
        out_specs=(rows, rows) + (weight,) * 9 + (P("fsdp"), P("fsdp")),
        check_vma=False,
    )
```
